32 devices in a mesh: grp: 4 (over z), shard: 8 (over y, x, core).
Axes of the slice: x: 2, y: 2, z: 4, core: 2. Of those that a mesh axis runs over, the one named last changes fastest.
Arguments:
- latents: bfloat16 [4096, 1024], P(('grp', 'shard')), may hold values from -6 to 6
- head_weight: bfloat16 [1024, 1024], P('shard'), may hold values from -0.1875 to 0.1875
- norm_gain: float32 [1024], replicated, may hold values from 0.1 to 1.9
- color_head: bfloat16 [4, 256], replicated, may hold values from -1.5 to 1.5
- sample_points: float32 [2048, 192], P(('grp', 'shard')), may hold values from -1 to 1
- sample_spacing: float32 [2048, 64], P(('grp', 'shard')), may hold values from 0.002 to 0.02
- ray_targets: float32 [3, 2048], P(None, ('grp', 'shard')), may hold values from 0 to 1
- ray_scene: int32 [2048], P(('grp', 'shard')), may hold values from 0 to 31, as said below
Outputs:
- rendered_color: float32 [3, 2048], P(None, ('grp', 'shard'))
- loss: float32 [], replicated
- head_grad: float32 [1024, 1024], P('shard')
- norm_gain_grad: float32 [1024], replicated
- latent_grad: bfloat16 [4096, 1024], P(('grp', 'shard'))
The draws below stay inside these ranges and needn't reach their ends.
Inputs may be any that keep to these rules, and one draw needn't show every extreme that they name: `ray_scene`: one scene, drawn from the seed, is named by exactly 8 rays of every device; no device names any scene more than 8 times; every scene is named by one ray or more, and the totals of the other scenes differ from one another by one at most.
All inputs are finite; a program needn't handle non-finite values.
Results may differ from the reference program's by a relative error of at most 0.017.
Values may be sent and summed in bfloat16 or wider, within the bound.
A program may use at most 64 MiB of HBM per device.

```python
import math
import jax
import jax.numpy as jnp
from jax import lax

D = 1024
WF = 256
LAYERS = 2
RS = 64
RAY_DEV = 64
LAT = 128
SCENES = 32
RAYS = 2048
DEVICES = 32


def draw_ray_scene(key, part):
    key_hot, key_rest, key_turn, key_place = jax.random.split(jax.random.fold_in(key, 11), 4)
    hot_scene = jax.random.randint(key_hot, (), 0, SCENES)
    others = jax.random.permutation(key_rest, SCENES - 1).astype(jnp.int32)
    others = others + (others >= hot_scene).astype(jnp.int32)
    offset_turn = jax.random.randint(key_turn, (), 0, SCENES - 1)
    places = jax.random.split(key_place, DEVICES)
    shuffled = jax.vmap(lambda place_key: jax.random.permutation(place_key, RAY_DEV))(places)
    ray_rank = jnp.argsort(shuffled, axis=1, stable=True).astype(jnp.int32)
    per_device = 4 * RAY_DEV // DEVICES
    device_ids = jnp.arange(DEVICES, dtype=jnp.int32)[:, None]
    position = jnp.remainder(offset_turn + device_ids * (RAY_DEV - per_device) + ray_rank - per_device, SCENES - 1)
    scene_ids = jnp.where(ray_rank < per_device, hot_scene, others[position])
    return scene_ids.reshape(RAYS).astype(jnp.int32)


def strengthened(array, stream_key, source, target, blocks, factor):
    def block_of(axis_at):
        return (jnp.arange(array.shape[axis_at]) // (array.shape[axis_at] // blocks)).reshape((-1,) + (1,) * (array.ndim - 1 - axis_at))

    one_side = jax.random.permutation(stream_key, blocks)[block_of(target)]
    other_side = (block_of(target) + blocks // 2) % blocks
    return jnp.where((block_of(source) == one_side) | (block_of(source) == other_side), factor * array, array)


def shard_levels(stream_key, shape, shards, low, largest):
    loudness = 1.0
    for axis_at, shards_of in shards:
        steps = jax.random.uniform(jax.random.fold_in(jax.random.fold_in(stream_key, 6), axis_at), (shards_of,), jnp.float32, low / len(shards), largest / len(shards))
        loudness = loudness * jnp.repeat(jnp.exp(steps), shape[axis_at] // shards_of).reshape((-1,) + (1,) * (len(shape) - 1 - axis_at))
    return loudness


def gaussian(own_key, shape, spread, bound, cuts=(), held_as=jnp.bfloat16):
    factor_of = shard_levels(own_key, shape, cuts, -0.22, 0.18) if cuts else 1.0
    result = jax.random.normal(own_key, shape, jnp.float32) * spread * factor_of
    return jnp.minimum(jnp.maximum(result, -bound), bound).astype(held_as)


def noise_with(rng, shape, scale, bound, pieces, heavy, kind=jnp.bfloat16):
    array = scale * jax.random.normal(rng, shape, jnp.float32)
    if pieces:
        array = array * shard_levels(rng, shape, pieces, -0.22, 0.18)
    return jnp.clip(strengthened(array, jax.random.fold_in(rng, 3), *heavy), -bound, bound).astype(kind)


def setup_inputs(seed: int = 0) -> dict:
    key_list = jax.random.split(jax.random.key(seed), 9)
    return {
        "latents": noise_with(key_list[0], (SCENES * LAT, D), 1.0, 6.0, ((0, 32),), (0, 1, 32, 2.75)),
        "head_weight": gaussian(key_list[1], (D, D), D ** -0.5, 0.1875, ((0, 8),)),
        "norm_gain": jnp.clip(1.0 + 0.18 * jax.random.normal(key_list[2], (D,), jnp.float32), 0.1, 1.9),
        "color_head": gaussian(key_list[3], (4, WF), (WF // 16) ** -0.5, 1.5),
        "sample_points": jnp.clip(jax.random.uniform(key_list[4], (RAYS, 3 * RS), jnp.float32, -1.0, 1.0) * shard_levels(key_list[4], (RAYS, 3 * RS), ((0, 32),), -0.4, 0.0), -1.0, 1.0),
        "sample_spacing": jnp.clip(jnp.exp(math.log(0.02) - 2.30258502 * jax.random.uniform(key_list[5], (RAYS, RS), jnp.float32) ** shard_levels(key_list[5], (RAYS, RS), ((0, 32),), -0.2, 0.2)), 0.002, 0.02),
        "ray_targets": jnp.clip(1.0 * jax.random.uniform(key_list[6], (3, RAYS), jnp.float32) ** shard_levels(key_list[6], (3, RAYS), ((1, 32),), -0.2, 0.2), 0.0, 1.0),
        "ray_scene": draw_ray_scene(jax.random.fold_in(key_list[8], 71), 0),
    }


norm_eps = 1e-06

def encode(sample_rows, field_width):
    column = jnp.arange(field_width)
    component = column % 3
    octave = (column // 6 % 8).astype(jnp.float32)
    frequency = jnp.exp2(octave) * math.pi
    phase_shift = (column // 3 % 2).astype(jnp.float32) * (0.5 * math.pi)
    picked = jnp.zeros((sample_rows.shape[0], field_width), jnp.float32)
    for coord in range(3):
        chosen = (component == coord).astype(jnp.float32)
        picked = picked + sample_rows[:, coord:coord + 1] * chosen[None, :]
    return jnp.sin(picked * frequency + phase_shift)

def point_rows(points, ray_depth):
    ray_number = points.shape[0]
    return points.reshape(ray_number, 3, ray_depth).transpose(0, 2, 1).reshape(ray_number * ray_depth, 3)

def render_rays(points, spacing, target, live_rays, scene_factor, w_first, w_second, color_head):
    ray_number, ray_depth = spacing.shape
    field_width = w_first.shape[0]
    fan_scale = field_width ** (-0.5)
    sample_rows = point_rows(points, ray_depth)
    h_zero = encode(sample_rows, field_width).astype(jnp.bfloat16)
    h_one = jax.nn.relu(jnp.dot(h_zero, w_first, preferred_element_type=jnp.float32) * fan_scale).astype(jnp.bfloat16)
    h_two = jax.nn.relu(jnp.dot(h_one, w_second, preferred_element_type=jnp.float32) * fan_scale).astype(jnp.bfloat16)
    raw_out = lax.dot_general(color_head, h_two, (((1,), (1,)), ((), ())), preferred_element_type=jnp.float32)
    density = jax.nn.softplus(raw_out[0]).reshape(ray_number, ray_depth)
    albedo = jax.nn.sigmoid(raw_out[1:4]).reshape(3, ray_number, ray_depth)
    optical = density * spacing
    optical_before = jnp.cumsum(optical, axis=1) - optical
    transmit = jnp.exp(-optical_before)
    survive = jnp.exp(-optical)
    blend = transmit * (1.0 - survive)
    ray_color = lax.optimization_barrier(jnp.sum(blend[None] * (albedo - 1.0), axis=2)) + 1.0
    residual = ray_color - target.T
    loss_part = jnp.sum(jnp.where(live_rays, lax.optimization_barrier(jnp.sum(residual * residual, axis=0)) * scene_factor, 0.0))
    grad_color = jnp.where(live_rays[None, :], 2.0 * residual * scene_factor, 0.0)
    d_albedo = grad_color[:, :, None] * blend[None]
    d_blend = lax.optimization_barrier(jnp.sum(grad_color[:, :, None] * (albedo - 1.0), axis=0))
    weighted = d_blend * blend
    behind = lax.optimization_barrier(jnp.sum(weighted, axis=1, keepdims=True)) - jnp.cumsum(weighted, axis=1)
    d_optical = d_blend * transmit * survive - behind
    d_density = (d_optical * spacing * jax.nn.sigmoid(raw_out[0]).reshape(ray_number, ray_depth)).reshape(1, ray_number * ray_depth)
    d_tint = (d_albedo * albedo * (1.0 - albedo)).reshape(3, ray_number * ray_depth)
    d_raw = jnp.concatenate([d_density, d_tint], axis=0).astype(jnp.bfloat16)
    d_htwo = lax.dot_general(d_raw, color_head, (((0,), (0,)), ((), ())), preferred_element_type=jnp.float32)
    d_atwo = (jnp.where(h_two > 0, d_htwo, 0.0) * fan_scale).astype(jnp.bfloat16)
    grad_second = lax.dot_general(h_one, d_atwo, (((0,), (0,)), ((), ())), preferred_element_type=jnp.float32)
    d_hone = lax.dot_general(d_atwo, w_second, (((1,), (1,)), ((), ())), preferred_element_type=jnp.float32)
    d_aone = (jnp.where(h_one > 0, d_hone, 0.0) * fan_scale).astype(jnp.bfloat16)
    grad_first = lax.dot_general(h_zero, d_aone, (((0,), (0,)), ((), ())), preferred_element_type=jnp.float32)
    return (ray_color, loss_part, grad_first, grad_second)

def reference(latents, head_weight, norm_gain, color_head, sample_points, sample_spacing, ray_targets, ray_scene):
    field_width = color_head.shape[1]
    ray_total, ray_depth = sample_spacing.shape
    latent_f32 = latents.astype(jnp.float32)
    inv_rms = lax.rsqrt(lax.optimization_barrier(jnp.mean(latent_f32 * latent_f32, axis=1, keepdims=True)) + norm_eps)
    x_hat = latent_f32 * inv_rms
    x_norm = (x_hat * norm_gain).astype(jnp.bfloat16)
    field_rows = jnp.dot(x_norm, head_weight, preferred_element_type=jnp.float32).astype(jnp.bfloat16)
    field_layers = field_rows.reshape(SCENES, LAYERS, field_width, field_width)
    scene_ids = jnp.arange(SCENES, dtype=jnp.int32)
    counts = lax.optimization_barrier(jnp.sum((ray_scene[:, None] == scene_ids[None, :]).astype(jnp.int32), axis=0))
    offsets = (jnp.cumsum(counts) - counts).astype(jnp.int32)
    sort_order = jnp.argsort(ray_scene, stable=True)
    inverse = jnp.argsort(sort_order, stable=True)
    sub_rays = RAY_DEV
    points_sorted = jnp.concatenate([sample_points[sort_order], jnp.zeros((sub_rays, sample_points.shape[1]), jnp.float32)], axis=0)
    spacing_sorted = jnp.concatenate([sample_spacing[sort_order], jnp.zeros((sub_rays, ray_depth), jnp.float32)], axis=0)
    target_sorted = jnp.concatenate([ray_targets.T[sort_order], jnp.zeros((sub_rays, 3), jnp.float32)], axis=0)

    def per_scene(running, scene_item):
        colors, loss_sum = running
        weights_pair, scene_rays, offset = scene_item
        scene_factor = 1.0 / (SCENES * scene_rays.astype(jnp.float32))
        w_first = weights_pair[0]
        w_second = weights_pair[1]

        def per_block(block_index, inner):
            grad_first, grad_second, colors, loss_sum = inner
            first_row = (offset + block_index * sub_rays).astype(jnp.int32)
            points = lax.dynamic_slice_in_dim(points_sorted, first_row, sub_rays, 0)
            spacing = lax.dynamic_slice_in_dim(spacing_sorted, first_row, sub_rays, 0)
            target = lax.dynamic_slice_in_dim(target_sorted, first_row, sub_rays, 0)
            live_rays = block_index * sub_rays + jnp.arange(sub_rays, dtype=jnp.int32) < scene_rays
            ray_color, loss_part, more_first, more_second = render_rays(points, spacing, target, live_rays, scene_factor, w_first, w_second, color_head)
            previous = lax.dynamic_slice_in_dim(colors, first_row, sub_rays, 1)
            colors = lax.dynamic_update_slice_in_dim(colors, jnp.where(live_rays[None, :], ray_color, previous), first_row, 1)
            return (grad_first + more_first, grad_second + more_second, colors, loss_sum + loss_part)
        zero_grad = jnp.zeros((field_width, field_width), jnp.float32)
        block_count = ((scene_rays + sub_rays - 1) // sub_rays).astype(jnp.int32)
        grad_first, grad_second, colors, loss_sum = lax.fori_loop(jnp.int32(0), block_count, per_block, (zero_grad, zero_grad, colors, loss_sum))
        return ((colors, loss_sum), jnp.stack([grad_first, grad_second]))
    start_colors = jnp.zeros((3, ray_total + sub_rays), jnp.float32)
    (colors, loss_sum), grad_layers = lax.scan(per_scene, (start_colors, jnp.zeros((), jnp.float32)), (field_layers, counts, offsets))
    rendered_color = colors[:, :ray_total][:, inverse]
    d_field = grad_layers.reshape(SCENES * LAT, D).astype(jnp.bfloat16)
    head_grad = lax.dot_general(x_norm, d_field, (((0,), (0,)), ((), ())), preferred_element_type=jnp.float32)
    d_norm = lax.dot_general(d_field, head_weight, (((1,), (1,)), ((), ())), preferred_element_type=jnp.float32)
    norm_gain_grad = lax.optimization_barrier(jnp.sum(d_norm * x_hat, axis=0))
    d_scaled = d_norm * norm_gain
    latent_grad = (inv_rms * (d_scaled - x_hat * lax.optimization_barrier(jnp.mean(d_scaled * x_hat, axis=1, keepdims=True)))).astype(jnp.bfloat16)
    return (rendered_color, loss_sum, head_grad, norm_gain_grad, latent_grad)
```

```python
import functools

import jax
import jax.numpy as jnp
from jax import lax
from jax.experimental import pallas as pl
from jax.experimental.pallas import tpu as pltpu
from jax.sharding import PartitionSpec as P

norm_eps = 1e-06

LANES = 128
HALVES = 2
FEATURES = 48
FOLDED = 16
BLOCK = 1024
SINE = (3.14159265358979, -5.16771278004997, 2.55016403987735, -0.599264529320792, 0.0821458866111282, -0.00737043094571435, 0.000466302805767613, -0.0000219153534478303)
MESH = pl.DeviceIdType.MESH


def sine_of_pi(turns):
    whole = jnp.floor(turns + 0.5)
    rest = turns - whole
    odd = whole - 2.0 * jnp.floor(whole * 0.5)
    square = rest * rest
    value = jnp.full_like(square, SINE[-1])
    for coefficient in SINE[-2::-1]:
        value = value * square + coefficient
    return value * (rest * (1.0 - 2.0 * odd))


def product(a, b):
    return jnp.dot(a, b, preferred_element_type=jnp.float32)


def exact(a, b, contract=(1, 0)):
    return lax.dot_general(
        a,
        b,
        (((contract[0],), (contract[1],)), ((), ())),
        preferred_element_type=jnp.float32,
        precision=lax.Precision.HIGHEST,
    )


def over_first(a, b):
    return lax.dot_general(a, b, (((0,), (0,)), ((), ())), preferred_element_type=jnp.float32)


def over_last(a, b):
    return lax.dot_general(a, b, (((1,), (1,)), ((), ())), preferred_element_type=jnp.float32)


def iota(shape, axis):
    return lax.broadcasted_iota(jnp.int32, shape, axis)


def store_rows(ref, start, count, stride, values):
    for lanes in range(ref.shape[0]):
        ref[lanes, pl.ds(start, count, stride=stride), :] = values[:, lanes * LANES : (lanes + 1) * LANES]


def load_rows(ref, start, count, stride):
    return jnp.concatenate(
        [ref[lanes, pl.ds(start, count, stride=stride), :] for lanes in range(ref.shape[0])], axis=1
    )


def joined(ref):
    return jnp.concatenate([ref[lanes] for lanes in range(ref.shape[0])], axis=1)


def encode_rows(axes, encoded):
    sines = [sine_of_pi(a) for a in axes]
    cosines = [sine_of_pi(a + 0.5) for a in axes]
    octaves = FEATURES // 6
    for octave in range(octaves):
        for c in range(3):
            encoded[pl.ds(octave * 6 + c, 8, stride=FEATURES), :] = sines[c]
            encoded[pl.ds(octave * 6 + 3 + c, 8, stride=FEATURES), :] = cosines[c]
        if octave < octaves - 1:
            for c in range(3):
                twice = sines[c] + sines[c]
                sines[c], cosines[c] = twice * cosines[c], 1.0 - twice * sines[c]


def forward_block(i, coords, first, second_t, head, encoded, zeros_all, ones_all, twos_all, raw):
    row = pl.multiple_of(i * 8, 8)
    encode_rows([coords[c, pl.ds(row, 8), :] for c in range(3)], encoded)
    h_zero = jnp.concatenate(
        [encoded[FEATURES * r : FEATURES * (r + 1), :].astype(jnp.bfloat16) for r in range(8)], axis=1
    )
    at = pl.multiple_of(i * BLOCK, BLOCK)
    zeros_all[:, pl.ds(at, BLOCK)] = h_zero
    twice = jnp.concatenate([h_zero, h_zero], axis=0)
    h_one = jnp.maximum(product(first[...], twice).astype(jnp.bfloat16), 0)
    ones_all[:, pl.ds(at, BLOCK)] = h_one
    h_two = jnp.maximum(product(second_t[...], h_one).astype(jnp.bfloat16), 0)
    twos_all[:, pl.ds(at, BLOCK)] = h_two
    values = product(head[...], h_two)
    for r in range(8):
        for c in range(4):
            raw[c, pl.ds(row + r, 1), :] = values[c : c + 1, r * LANES : (r + 1) * LANES]


def backward_block(i, draw, second, head_t, zeros_all, ones_all, twos_all, grad_first, grad_second):
    at = pl.multiple_of(i * BLOCK, BLOCK)
    d_raw = draw[:, pl.ds(at, BLOCK)].astype(jnp.bfloat16)
    zero = jnp.zeros((), jnp.bfloat16)
    d_two = product(head_t[...], d_raw).astype(jnp.bfloat16)
    d_atwo = jnp.where(twos_all[:, pl.ds(at, BLOCK)] > 0, d_two, zero)
    h_one = ones_all[:, pl.ds(at, BLOCK)]
    grad_second[...] += over_last(h_one, d_atwo)
    d_one = product(second[...], d_atwo).astype(jnp.bfloat16)
    d_aone = jnp.where(h_one > 0, d_one, zero)
    grad_first[...] += over_last(zeros_all[:, pl.ds(at, BLOCK)], d_aone)


def render_middle(ray_depth, raw, spacing, targets, factor, draw):
    row = iota((LANES, LANES), 0)
    column = iota((LANES, LANES), 1)
    same = row // ray_depth == column // ray_depth
    before_sum = jnp.where(jnp.logical_and(same, row < column), 1.0, 0.0)
    behind_sum = jnp.where(jnp.logical_and(same, row > column), 1.0, 0.0)
    whole_sum = jnp.where(same, 1.0, 0.0)
    density_raw = raw[0]
    density = jnp.maximum(density_raw, 0.0) + jnp.log1p(jnp.exp(-jnp.abs(density_raw)))
    optical = density * spacing
    transmit = jnp.exp(-exact(optical, before_sum))
    survive = jnp.exp(-optical)
    blend = transmit * (1.0 - survive)
    d_blend = jnp.zeros_like(blend)
    loss = jnp.zeros_like(blend)
    tints = []
    colors = []
    for c in range(3):
        albedo = 1.0 / (1.0 + jnp.exp(-raw[c + 1]))
        color = exact(blend * (albedo - 1.0), whole_sum) + 1.0
        colors.append(color)
        residual = color - targets[c]
        loss = loss + residual * residual
        grad_color = 2.0 * residual * factor
        d_blend = d_blend + grad_color * (albedo - 1.0)
        tints.append(grad_color * blend * albedo * (1.0 - albedo))
    behind = exact(d_blend * blend, behind_sum)
    d_optical = d_blend * transmit * survive - behind
    d_density = d_optical * spacing * (1.0 / (1.0 + jnp.exp(-density_raw)))
    for c, value in enumerate([d_density] + tints):
        for i in range(value.shape[0]):
            draw[c : c + 1, i * LANES : (i + 1) * LANES] = value[i : i + 1, :]
    return colors, loss * factor


def greet_all(groups, shards):
    me = lax.axis_index("grp") * shards + lax.axis_index("shard")
    total = groups * shards
    barrier = pltpu.get_barrier_semaphore()

    def greet(step, carry):
        other = lax.rem(me + step, total)
        pl.semaphore_signal(
            barrier, inc=1, device_id=(other // shards, lax.rem(other, shards)), device_id_type=MESH
        )
        return carry

    lax.fori_loop(1, total, greet, 0)
    return lambda: pl.semaphore_wait(barrier, total - 1)


def messages(groups, shards, source, landed, sent, arrived):
    me = lax.axis_index("grp") * shards + lax.axis_index("shard")
    total = groups * shards

    def copy(other, place):
        return pltpu.make_async_remote_copy(
            src_ref=source(other),
            dst_ref=landed.at[place],
            send_sem=sent.at[other],
            recv_sem=arrived.at[place],
            device_id=(other // shards, lax.rem(other, shards)),
            device_id_type=MESH,
        )

    def start():
        def one(step, carry):
            copy(lax.rem(me + step, total), me).start()
            return carry

        lax.fori_loop(1, total, one, 0)

    def receive():
        def one(step, carry):
            other = lax.rem(me + total - step, total)
            copy(other, other).wait_recv()
            return carry

        lax.fori_loop(1, total, one, 0)

    def finish():
        def one(step, carry):
            copy(lax.rem(me + step, total), me).wait_send()
            return carry

        lax.fori_loop(1, total, one, 0)

    return start, receive, finish


def plane_gather(source, place, sent, passed, arrived):
    group = lax.axis_index("grp")
    shard = lax.axis_index("shard")
    shards = lax.axis_size("shard")
    chips = shards // 2
    chip = shard // 2
    core = lax.rem(shard, 2)
    partner = chip * 2 + 1 - core
    peers = [lax.rem(chip + step, chips) * 2 + core for step in range(1, chips)]
    origins = [lax.rem(chip + chips - step, chips) * 2 + core for step in range(1, chips)]

    def remote(src, dst, send_sem, recv_sem, to):
        return pltpu.make_async_remote_copy(
            src_ref=src,
            dst_ref=dst,
            send_sem=send_sem,
            recv_sem=recv_sem,
            device_id=(group, to),
            device_id_type=MESH,
        )

    def to(other):
        return remote(source, place(shard), sent.at[other], arrived.at[shard], other)

    def passing(origin):
        return remote(place(origin), place(origin), passed.at[origin], arrived.at[origin], partner)

    def start():
        for other in peers:
            to(other).start()
        to(partner).start()

    def receive(use):
        passing(partner).wait_recv()
        use(partner)
        for origin in origins:
            passing(origin).wait_recv()
            passing(origin).start()
            use(origin)
        for origin in origins:
            across = origin + 1 - 2 * core
            passing(across).wait_recv()
            use(across)

    def finish():
        for other in peers:
            to(other).wait_send()
        to(partner).wait_send()
        for origin in origins:
            passing(origin).wait_send()

    return start, receive, finish


def whole_kernel(
    groups,
    shards,
    latent_ref,
    weight_ref,
    weight_part_ref,
    gain_ref,
    gain_rows_ref,
    head_ref,
    points_ref,
    spacing_ref,
    target_ref,
    scene_ref,
    color_ref,
    loss_ref,
    grad_ref,
    gain_grad_ref,
    latent_grad_ref,
    message,
    landed,
    turned_own,
    turned,
    weights,
    wide_first,
    wide_second,
    first_t,
    second,
    second_t,
    head_t,
    encoded,
    coords,
    zeros_all,
    ones_all,
    twos_all,
    raw,
    draw,
    grad_first,
    grad_second,
    shades,
    landed_shades,
    d_field,
    fields,
    part,
    parts,
    done,
    gain_row,
    landed_gain,
    message_sent,
    message_arrived,
    shade_sent,
    shade_arrived,
    gain_sent,
    gain_arrived,
    turned_sent,
    turned_arrived,
    weight_sent,
    weight_passed,
    weight_arrived,
    field_sent,
    field_passed,
    field_arrived,
    part_sent,
    part_arrived,
    done_sent,
    done_arrived,
):
    group = lax.axis_index("grp")
    shard = lax.axis_index("shard")
    me = group * shards + shard
    total = groups * shards
    tokens, model = latent_ref.shape
    rows = model // shards
    width = head_ref.shape[1]
    ray_count, ray_depth = spacing_ref.shape
    slots = 4 * ray_count // total
    pairs = slots // 2
    fan_scale = width ** (-0.5)
    per_layer = width * width // model
    strips = model // width
    period = FEATURES // strips
    fold_rows = 2 * FOLDED + per_layer
    sent_rows = FOLDED + per_layer
    f32 = jnp.float32
    bf16 = jnp.bfloat16

    wait_all = greet_all(groups, shards)

    latent = latent_ref[...].astype(f32)
    inv_rms = lax.rsqrt(jnp.mean(latent * latent, axis=1, keepdims=True) + norm_eps)
    x_norm = (latent * inv_rms * gain_ref[...]).astype(bf16)
    fold = jnp.where(
        iota((FOLDED, per_layer), 1) % period == iota((FOLDED, per_layer), 0), 1.0, 0.0
    ).astype(bf16)
    folded = product(fold, x_norm[:per_layer])
    folded_high = folded.astype(bf16).astype(f32)
    stacked = jnp.concatenate(
        [folded_high, folded - folded_high, x_norm[per_layer:].astype(f32)], axis=0
    )
    turned_own[...] = stacked.T.astype(bf16).reshape(turned_own.shape)

    scene = scene_ref[...]
    ray_row = iota((ray_count, ray_count), 0)
    ray_column = iota((ray_count, ray_count), 1)
    scene_wide = jnp.broadcast_to(scene, (ray_count, ray_count))
    scene_tall = jnp.sum(jnp.where(ray_row == ray_column, scene_wide, 0), axis=1, keepdims=True)
    same_scene = scene_tall == scene_wide
    rank_wide = jnp.sum(
        jnp.where(jnp.logical_and(same_scene, ray_row < ray_column), 1, 0), axis=0, keepdims=True
    )
    rank_tall = jnp.sum(
        jnp.where(jnp.logical_and(same_scene, ray_column < ray_row), 1, 0), axis=1, keepdims=True
    )
    plane_axes = points_ref[:, :LANES]
    depth_axes = jnp.concatenate([points_ref[:, LANES:], spacing_ref[...]], axis=1)
    owner = iota((total, ray_count), 0)
    mine = scene == owner
    lane = iota((1, LANES), 1)
    for j in range(slots):
        chosen = jnp.where(jnp.logical_and(mine, rank_wide == j), 1.0, 0.0)
        message[:, j, :] = exact(chosen, plane_axes)
        message[:, slots + j, :] = exact(chosen, depth_axes)
    spread = jnp.where(iota((3, LANES), 1) // slots == iota((3, LANES), 0), 1.0, 0.0)
    extra = exact(target_ref[...], spread, (0, 0)) + jnp.where(lane // slots == 3, 1.0, 0.0)
    extra = jnp.where(rank_tall == lane % slots, extra, 0.0)
    message[:, 2 * slots, :] = exact(jnp.where(mine, 1.0, 0.0), extra)
    head_t[...] = (head_ref[...].astype(f32) * fan_scale).T.astype(bf16)
    grad_first[...] = jnp.zeros_like(grad_first)
    grad_second[...] = jnp.zeros_like(grad_second)

    wait_all()

    def weight_place(origin):
        return weights.at[pl.ds(pl.multiple_of(origin * rows, rows), rows)]

    def weight_of(origin):
        return weights[pl.ds(pl.multiple_of(origin * rows, rows), rows), :]

    start_weights, receive_weights, finish_weights = plane_gather(
        weight_ref, weight_place, weight_sent, weight_passed, weight_arrived
    )
    start_messages, receive_messages, finish_messages = messages(
        groups, shards, lambda other: message.at[other], landed, message_sent, message_arrived
    )
    start_weights()
    start_messages()
    weights[pl.ds(pl.multiple_of(shard * rows, rows), rows), :] = weight_ref[...]
    landed[me] = message[me]
    field_sum = [over_first(turned_own[shard], weight_ref[...])]

    def add_field(origin):
        field_sum[0] = field_sum[0] + over_first(turned_own[origin], weight_of(origin))

    receive_weights(add_field)

    def turned_copy(other, place):
        return pltpu.make_async_remote_copy(
            src_ref=turned_own.at[other],
            dst_ref=turned.at[place],
            send_sem=turned_sent.at[other],
            recv_sem=turned_arrived.at[place],
            device_id=(group, other),
            device_id_type=MESH,
        )

    others = [lax.rem(shard + step, shards) for step in range(1, shards)]
    for other in others:
        turned_copy(other, shard).start()
    turned[shard] = turned_own[shard]

    field = field_sum[0]
    first_rows = (field[:FOLDED] + field[FOLDED : 2 * FOLDED]) * fan_scale
    second_rows = field[2 * FOLDED :].astype(bf16).astype(f32) * fan_scale
    for m in range(strips):
        strip = slice(m * width, (m + 1) * width)
        store_rows(wide_first, m, FOLDED, strips, first_rows[:, strip])
        store_rows(wide_second, m, per_layer, strips, second_rows[:, strip])
    first = joined(wide_first)[:FEATURES]
    wide = joined(wide_second)
    first_high = first.astype(bf16).astype(f32)
    first_t[...] = jnp.concatenate([first_high, first - first_high], axis=0).T.astype(bf16)
    second[...] = wide.astype(bf16)
    second_t[...] = wide.T.astype(bf16)

    receive_messages()
    flat = jnp.concatenate([landed[:, j, :] for j in range(slots)], axis=0)
    deep = jnp.concatenate([landed[:, slots + j, :] for j in range(slots)], axis=0)
    extras = landed[:, 2 * slots, :]
    half_rows = pairs * total
    low = lane < ray_depth

    def unpack(values):
        lower, upper = values[:half_rows], values[half_rows:]
        return (
            jnp.where(low, lower, pltpu.roll(upper, ray_depth, 1)),
            jnp.where(low, pltpu.roll(lower, ray_depth, 1), upper),
        )

    coords[0], coords[1] = unpack(flat)
    coords[2], spacing = unpack(deep)

    def widen(c):
        return jnp.concatenate(
            [
                jnp.where(
                    low,
                    extras[:, c * slots + j : c * slots + j + 1],
                    extras[:, c * slots + j + pairs : c * slots + j + pairs + 1],
                )
                for j in range(pairs)
            ],
            axis=0,
        )

    scene_rays = jnp.sum(
        jnp.where(lane // slots == 3, extras, 0.0), axis=(0, 1), keepdims=True
    )
    factor = widen(3) / (total * scene_rays)
    targets = [widen(c) for c in range(3)]
    blocks = half_rows * LANES // BLOCK

    def forward(i, carry):
        forward_block(
            i, coords, first_t, second_t, head_ref, encoded, zeros_all, ones_all, twos_all, raw
        )
        return carry

    lax.fori_loop(0, blocks, forward, 0)
    colors, losses = render_middle(ray_depth, raw, spacing, targets, factor, draw)
    shade = jnp.where(
        lane == 3 * slots, jnp.sum(losses, axis=(0, 1), keepdims=True) * (1.0 / ray_depth), 0.0
    )
    shade = jnp.broadcast_to(shade, (total, LANES))
    for c in range(3):
        for j in range(pairs):
            values = colors[c][j * total : (j + 1) * total]
            at = c * slots + j
            shade = jnp.where(lane == at, values[:, 0:1], shade)
            shade = jnp.where(lane == at + pairs, values[:, ray_depth : ray_depth + 1], shade)
    shades[:, 0, :] = shade
    start_shades, receive_shades, finish_shades = messages(
        groups, shards, lambda other: shades.at[other], landed_shades, shade_sent, shade_arrived
    )
    start_shades()
    landed_shades[me] = shades[me]

    def backward(i, carry):
        backward_block(
            i, draw, second, head_t, zeros_all, ones_all, twos_all, grad_first, grad_second
        )
        return carry

    lax.fori_loop(0, blocks, backward, 0)

    for lanes in range(width // LANES):
        wide_first[lanes, :FEATURES, :] = grad_first[:, lanes * LANES : (lanes + 1) * LANES]
        wide_second[lanes] = grad_second[:, lanes * LANES : (lanes + 1) * LANES]
    columns = model // HALVES
    for m in range(strips):
        half, place = divmod(m * width, columns)
        strip = slice(place, place + width)
        head_rows = load_rows(wide_first, m, FOLDED, strips)
        head_rows = jnp.where(iota((FOLDED, 1), 0) < period, head_rows, 0.0)
        d_field[half, :FOLDED, strip] = head_rows.astype(bf16)
        d_field[half, FOLDED:, strip] = load_rows(wide_second, m, per_layer, strips).astype(bf16)

    gathers = [
        plane_gather(
            d_field.at[half],
            lambda origin, half=half: fields.at[half, origin],
            field_sent.at[half],
            field_passed.at[half],
            field_arrived.at[half],
        )
        for half in range(HALVES)
    ]
    for half in range(HALVES):
        gathers[half][0]()

    for other in others:
        turned_copy(other, other).wait_recv()

    group_steps = [lax.rem(group + step, groups) for step in range(1, groups)]

    def part_copy(half, other, place):
        return pltpu.make_async_remote_copy(
            src_ref=part.at[half, other],
            dst_ref=parts.at[half, place],
            send_sem=part_sent.at[half, other],
            recv_sem=part_arrived.at[half, place],
            device_id=(other, shard),
            device_id_type=MESH,
        )

    def done_copy(half, other, place):
        return pltpu.make_async_remote_copy(
            src_ref=done.at[half, place],
            dst_ref=done.at[half, place],
            send_sem=done_sent.at[half, other],
            recv_sem=done_arrived.at[half, place],
            device_id=(other, shard),
            device_id_type=MESH,
        )

    def head_term(origin, values):
        lead = values[:FOLDED]
        return product(turned[origin], jnp.concatenate([lead, lead, values[FOLDED:]], axis=0))

    def gather_half(half):
        head_sum = [head_term(shard, d_field[half])]

        def add_head(origin):
            head_sum[0] = head_sum[0] + head_term(origin, fields[half, origin])

        gathers[half][1](add_head)
        part[half] = head_sum[0].astype(bf16).reshape(part.shape[1:])
        for other in group_steps:
            part_copy(half, other, group).start()

    gain_terms = []

    def sum_half(half):
        slice_sum = part[half, group].astype(f32)
        for other in group_steps:
            part_copy(half, other, other).wait_recv()
            slice_sum = slice_sum + parts[half, other].astype(f32)
        done[half, group] = slice_sum.astype(bf16)
        for other in group_steps:
            done_copy(half, other, group).start()
        weight = weight_part_ref[group][:, half * columns : (half + 1) * columns].astype(f32)
        gain_terms.append(exact(jnp.ones((8, columns), f32), slice_sum * weight, (1, 1)))

    gather_half(0)
    gather_half(1)
    sum_half(0)
    sum_half(1)
    slice_rows = rows // groups
    gain_row[0:1, :slice_rows] = (gain_terms[0] + gain_terms[1])[0:1]
    start_gain, receive_gain, finish_gain = messages(
        groups, shards, lambda other: gain_row, landed_gain, gain_sent, gain_arrived
    )
    start_gain()
    landed_gain[me] = gain_row[...]

    token = iota((tokens, sent_rows), 0)
    source = jnp.where(token < per_layer, token % period, token - per_layer + FOLDED)
    copies = jnp.where(source == iota((tokens, sent_rows), 1), 1.0, 0.0).astype(bf16)
    own_field = jnp.concatenate([d_field[half] for half in range(HALVES)], axis=1)
    d_norm = over_last(product(copies, own_field).astype(bf16), weights[...])
    latent = latent_ref[...].astype(f32)
    inv_rms = lax.rsqrt(jnp.mean(latent * latent, axis=1, keepdims=True) + norm_eps)
    x_hat = latent * inv_rms
    d_scaled = d_norm * gain_ref[...]
    latent_grad_ref[...] = (
        inv_rms * (d_scaled - x_hat * jnp.mean(d_scaled * x_hat, axis=1, keepdims=True))
    ).astype(bf16)

    receive_shades()
    returned = landed_shades[:, 0, :]
    loss_ref[...] = jnp.sum(
        jnp.where(lane == 3 * slots, returned, 0.0), axis=(0, 1), keepdims=True
    )
    picked = exact(returned, jnp.where(mine, 1.0, 0.0), (0, 0))
    place = iota((LANES, ray_count), 0)
    for c in range(3):
        color_ref[c : c + 1, :] = jnp.sum(
            jnp.where(place == c * slots + rank_wide, picked, 0.0), axis=0, keepdims=True
        )

    for half in range(HALVES):
        grad_ref[group, :, half * columns : (half + 1) * columns] = done[half, group]
        for other in group_steps:
            done_copy(half, other, other).wait_recv()
            grad_ref[other, :, half * columns : (half + 1) * columns] = done[half, other]
    receive_gain()
    gains = landed_gain[:, 0, :slice_rows]
    gains = jnp.concatenate([gains[g * shards : (g + 1) * shards] for g in range(groups)], axis=1)
    gain_grad_ref[...] = gains / gain_rows_ref[...]

    finish_weights()
    finish_messages()
    finish_shades()
    finish_gain()
    for other in others:
        turned_copy(other, shard).wait_send()
    for half in range(HALVES):
        gathers[half][2]()
        for other in group_steps:
            part_copy(half, other, group).wait_send()
            done_copy(half, other, group).wait_send()


def body(
    latents,
    head_weight,
    norm_gain,
    color_head,
    sample_points,
    sample_spacing,
    ray_targets,
    ray_scene,
):
    groups, shards = lax.axis_size("grp"), lax.axis_size("shard")
    devices = groups * shards
    ray_count, ray_depth = sample_spacing.shape
    tokens, model = latents.shape
    width = color_head.shape[1]
    rows = model // shards
    slots = 4 * ray_count // devices
    per_layer = width * width // model
    fold_rows = 2 * FOLDED + per_layer
    sent_rows = FOLDED + per_layer
    samples = slots * devices * ray_depth
    columns = model // HALVES
    slice_rows = rows // groups
    in_vmem = pl.BlockSpec(memory_space=pltpu.VMEM)
    dma = pltpu.SemaphoreType.DMA
    f32, bf16 = jnp.float32, jnp.bfloat16
    vmem = pltpu.VMEM
    colors, loss, head, gain, latent_grad = pl.pallas_call(
        functools.partial(whole_kernel, groups, shards),
        in_specs=[in_vmem] * 10,
        out_specs=[in_vmem] * 5,
        out_shape=[
            jax.ShapeDtypeStruct((3, ray_count), f32),
            jax.ShapeDtypeStruct((1, 1), f32),
            jax.ShapeDtypeStruct((groups, slice_rows, model), bf16),
            jax.ShapeDtypeStruct((shards, rows), f32),
            jax.ShapeDtypeStruct((tokens, model), bf16),
        ],
        scratch_shapes=[
            vmem((devices, 2 * slots + 1, LANES), f32),
            vmem((devices, 2 * slots + 1, LANES), f32),
            vmem((shards, rows, fold_rows), bf16),
            vmem((shards, rows, fold_rows), bf16),
            vmem((model, model), bf16),
            vmem((width // LANES, FOLDED * model // width, LANES), f32),
            vmem((width // LANES, width, LANES), f32),
            vmem((width, 2 * FEATURES), bf16),
            vmem((width, width), bf16),
            vmem((width, width), bf16),
            vmem((width, 4), bf16),
            vmem((8 * FEATURES, LANES), f32),
            vmem((3, samples // LANES, LANES), f32),
            vmem((FEATURES, samples), bf16),
            vmem((width, samples), bf16),
            vmem((width, samples), bf16),
            vmem((4, samples // LANES, LANES), f32),
            vmem((4, samples), f32),
            vmem((FEATURES, width), f32),
            vmem((width, width), f32),
            vmem((devices, 1, LANES), f32),
            vmem((devices, 1, LANES), f32),
            vmem((HALVES, sent_rows, columns), bf16),
            vmem((HALVES, shards, sent_rows, columns), bf16),
            vmem((HALVES, groups, slice_rows, columns), bf16),
            vmem((HALVES, groups, slice_rows, columns), bf16),
            vmem((HALVES, groups, slice_rows, columns), bf16),
            vmem((1, LANES), f32),
            vmem((devices, 1, LANES), f32),
            dma((devices,)),
            dma((devices,)),
            dma((devices,)),
            dma((devices,)),
            dma((devices,)),
            dma((devices,)),
            dma((shards,)),
            dma((shards,)),
            dma((shards,)),
            dma((shards,)),
            dma((shards,)),
            dma((HALVES, shards)),
            dma((HALVES, shards)),
            dma((HALVES, shards)),
            dma((HALVES, groups)),
            dma((HALVES, groups)),
            dma((HALVES, groups)),
            dma((HALVES, groups)),
        ],
        compiler_params=pltpu.CompilerParams(collective_id=1, has_side_effects=True),
    )(
        latents,
        head_weight,
        head_weight.reshape(groups, slice_rows, model),
        norm_gain.reshape(1, model),
        norm_gain.reshape(shards, rows),
        color_head,
        sample_points,
        sample_spacing,
        ray_targets,
        ray_scene.reshape(1, ray_count),
    )
    head_grad = head.astype(f32).reshape(rows, model)
    return (colors, loss[0, 0], head_grad, gain.reshape(model), latent_grad)


def solution(mesh):
    placed = (
        P(("grp", "shard"), None),
        P("shard", None),
        P(),
        P(),
        P(("grp", "shard"), None),
        P(("grp", "shard"), None),
        P(None, ("grp", "shard")),
        P(("grp", "shard")),
    )
    return jax.shard_map(
        body,
        mesh=mesh,
        in_specs=placed,
        out_specs=(
            P(None, ("grp", "shard")),
            P(),
            P("shard", None),
            P(),
            P(("grp", "shard"), None),
        ),
        check_vma=False,
    )
```

```python
import functools

import jax
import jax.numpy as jnp
from jax import lax
from jax.experimental import pallas as pl
from jax.experimental.pallas import tpu as pltpu
from jax.sharding import PartitionSpec as P

norm_eps = 1e-06

LANES = 128
HALVES = 2
FEATURES = 48
FOLDED = 16
BLOCK = 1024
SINE = (3.14159265358979, -5.16771278004997, 2.55016403987735, -0.599264529320792, 0.0821458866111282, -0.00737043094571435, 0.000466302805767613, -0.0000219153534478303)
MESH = pl.DeviceIdType.MESH


def sine_of_pi(turns):
    whole = jnp.floor(turns + 0.5)
    rest = turns - whole
    odd = whole - 2.0 * jnp.floor(whole * 0.5)
    square = rest * rest
    value = jnp.full_like(square, SINE[-1])
    for coefficient in SINE[-2::-1]:
        value = value * square + coefficient
    return value * (rest * (1.0 - 2.0 * odd))


def product(a, b):
    return jnp.dot(a, b, preferred_element_type=jnp.float32)


def exact(a, b, contract=(1, 0)):
    return lax.dot_general(
        a,
        b,
        (((contract[0],), (contract[1],)), ((), ())),
        preferred_element_type=jnp.float32,
        precision=lax.Precision.HIGHEST,
    )


def over_first(a, b):
    return lax.dot_general(a, b, (((0,), (0,)), ((), ())), preferred_element_type=jnp.float32)


def over_last(a, b):
    return lax.dot_general(a, b, (((1,), (1,)), ((), ())), preferred_element_type=jnp.float32)


def iota(shape, axis):
    return lax.broadcasted_iota(jnp.int32, shape, axis)


def store_rows(ref, start, count, stride, values):
    for lanes in range(ref.shape[0]):
        ref[lanes, pl.ds(start, count, stride=stride), :] = values[:, lanes * LANES : (lanes + 1) * LANES]


def load_rows(ref, start, count, stride):
    return jnp.concatenate(
        [ref[lanes, pl.ds(start, count, stride=stride), :] for lanes in range(ref.shape[0])], axis=1
    )


def joined(ref):
    return jnp.concatenate([ref[lanes] for lanes in range(ref.shape[0])], axis=1)


def encode_rows(axes, encoded):
    sines = [sine_of_pi(a) for a in axes]
    cosines = [sine_of_pi(a + 0.5) for a in axes]
    octaves = FEATURES // 6
    for octave in range(octaves):
        for c in range(3):
            encoded[pl.ds(octave * 6 + c, 8, stride=FEATURES), :] = sines[c]
            encoded[pl.ds(octave * 6 + 3 + c, 8, stride=FEATURES), :] = cosines[c]
        if octave < octaves - 1:
            for c in range(3):
                twice = sines[c] + sines[c]
                sines[c], cosines[c] = twice * cosines[c], 1.0 - twice * sines[c]


def forward_block(i, coords, first, second_t, head, encoded, zeros_all, ones_all, twos_all, raw):
    row = pl.multiple_of(i * 8, 8)
    encode_rows([coords[c, pl.ds(row, 8), :] for c in range(3)], encoded)
    h_zero = jnp.concatenate(
        [encoded[FEATURES * r : FEATURES * (r + 1), :].astype(jnp.bfloat16) for r in range(8)], axis=1
    )
    at = pl.multiple_of(i * BLOCK, BLOCK)
    zeros_all[:, pl.ds(at, BLOCK)] = h_zero
    twice = jnp.concatenate([h_zero, h_zero], axis=0)
    h_one = jnp.maximum(product(first[...], twice).astype(jnp.bfloat16), 0)
    ones_all[:, pl.ds(at, BLOCK)] = h_one
    h_two = jnp.maximum(product(second_t[...], h_one).astype(jnp.bfloat16), 0)
    twos_all[:, pl.ds(at, BLOCK)] = h_two
    values = product(head[...], h_two)
    for r in range(8):
        for c in range(4):
            raw[c, pl.ds(row + r, 1), :] = values[c : c + 1, r * LANES : (r + 1) * LANES]


def backward_block(i, draw, second, head_t, zeros_all, ones_all, twos_all, grad_first, grad_second):
    at = pl.multiple_of(i * BLOCK, BLOCK)
    d_raw = draw[:, pl.ds(at, BLOCK)].astype(jnp.bfloat16)
    zero = jnp.zeros((), jnp.bfloat16)
    d_two = product(head_t[...], d_raw).astype(jnp.bfloat16)
    d_atwo = jnp.where(twos_all[:, pl.ds(at, BLOCK)] > 0, d_two, zero)
    h_one = ones_all[:, pl.ds(at, BLOCK)]
    grad_second[...] += over_last(h_one, d_atwo)
    d_one = product(second[...], d_atwo).astype(jnp.bfloat16)
    d_aone = jnp.where(h_one > 0, d_one, zero)
    grad_first[...] += over_last(zeros_all[:, pl.ds(at, BLOCK)], d_aone)


def render_middle(ray_depth, raw, spacing, targets, factor, draw):
    row = iota((LANES, LANES), 0)
    column = iota((LANES, LANES), 1)
    same = row // ray_depth == column // ray_depth
    before_sum = jnp.where(jnp.logical_and(same, row < column), 1.0, 0.0)
    behind_sum = jnp.where(jnp.logical_and(same, row > column), 1.0, 0.0)
    whole_sum = jnp.where(same, 1.0, 0.0)
    density_raw = raw[0]
    density = jnp.maximum(density_raw, 0.0) + jnp.log1p(jnp.exp(-jnp.abs(density_raw)))
    optical = density * spacing
    transmit = jnp.exp(-exact(optical, before_sum))
    survive = jnp.exp(-optical)
    blend = transmit * (1.0 - survive)
    d_blend = jnp.zeros_like(blend)
    loss = jnp.zeros_like(blend)
    tints = []
    colors = []
    for c in range(3):
        albedo = 1.0 / (1.0 + jnp.exp(-raw[c + 1]))
        color = exact(blend * (albedo - 1.0), whole_sum) + 1.0
        colors.append(color)
        residual = color - targets[c]
        loss = loss + residual * residual
        grad_color = 2.0 * residual * factor
        d_blend = d_blend + grad_color * (albedo - 1.0)
        tints.append(grad_color * blend * albedo * (1.0 - albedo))
    behind = exact(d_blend * blend, behind_sum)
    d_optical = d_blend * transmit * survive - behind
    d_density = d_optical * spacing * (1.0 / (1.0 + jnp.exp(-density_raw)))
    for c, value in enumerate([d_density] + tints):
        for i in range(value.shape[0]):
            draw[c : c + 1, i * LANES : (i + 1) * LANES] = value[i : i + 1, :]
    return colors, loss * factor


def ray_room(devices, shards, ray_count):
    slots = 4 * ray_count // devices
    others = pl.cdiv(devices * (ray_count - slots), devices - 1)
    return pl.cdiv(others, 16) * 16, pl.cdiv(pl.cdiv(slots * devices, shards), 16) * 16


def greet_all(groups, shards):
    me = lax.axis_index("grp") * shards + lax.axis_index("shard")
    total = groups * shards
    barrier = pltpu.get_barrier_semaphore()

    def greet(step, carry):
        other = lax.rem(me + step, total)
        pl.semaphore_signal(
            barrier, inc=1, device_id=(other // shards, lax.rem(other, shards)), device_id_type=MESH
        )
        return carry

    lax.fori_loop(1, total, greet, 0)
    return lambda: pl.semaphore_wait(barrier, total - 1)


def messages(groups, shards, source, landed, sent, arrived):
    me = lax.axis_index("grp") * shards + lax.axis_index("shard")
    total = groups * shards

    def copy(other, place):
        return pltpu.make_async_remote_copy(
            src_ref=source(other),
            dst_ref=landed.at[place],
            send_sem=sent.at[other],
            recv_sem=arrived.at[place],
            device_id=(other // shards, lax.rem(other, shards)),
            device_id_type=MESH,
        )

    def start():
        def one(step, carry):
            copy(lax.rem(me + step, total), me).start()
            return carry

        lax.fori_loop(1, total, one, 0)

    def receive():
        def one(step, carry):
            other = lax.rem(me + total - step, total)
            copy(other, other).wait_recv()
            return carry

        lax.fori_loop(1, total, one, 0)

    def finish():
        def one(step, carry):
            copy(lax.rem(me + step, total), me).wait_send()
            return carry

        lax.fori_loop(1, total, one, 0)

    return start, receive, finish


def plane_gather(source, place, sent, passed, arrived):
    group = lax.axis_index("grp")
    shard = lax.axis_index("shard")
    shards = lax.axis_size("shard")
    chips = shards // 2
    chip = shard // 2
    core = lax.rem(shard, 2)
    partner = chip * 2 + 1 - core
    peers = [lax.rem(chip + step, chips) * 2 + core for step in range(1, chips)]
    origins = [lax.rem(chip + chips - step, chips) * 2 + core for step in range(1, chips)]

    def remote(src, dst, send_sem, recv_sem, to):
        return pltpu.make_async_remote_copy(
            src_ref=src,
            dst_ref=dst,
            send_sem=send_sem,
            recv_sem=recv_sem,
            device_id=(group, to),
            device_id_type=MESH,
        )

    def to(other):
        return remote(source, place(shard), sent.at[other], arrived.at[shard], other)

    def passing(origin):
        return remote(place(origin), place(origin), passed.at[origin], arrived.at[origin], partner)

    def start():
        for other in peers:
            to(other).start()
        to(partner).start()

    def receive(use):
        passing(partner).wait_recv()
        use(partner)
        for origin in origins:
            passing(origin).wait_recv()
            passing(origin).start()
            use(origin)
        for origin in origins:
            across = origin + 1 - 2 * core
            passing(across).wait_recv()
            use(across)

    def finish():
        for other in peers:
            to(other).wait_send()
        to(partner).wait_send()
        for origin in origins:
            passing(origin).wait_send()

    return start, receive, finish


def whole_kernel(
    groups,
    shards,
    latent_ref,
    weight_ref,
    weight_part_ref,
    gain_ref,
    gain_rows_ref,
    head_ref,
    points_ref,
    spacing_ref,
    target_ref,
    scene_ref,
    color_ref,
    loss_ref,
    grad_ref,
    gain_grad_ref,
    latent_grad_ref,
    count_row,
    landed_counts,
    lead_own,
    leads,
    hot_part,
    hot_parts,
    hot_piece,
    hot_all,
    message,
    landed,
    turned_own,
    turned,
    weights,
    wide_first,
    wide_second,
    first_t,
    second,
    second_t,
    head_t,
    encoded,
    coords,
    zeros_all,
    ones_all,
    twos_all,
    raw,
    draw,
    grad_first,
    grad_second,
    shades,
    landed_shades,
    d_field,
    fields,
    part,
    parts,
    done,
    gain_row,
    landed_gain,
    count_sent,
    count_arrived,
    lead_sent,
    lead_passed,
    lead_arrived,
    hot_sent,
    hot_arrived,
    piece_sent,
    piece_passed,
    piece_arrived,
    message_sent,
    message_arrived,
    shade_sent,
    shade_arrived,
    gain_sent,
    gain_arrived,
    turned_sent,
    turned_arrived,
    weight_sent,
    weight_passed,
    weight_arrived,
    field_sent,
    field_passed,
    field_arrived,
    part_sent,
    part_arrived,
    done_sent,
    done_arrived,
):
    group = lax.axis_index("grp")
    shard = lax.axis_index("shard")
    me = group * shards + shard
    total = groups * shards
    tokens, model = latent_ref.shape
    rows = model // shards
    width = head_ref.shape[1]
    ray_count, ray_depth = spacing_ref.shape
    slots = 4 * ray_count // total
    fan_scale = width ** (-0.5)
    per_layer = width * width // model
    strips = model // width
    period = FEATURES // strips
    fold_rows = 2 * FOLDED + per_layer
    sent_rows = FOLDED + per_layer
    own_rays, hot_rays = ray_room(total, shards, ray_count)
    f32 = jnp.float32
    bf16 = jnp.bfloat16

    wait_all = greet_all(groups, shards)

    latent = latent_ref[...].astype(f32)
    inv_rms = lax.rsqrt(jnp.mean(latent * latent, axis=1, keepdims=True) + norm_eps)
    x_norm = (latent * inv_rms * gain_ref[...]).astype(bf16)
    fold = jnp.where(
        iota((FOLDED, per_layer), 1) % period == iota((FOLDED, per_layer), 0), 1.0, 0.0
    ).astype(bf16)
    folded = product(fold, x_norm[:per_layer])
    folded_high = folded.astype(bf16).astype(f32)
    stacked = jnp.concatenate(
        [folded_high, folded - folded_high, x_norm[per_layer:].astype(f32)], axis=0
    )
    turned_own[...] = stacked.T.astype(bf16).reshape(turned_own.shape)

    scene = scene_ref[...]
    lane = iota((1, LANES), 1)
    ray_row = iota((ray_count, ray_count), 0)
    ray_column = iota((ray_count, ray_count), 1)
    scene_wide = jnp.broadcast_to(scene, (ray_count, ray_count))
    scene_tall = jnp.sum(jnp.where(ray_row == ray_column, scene_wide, 0), axis=1, keepdims=True)
    count_row[...] = jnp.sum(jnp.where(scene_tall == lane, 1.0, 0.0), axis=0, keepdims=True)
    same_scene = scene_tall == scene_wide
    rank_wide = jnp.sum(
        jnp.where(jnp.logical_and(same_scene, ray_row < ray_column), 1, 0), axis=0, keepdims=True
    )
    rank_tall = jnp.sum(
        jnp.where(jnp.logical_and(same_scene, ray_column < ray_row), 1, 0), axis=1, keepdims=True
    )
    head_t[...] = (head_ref[...].astype(f32) * fan_scale).T.astype(bf16)
    grad_first[...] = jnp.zeros_like(grad_first)
    grad_second[...] = jnp.zeros_like(grad_second)

    wait_all()

    def turned_copy(other, place):
        return pltpu.make_async_remote_copy(
            src_ref=turned_own.at[other],
            dst_ref=turned.at[place],
            send_sem=turned_sent.at[other],
            recv_sem=turned_arrived.at[place],
            device_id=(group, other),
            device_id_type=MESH,
        )

    def weight_place(origin):
        return weights.at[pl.ds(pl.multiple_of(origin * rows, rows), rows)]

    def weight_of(origin):
        return weights[pl.ds(pl.multiple_of(origin * rows, rows), rows), :]

    others = [lax.rem(shard + step, shards) for step in range(1, shards)]
    start_counts, receive_counts, finish_counts = messages(
        groups, shards, lambda other: count_row, landed_counts, count_sent, count_arrived
    )
    start_weights, receive_weights, finish_weights = plane_gather(
        weight_ref, weight_place, weight_sent, weight_passed, weight_arrived
    )
    start_messages, receive_messages, finish_messages = messages(
        groups, shards, lambda other: message.at[other], landed, message_sent, message_arrived
    )
    start_lead, receive_lead, finish_lead = plane_gather(
        lead_own, lambda origin: leads.at[origin], lead_sent, lead_passed, lead_arrived
    )
    start_counts()
    for other in others:
        turned_copy(other, shard).start()
    start_weights()
    landed_counts[me] = count_row[...]
    turned[shard] = turned_own[shard]
    weights[pl.ds(pl.multiple_of(shard * rows, rows), rows), :] = weight_ref[...]

    receive_counts()
    counts = landed_counts[:, 0, :]
    hot_lanes = jnp.min(jnp.where(counts == slots, 1, 0), axis=0, keepdims=True)
    hot = jnp.sum(jnp.where(hot_lanes > 0, lane, 0), axis=1, keepdims=True)
    hot_here = hot // shards == group
    hot_ray = scene == hot
    hot_target = (hot // shards) * shards + (me * slots + rank_wide) % shards
    owner = iota((total, ray_count), 0)
    mine = jnp.where(hot_ray, -1, scene) == owner
    led = jnp.where(hot_ray, hot_target, -1) == owner
    payload = jnp.concatenate([points_ref[...], spacing_ref[...]], axis=1)
    chosen = jnp.concatenate(
        [jnp.where(jnp.where(mine, rank_wide, -1) == j, 1.0, 0.0) for j in range(slots)]
        + [jnp.where(led, 1.0, 0.0)],
        axis=0,
    )
    filled = exact(chosen, payload)
    for j in range(slots + 1):
        message[:, 2 * j, :] = filled[j * total : (j + 1) * total, :LANES]
        message[:, 2 * j + 1, :] = filled[j * total : (j + 1) * total, LANES:]
    spread = jnp.where(iota((3, LANES), 1) % 4 == iota((3, LANES), 0), 1.0, 0.0)
    extra = exact(target_ref[...], spread, (0, 0)) + jnp.where(lane % 4 == 3, 1.0, 0.0)
    own_extra = jnp.where(rank_tall == lane // 4, extra, 0.0)
    hot_extra = jnp.where(lane // 4 == slots, extra, 0.0)
    message[:, 2 * slots + 2, :] = exact(jnp.where(mine, 1.0, 0.0), own_extra) + exact(
        jnp.where(led, 1.0, 0.0), hot_extra
    )
    start_messages()
    landed[me] = message[me]

    for other in others:
        turned_copy(other, other).wait_recv()
    hot_shard = jnp.where(hot_here, hot % shards, -1)
    lead = jnp.zeros((rows, fold_rows), f32)
    for origin in range(shards):
        lead = lead + jnp.where(hot_shard == origin, turned[origin].astype(f32), 0.0)
    lead_own[...] = lead.astype(bf16)
    start_lead()
    leads[shard] = lead_own[...]

    field_sum = [over_first(turned_own[shard], weight_ref[...])]

    def add_field(origin):
        field_sum[0] = field_sum[0] + over_first(turned_own[origin], weight_of(origin))

    receive_weights(add_field)

    def set_weights(which, field):
        first_rows = (field[:FOLDED] + field[FOLDED : 2 * FOLDED]) * fan_scale
        second_rows = field[2 * FOLDED :].astype(bf16).astype(f32) * fan_scale
        for m in range(strips):
            strip = slice(m * width, (m + 1) * width)
            store_rows(wide_first, m, FOLDED, strips, first_rows[:, strip])
            store_rows(wide_second, m, per_layer, strips, second_rows[:, strip])
        first = joined(wide_first)[:FEATURES]
        wide = joined(wide_second)
        first_high = first.astype(bf16).astype(f32)
        first_t[which] = jnp.concatenate([first_high, first - first_high], axis=0).T.astype(bf16)
        second[which] = wide.astype(bf16)
        second_t[which] = wide.T.astype(bf16)

    set_weights(0, field_sum[0])

    receive_messages()
    wanted = jnp.where(lane == me, 1.0, 0.0) * jnp.where(hot == me, 0.0, 1.0)
    numbers = exact(jnp.broadcast_to(wanted, (8, LANES)), counts, (1, 1))
    before = jnp.where(iota((total, total), 0) < iota((total, total), 1), 1.0, 0.0)
    offsets = exact(numbers, before)[0:1]
    numbers = numbers[0:1]
    extras = landed[:, 2 * slots + 2, :]

    def arrived_slot(j):
        lifted = extras if j == 0 else pltpu.roll(extras, LANES - 4 * j, 1)
        return jnp.concatenate([landed[:, 2 * j, :], landed[:, 2 * j + 1, :], lifted], axis=1)

    slot_row = iota((own_rays, total), 0).astype(f32)
    keeps = [
        jnp.where(jnp.where(numbers > j, offsets + j, -1.0) == slot_row, 1.0, 0.0)
        for j in range(slots)
    ]
    own_slots = sum(exact(keeps[j], arrived_slot(j)) for j in range(slots))
    hot_place = (iota((hot_rays, total), 0) * shards + shard) // slots
    hot_keep = jnp.where(hot_place == iota((hot_rays, total), 1), 1.0, 0.0)
    hot_slots = exact(hot_keep, arrived_slot(slots))
    own_pairs, hot_pairs = own_rays // 2, hot_rays // 2
    all_pairs = own_pairs + hot_pairs
    lower = jnp.concatenate([own_slots[:own_pairs], hot_slots[:hot_pairs]], axis=0)
    upper = jnp.concatenate([own_slots[own_pairs:], hot_slots[hot_pairs:]], axis=0)
    low = lane < ray_depth

    def unpack(at):
        left, right = lower[:, at : at + LANES], upper[:, at : at + LANES]
        return (
            jnp.where(low, left, pltpu.roll(right, ray_depth, 1)),
            jnp.where(low, pltpu.roll(left, ray_depth, 1), right),
        )

    coords[0], coords[1] = unpack(0)
    coords[2], spacing = unpack(LANES)

    def widen(c):
        at = 2 * LANES + c
        return jnp.where(low, lower[:, at : at + 1], upper[:, at : at + 1])

    own_count = jnp.sum(numbers, axis=1, keepdims=True)
    own_factor = 1.0 / (total * jnp.maximum(own_count, 1.0))
    hot_factor = 1.0 / (total * total * slots)
    factor = widen(3) * jnp.where(iota((all_pairs, 1), 0) < own_pairs, own_factor, hot_factor)
    targets = [widen(c) for c in range(3)]
    own_blocks = own_pairs // 8
    blocks = all_pairs // 8

    def forward(which):
        def step(i, carry):
            forward_block(
                i,
                coords,
                first_t.at[which],
                second_t.at[which],
                head_ref,
                encoded,
                zeros_all,
                ones_all,
                twos_all,
                raw,
            )
            return carry

        return step

    lax.fori_loop(0, own_blocks, forward(0), 0)
    lead_field = [over_first(lead_own[...], weight_ref[...])]

    def add_lead(origin):
        lead_field[0] = lead_field[0] + over_first(leads[origin], weight_of(origin))

    receive_lead(add_lead)
    set_weights(1, lead_field[0])
    lax.fori_loop(own_blocks, blocks, forward(1), 0)
    colors, losses = render_middle(ray_depth, raw, spacing, targets, factor, draw)
    shade = jnp.where(
        lane == 4 * slots + 4,
        jnp.sum(losses, axis=(0, 1), keepdims=True) * (1.0 / ray_depth),
        0.0,
    )

    def color_rows(start, stop):
        columns = []
        for side in (0, ray_depth):
            values = jnp.zeros((stop - start, LANES), f32)
            for c in range(3):
                values = jnp.where(lane == c, colors[c][start:stop, side : side + 1], values)
            columns.append(values)
        return jnp.concatenate(columns, axis=0)

    own_colors = color_rows(0, own_pairs)
    hot_colors = color_rows(own_pairs, all_pairs)
    for j in range(slots):
        back = exact(keeps[j], own_colors, (0, 0))
        shade = shade + (back if j == 0 else pltpu.roll(back, 4 * j, 1))
    shade = shade + pltpu.roll(exact(hot_keep, hot_colors, (0, 0)), 4 * slots, 1)
    shades[:, 0, :] = shade
    start_shades, receive_shades, finish_shades = messages(
        groups, shards, lambda other: shades.at[other], landed_shades, shade_sent, shade_arrived
    )
    start_shades()
    landed_shades[me] = shades[me]

    def backward(which):
        def step(i, carry):
            backward_block(
                i, draw, second.at[which], head_t, zeros_all, ones_all, twos_all, grad_first, grad_second
            )
            return carry

        return step

    columns = model // HALVES
    piece = model // shards

    def field_strips():
        for lanes in range(width // LANES):
            at = slice(lanes * LANES, (lanes + 1) * LANES)
            wide_first[lanes, :FEATURES, :] = grad_first[:, at]
            wide_second[lanes] = grad_second[:, at]
        strip_values = []
        for m in range(strips):
            head_rows = load_rows(wide_first, m, FOLDED, strips)
            head_rows = jnp.where(iota((FOLDED, 1), 0) < period, head_rows, 0.0)
            strip_values.append(
                jnp.concatenate([head_rows, load_rows(wide_second, m, per_layer, strips)], axis=0)
            )
        return strip_values

    def hot_copy(other, place):
        return pltpu.make_async_remote_copy(
            src_ref=hot_part.at[other],
            dst_ref=hot_parts.at[place],
            send_sem=hot_sent.at[other],
            recv_sem=hot_arrived.at[place],
            device_id=(group, other),
            device_id_type=MESH,
        )

    lax.fori_loop(own_blocks, blocks, backward(1), 0)
    hot_strips = jnp.concatenate(field_strips(), axis=1)
    for p in range(shards):
        hot_part[p] = hot_strips[:, p * piece : (p + 1) * piece].astype(bf16)
    for other in others:
        hot_copy(other, shard).start()
    grad_first[...] = jnp.zeros_like(grad_first)
    grad_second[...] = jnp.zeros_like(grad_second)
    lax.fori_loop(0, own_blocks, backward(0), 0)
    for m, values in enumerate(field_strips()):
        half, place = divmod(m * width, columns)
        d_field[half, :, place : place + width] = values.astype(bf16)

    gathers = [
        plane_gather(
            d_field.at[half],
            lambda origin, half=half: fields.at[half, origin],
            field_sent.at[half],
            field_passed.at[half],
            field_arrived.at[half],
        )
        for half in range(HALVES)
    ]
    for half in range(HALVES):
        gathers[half][0]()
    piece_sum = hot_part[shard].astype(f32)
    for other in others:
        hot_copy(other, other).wait_recv()
        piece_sum = piece_sum + hot_parts[other].astype(f32)
    hot_piece[...] = piece_sum.astype(bf16)
    start_hot, receive_hot, finish_hot = plane_gather(
        hot_piece, lambda origin: hot_all.at[origin], piece_sent, piece_passed, piece_arrived
    )
    start_hot()
    hot_all[shard] = hot_piece[...]

    group_steps = [lax.rem(group + step, groups) for step in range(1, groups)]

    def part_copy(half, other, place):
        return pltpu.make_async_remote_copy(
            src_ref=part.at[half, other],
            dst_ref=parts.at[half, place],
            send_sem=part_sent.at[half, other],
            recv_sem=part_arrived.at[half, place],
            device_id=(other, shard),
            device_id_type=MESH,
        )

    def done_copy(half, other, place):
        return pltpu.make_async_remote_copy(
            src_ref=done.at[half, place],
            dst_ref=done.at[half, place],
            send_sem=done_sent.at[half, other],
            recv_sem=done_arrived.at[half, place],
            device_id=(other, shard),
            device_id_type=MESH,
        )

    def head_term(origin, values):
        lead = values[:FOLDED]
        return product(turned[origin], jnp.concatenate([lead, lead, values[FOLDED:]], axis=0))

    def gather_half(half):
        head_sum = [head_term(shard, d_field[half])]

        def add_head(origin):
            head_sum[0] = head_sum[0] + head_term(origin, fields[half, origin])

        gathers[half][1](add_head)
        if half == 0:
            receive_hot(lambda origin: None)
        per_half = shards // HALVES
        hot_values = jnp.concatenate(
            [hot_all[p] for p in range(half * per_half, (half + 1) * per_half)], axis=1
        )
        hot_top = hot_values[:FOLDED]
        head_sum[0] = head_sum[0] + product(
            lead_own[...], jnp.concatenate([hot_top, hot_top, hot_values[FOLDED:]], axis=0)
        )
        part[half] = head_sum[0].astype(bf16).reshape(part.shape[1:])
        for other in group_steps:
            part_copy(half, other, group).start()

    gain_terms = []

    def sum_half(half):
        slice_sum = part[half, group].astype(f32)
        for other in group_steps:
            part_copy(half, other, other).wait_recv()
            slice_sum = slice_sum + parts[half, other].astype(f32)
        done[half, group] = slice_sum.astype(bf16)
        for other in group_steps:
            done_copy(half, other, group).start()
        weight = weight_part_ref[group][:, half * columns : (half + 1) * columns].astype(f32)
        gain_terms.append(exact(jnp.ones((8, columns), f32), slice_sum * weight, (1, 1)))

    gather_half(0)
    gather_half(1)
    sum_half(0)
    sum_half(1)
    slice_rows = rows // groups
    gain_row[0:1, :slice_rows] = (gain_terms[0] + gain_terms[1])[0:1]
    start_gain, receive_gain, finish_gain = messages(
        groups, shards, lambda other: gain_row, landed_gain, gain_sent, gain_arrived
    )
    start_gain()
    landed_gain[me] = gain_row[...]

    token = iota((tokens, sent_rows), 0)
    source = jnp.where(token < per_layer, token % period, token - per_layer + FOLDED)
    copies = jnp.where(source == iota((tokens, sent_rows), 1), 1.0, 0.0).astype(bf16)
    own_field = jnp.concatenate([d_field[half] for half in range(HALVES)], axis=1)
    hot_field = jnp.concatenate([hot_all[p] for p in range(shards)], axis=1)
    own_field = jnp.where(hot == me, hot_field.astype(f32), own_field.astype(f32)).astype(bf16)
    d_norm = over_last(product(copies, own_field).astype(bf16), weights[...])
    latent = latent_ref[...].astype(f32)
    inv_rms = lax.rsqrt(jnp.mean(latent * latent, axis=1, keepdims=True) + norm_eps)
    x_hat = latent * inv_rms
    d_scaled = d_norm * gain_ref[...]
    latent_grad_ref[...] = (
        inv_rms * (d_scaled - x_hat * jnp.mean(d_scaled * x_hat, axis=1, keepdims=True))
    ).astype(bf16)

    receive_shades()
    returned = landed_shades[:, 0, :]
    loss_ref[...] = jnp.sum(
        jnp.where(lane == 4 * slots + 4, returned, 0.0), axis=(0, 1), keepdims=True
    )
    picked = exact(
        returned, jnp.where(mine, 1.0, 0.0) + jnp.where(led, 1.0, 0.0), (0, 0)
    )
    first_place = jnp.where(hot_ray, 4 * slots, 4 * rank_wide)
    place = iota((LANES, ray_count), 0)
    for c in range(3):
        color_ref[c : c + 1, :] = jnp.sum(
            jnp.where(place == first_place + c, picked, 0.0), axis=0, keepdims=True
        )

    for half in range(HALVES):
        grad_ref[group, :, half * columns : (half + 1) * columns] = done[half, group]
        for other in group_steps:
            done_copy(half, other, other).wait_recv()
            grad_ref[other, :, half * columns : (half + 1) * columns] = done[half, other]
    receive_gain()
    gains = landed_gain[:, 0, :slice_rows]
    gains = jnp.concatenate([gains[g * shards : (g + 1) * shards] for g in range(groups)], axis=1)
    gain_grad_ref[...] = gains / gain_rows_ref[...]

    finish_counts()
    finish_weights()
    finish_messages()
    finish_lead()
    finish_hot()
    for other in others:
        hot_copy(other, shard).wait_send()
    finish_shades()
    finish_gain()
    for other in others:
        turned_copy(other, shard).wait_send()
    for half in range(HALVES):
        gathers[half][2]()
        for other in group_steps:
            part_copy(half, other, group).wait_send()
            done_copy(half, other, group).wait_send()


def body(
    latents,
    head_weight,
    norm_gain,
    color_head,
    sample_points,
    sample_spacing,
    ray_targets,
    ray_scene,
):
    groups, shards = lax.axis_size("grp"), lax.axis_size("shard")
    devices = groups * shards
    ray_count, ray_depth = sample_spacing.shape
    tokens, model = latents.shape
    width = color_head.shape[1]
    rows = model // shards
    slots = 4 * ray_count // devices
    per_layer = width * width // model
    fold_rows = 2 * FOLDED + per_layer
    sent_rows = FOLDED + per_layer
    samples = sum(ray_room(devices, shards, ray_count)) * ray_depth
    columns = model // HALVES
    slice_rows = rows // groups
    in_vmem = pl.BlockSpec(memory_space=pltpu.VMEM)
    dma = pltpu.SemaphoreType.DMA
    f32, bf16 = jnp.float32, jnp.bfloat16
    vmem = pltpu.VMEM
    colors, loss, head, gain, latent_grad = pl.pallas_call(
        functools.partial(whole_kernel, groups, shards),
        in_specs=[in_vmem] * 10,
        out_specs=[in_vmem] * 5,
        out_shape=[
            jax.ShapeDtypeStruct((3, ray_count), f32),
            jax.ShapeDtypeStruct((1, 1), f32),
            jax.ShapeDtypeStruct((groups, slice_rows, model), bf16),
            jax.ShapeDtypeStruct((shards, rows), f32),
            jax.ShapeDtypeStruct((tokens, model), bf16),
        ],
        scratch_shapes=[
            vmem((1, LANES), f32),
            vmem((devices, 1, LANES), f32),
            vmem((rows, fold_rows), bf16),
            vmem((shards, rows, fold_rows), bf16),
            vmem((shards, sent_rows, rows), bf16),
            vmem((shards, sent_rows, rows), bf16),
            vmem((sent_rows, rows), bf16),
            vmem((shards, sent_rows, rows), bf16),
            vmem((devices, 2 * slots + 3, LANES), f32),
            vmem((devices, 2 * slots + 3, LANES), f32),
            vmem((shards, rows, fold_rows), bf16),
            vmem((shards, rows, fold_rows), bf16),
            vmem((model, model), bf16),
            vmem((width // LANES, FOLDED * model // width, LANES), f32),
            vmem((width // LANES, width, LANES), f32),
            vmem((2, width, 2 * FEATURES), bf16),
            vmem((2, width, width), bf16),
            vmem((2, width, width), bf16),
            vmem((width, 4), bf16),
            vmem((8 * FEATURES, LANES), f32),
            vmem((3, samples // LANES, LANES), f32),
            vmem((FEATURES, samples), bf16),
            vmem((width, samples), bf16),
            vmem((width, samples), bf16),
            vmem((4, samples // LANES, LANES), f32),
            vmem((4, samples), f32),
            vmem((FEATURES, width), f32),
            vmem((width, width), f32),
            vmem((devices, 1, LANES), f32),
            vmem((devices, 1, LANES), f32),
            vmem((HALVES, sent_rows, columns), bf16),
            vmem((HALVES, shards, sent_rows, columns), bf16),
            vmem((HALVES, groups, slice_rows, columns), bf16),
            vmem((HALVES, groups, slice_rows, columns), bf16),
            vmem((HALVES, groups, slice_rows, columns), bf16),
            vmem((1, LANES), f32),
            vmem((devices, 1, LANES), f32),
            dma((devices,)),
            dma((devices,)),
            dma((shards,)),
            dma((shards,)),
            dma((shards,)),
            dma((shards,)),
            dma((shards,)),
            dma((shards,)),
            dma((shards,)),
            dma((shards,)),
            dma((devices,)),
            dma((devices,)),
            dma((devices,)),
            dma((devices,)),
            dma((devices,)),
            dma((devices,)),
            dma((shards,)),
            dma((shards,)),
            dma((shards,)),
            dma((shards,)),
            dma((shards,)),
            dma((HALVES, shards)),
            dma((HALVES, shards)),
            dma((HALVES, shards)),
            dma((HALVES, groups)),
            dma((HALVES, groups)),
            dma((HALVES, groups)),
            dma((HALVES, groups)),
        ],
        compiler_params=pltpu.CompilerParams(collective_id=1, has_side_effects=True),
    )(
        latents,
        head_weight,
        head_weight.reshape(groups, slice_rows, model),
        norm_gain.reshape(1, model),
        norm_gain.reshape(shards, rows),
        color_head,
        sample_points,
        sample_spacing,
        ray_targets,
        ray_scene.reshape(1, ray_count),
    )
    head_grad = head.astype(f32).reshape(rows, model)
    return (colors, loss[0, 0], head_grad, gain.reshape(model), latent_grad)


def solution(mesh):
    placed = (
        P(("grp", "shard"), None),
        P("shard", None),
        P(),
        P(),
        P(("grp", "shard"), None),
        P(("grp", "shard"), None),
        P(None, ("grp", "shard")),
        P(("grp", "shard")),
    )
    return jax.shard_map(
        body,
        mesh=mesh,
        in_specs=placed,
        out_specs=(
            P(None, ("grp", "shard")),
            P(),
            P("shard", None),
            P(),
            P(("grp", "shard"), None),
        ),
        check_vma=False,
    )
```

```python
import functools

import jax
import jax.numpy as jnp
from jax import lax
from jax.experimental import pallas as pl
from jax.experimental.pallas import tpu as pltpu
from jax.sharding import PartitionSpec as P

norm_eps = 1e-06

LANES = 128
HALVES = 2
FEATURES = 48
FOLDED = 16
BLOCK = 1024
SINE = (3.14159265358979, -5.16771278004997, 2.55016403987735, -0.599264529320792, 0.0821458866111282, -0.00737043094571435, 0.000466302805767613, -0.0000219153534478303)
MESH = pl.DeviceIdType.MESH


def sine_of_pi(turns):
    whole = jnp.floor(turns + 0.5)
    rest = turns - whole
    odd = whole - 2.0 * jnp.floor(whole * 0.5)
    square = rest * rest
    value = jnp.full_like(square, SINE[-1])
    for coefficient in SINE[-2::-1]:
        value = value * square + coefficient
    return value * (rest * (1.0 - 2.0 * odd))


def product(a, b):
    return jnp.dot(a, b, preferred_element_type=jnp.float32)


def exact(a, b, contract=(1, 0)):
    return lax.dot_general(
        a,
        b,
        (((contract[0],), (contract[1],)), ((), ())),
        preferred_element_type=jnp.float32,
        precision=lax.Precision.HIGHEST,
    )


def select(onehot, values, contract=(1, 0)):
    total = 0.0
    for _ in range(3):
        term = values.astype(jnp.bfloat16)
        values = values - term.astype(jnp.float32)
        total = total + lax.dot_general(
            onehot,
            term,
            (((contract[0],), (contract[1],)), ((), ())),
            preferred_element_type=jnp.float32,
        )
    return total


def over_first_select(values, onehot):
    total = 0.0
    for _ in range(3):
        term = values.astype(jnp.bfloat16)
        values = values - term.astype(jnp.float32)
        total = total + over_first(term, onehot)
    return total


def chosen_as(mask):
    return jnp.where(mask, 1.0, 0.0).astype(jnp.bfloat16)


def over_first(a, b):
    return lax.dot_general(a, b, (((0,), (0,)), ((), ())), preferred_element_type=jnp.float32)


def over_last(a, b):
    return lax.dot_general(a, b, (((1,), (1,)), ((), ())), preferred_element_type=jnp.float32)


def iota(shape, axis):
    return lax.broadcasted_iota(jnp.int32, shape, axis)


def store_rows(ref, start, count, stride, values):
    for lanes in range(ref.shape[0]):
        ref[lanes, pl.ds(start, count, stride=stride), :] = values[:, lanes * LANES : (lanes + 1) * LANES]


def load_rows(ref, start, count, stride):
    return jnp.concatenate(
        [ref[lanes, pl.ds(start, count, stride=stride), :] for lanes in range(ref.shape[0])], axis=1
    )


def joined(ref):
    return jnp.concatenate([ref[lanes] for lanes in range(ref.shape[0])], axis=1)


def encode_rows(axes, encoded):
    sines = [sine_of_pi(a) for a in axes]
    cosines = [sine_of_pi(a + 0.5) for a in axes]
    octaves = FEATURES // 6
    for octave in range(octaves):
        for c in range(3):
            encoded[pl.ds(octave * 6 + c, 8, stride=FEATURES), :] = sines[c]
            encoded[pl.ds(octave * 6 + 3 + c, 8, stride=FEATURES), :] = cosines[c]
        if octave < octaves - 1:
            for c in range(3):
                twice = sines[c] + sines[c]
                sines[c], cosines[c] = twice * cosines[c], 1.0 - twice * sines[c]


def forward_block(i, coords, first, second_t, head, encoded, zeros_all, ones_all, twos_all, raw):
    row = pl.multiple_of(i * 8, 8)
    encode_rows([coords[c, pl.ds(row, 8), :] for c in range(3)], encoded)
    h_zero = jnp.concatenate(
        [encoded[FEATURES * r : FEATURES * (r + 1), :].astype(jnp.bfloat16) for r in range(8)], axis=1
    )
    at = pl.multiple_of(i * BLOCK, BLOCK)
    zeros_all[:, pl.ds(at, BLOCK)] = h_zero
    twice = jnp.concatenate([h_zero, h_zero], axis=0)
    h_one = jnp.maximum(product(first[...], twice).astype(jnp.bfloat16), 0)
    ones_all[:, pl.ds(at, BLOCK)] = h_one
    h_two = jnp.maximum(product(second_t[...], h_one).astype(jnp.bfloat16), 0)
    twos_all[:, pl.ds(at, BLOCK)] = h_two
    values = product(head[...], h_two)
    for r in range(8):
        for c in range(4):
            raw[c, pl.ds(row + r, 1), :] = values[c : c + 1, r * LANES : (r + 1) * LANES]


def backward_block(i, draw, second, head_t, zeros_all, ones_all, twos_all, grad_first, grad_second):
    at = pl.multiple_of(i * BLOCK, BLOCK)
    d_raw = draw[:, pl.ds(at, BLOCK)].astype(jnp.bfloat16)
    zero = jnp.zeros((), jnp.bfloat16)
    d_two = product(head_t[...], d_raw).astype(jnp.bfloat16)
    d_atwo = jnp.where(twos_all[:, pl.ds(at, BLOCK)] > 0, d_two, zero)
    h_one = ones_all[:, pl.ds(at, BLOCK)]
    grad_second[...] += over_last(h_one, d_atwo)
    d_one = product(second[...], d_atwo).astype(jnp.bfloat16)
    d_aone = jnp.where(h_one > 0, d_one, zero)
    grad_first[...] += over_last(zeros_all[:, pl.ds(at, BLOCK)], d_aone)


def render_middle(ray_depth, raw, spacing, targets, factor, draw):
    row = iota((LANES, LANES), 0)
    column = iota((LANES, LANES), 1)
    same = row // ray_depth == column // ray_depth
    before_sum = jnp.where(jnp.logical_and(same, row < column), 1.0, 0.0)
    behind_sum = jnp.where(jnp.logical_and(same, row > column), 1.0, 0.0)
    whole_sum = jnp.where(same, 1.0, 0.0)
    density_raw = raw[0]
    density = jnp.maximum(density_raw, 0.0) + jnp.log1p(jnp.exp(-jnp.abs(density_raw)))
    optical = density * spacing
    transmit = jnp.exp(-exact(optical, before_sum))
    survive = jnp.exp(-optical)
    blend = transmit * (1.0 - survive)
    d_blend = jnp.zeros_like(blend)
    loss = jnp.zeros_like(blend)
    tints = []
    colors = []
    for c in range(3):
        albedo = 1.0 / (1.0 + jnp.exp(-raw[c + 1]))
        color = exact(blend * (albedo - 1.0), whole_sum) + 1.0
        colors.append(color)
        residual = color - targets[c]
        loss = loss + residual * residual
        grad_color = 2.0 * residual * factor
        d_blend = d_blend + grad_color * (albedo - 1.0)
        tints.append(grad_color * blend * albedo * (1.0 - albedo))
    behind = exact(d_blend * blend, behind_sum)
    d_optical = d_blend * transmit * survive - behind
    d_density = d_optical * spacing * (1.0 / (1.0 + jnp.exp(-density_raw)))
    for c, value in enumerate([d_density] + tints):
        for i in range(value.shape[0]):
            draw[c : c + 1, i * LANES : (i + 1) * LANES] = value[i : i + 1, :]
    return colors, loss * factor


def ray_room(devices, shards, ray_count):
    slots = 4 * ray_count // devices
    others = pl.cdiv(devices * (ray_count - slots), devices - 1)
    return pl.cdiv(others, 16) * 16, pl.cdiv(pl.cdiv(slots * devices, shards), 16) * 16


def greet_all(groups, shards):
    me = lax.axis_index("grp") * shards + lax.axis_index("shard")
    total = groups * shards
    barrier = pltpu.get_barrier_semaphore()

    def greet(step, carry):
        other = lax.rem(me + step, total)
        pl.semaphore_signal(
            barrier, inc=1, device_id=(other // shards, lax.rem(other, shards)), device_id_type=MESH
        )
        return carry

    lax.fori_loop(1, total, greet, 0)
    return lambda: pl.semaphore_wait(barrier, total - 1)


def messages(groups, shards, source, landed, sent, arrived):
    me = lax.axis_index("grp") * shards + lax.axis_index("shard")
    total = groups * shards

    def start():
        def one(step, carry):
            other = lax.rem(me + step, total)
            pltpu.make_async_remote_copy(
                src_ref=source(other),
                dst_ref=landed.at[me],
                send_sem=sent,
                recv_sem=arrived,
                device_id=(other // shards, lax.rem(other, shards)),
                device_id_type=MESH,
            ).start()
            return carry

        lax.fori_loop(1, total, one, 0)

    everything = landed.at[pl.ds(0, total - 1)]

    def receive():
        pltpu.make_async_copy(everything, everything, arrived).wait()

    def finish():
        pltpu.make_async_copy(everything, everything, sent).wait()

    return start, receive, finish


def plane_gather(source, place, sent, passed, arrived):
    group = lax.axis_index("grp")
    shard = lax.axis_index("shard")
    shards = lax.axis_size("shard")
    chips = shards // 2
    chip = shard // 2
    core = lax.rem(shard, 2)
    partner = chip * 2 + 1 - core
    peers = [lax.rem(chip + step, chips) * 2 + core for step in range(1, chips)]
    origins = [lax.rem(chip + chips - step, chips) * 2 + core for step in range(1, chips)]

    def remote(src, dst, send_sem, recv_sem, to):
        return pltpu.make_async_remote_copy(
            src_ref=src,
            dst_ref=dst,
            send_sem=send_sem,
            recv_sem=recv_sem,
            device_id=(group, to),
            device_id_type=MESH,
        )

    def to(other):
        return remote(source, place(shard), sent.at[other], arrived.at[shard], other)

    def passing(origin):
        return remote(place(origin), place(origin), passed.at[origin], arrived.at[origin], partner)

    def start():
        for other in peers:
            to(other).start()
        to(partner).start()

    def receive(use):
        passing(partner).wait_recv()
        use(partner)
        for origin in origins:
            passing(origin).wait_recv()
            passing(origin).start()
            use(origin)
        for origin in origins:
            across = origin + 1 - 2 * core
            passing(across).wait_recv()
            use(across)

    def finish():
        for other in peers:
            to(other).wait_send()
        to(partner).wait_send()
        for origin in origins:
            passing(origin).wait_send()

    return start, receive, finish


def whole_kernel(
    groups,
    shards,
    latent_ref,
    weight_ref,
    weight_part_ref,
    gain_ref,
    gain_rows_ref,
    head_ref,
    points_ref,
    spacing_ref,
    target_ref,
    scene_ref,
    color_ref,
    loss_ref,
    grad_ref,
    gain_grad_ref,
    latent_grad_ref,
    count_row,
    landed_counts,
    lead_own,
    leads,
    hot_part,
    hot_parts,
    hot_piece,
    hot_all,
    message,
    landed,
    turned_own,
    turned,
    weights,
    wide_first,
    wide_second,
    first_t,
    second,
    second_t,
    head_t,
    encoded,
    coords,
    zeros_all,
    ones_all,
    twos_all,
    raw,
    draw,
    grad_first,
    grad_second,
    shades,
    landed_shades,
    d_field,
    fields,
    part,
    parts,
    done,
    gain_row,
    landed_gain,
    count_sent,
    count_arrived,
    lead_sent,
    lead_passed,
    lead_arrived,
    hot_sent,
    hot_arrived,
    piece_sent,
    piece_passed,
    piece_arrived,
    message_sent,
    message_arrived,
    shade_sent,
    shade_arrived,
    gain_sent,
    gain_arrived,
    turned_sent,
    turned_arrived,
    weight_sent,
    weight_passed,
    weight_arrived,
    field_sent,
    field_passed,
    field_arrived,
    part_sent,
    part_arrived,
    done_sent,
    done_arrived,
):
    group = lax.axis_index("grp")
    shard = lax.axis_index("shard")
    me = group * shards + shard
    total = groups * shards
    tokens, model = latent_ref.shape
    rows = model // shards
    width = head_ref.shape[1]
    ray_count, ray_depth = spacing_ref.shape
    slots = 4 * ray_count // total
    fan_scale = width ** (-0.5)
    per_layer = width * width // model
    strips = model // width
    period = FEATURES // strips
    fold_rows = 2 * FOLDED + per_layer
    sent_rows = FOLDED + per_layer
    own_rays, hot_rays = ray_room(total, shards, ray_count)
    f32 = jnp.float32
    bf16 = jnp.bfloat16

    wait_all = greet_all(groups, shards)

    latent = latent_ref[...].astype(f32)
    inv_rms = lax.rsqrt(jnp.mean(latent * latent, axis=1, keepdims=True) + norm_eps)
    x_norm = (latent * inv_rms * gain_ref[...]).astype(bf16)
    fold = jnp.where(
        iota((FOLDED, per_layer), 1) % period == iota((FOLDED, per_layer), 0), 1.0, 0.0
    ).astype(bf16)
    folded = product(fold, x_norm[:per_layer])
    folded_high = folded.astype(bf16).astype(f32)
    stacked = jnp.concatenate(
        [folded_high, folded - folded_high, x_norm[per_layer:].astype(f32)], axis=0
    )
    turned_own[...] = stacked.T.astype(bf16).reshape(turned_own.shape)

    scene = scene_ref[...]
    lane = iota((1, LANES), 1)
    ray_row = iota((ray_count, ray_count), 0)
    ray_column = iota((ray_count, ray_count), 1)
    scene_wide = jnp.broadcast_to(scene, (ray_count, ray_count))
    scene_tall = jnp.sum(jnp.where(ray_row == ray_column, scene_wide, 0), axis=1, keepdims=True)
    count_row[...] = jnp.sum(jnp.where(scene_tall == lane, 1.0, 0.0), axis=0, keepdims=True)
    same_scene = scene_tall == scene_wide
    rank_wide = jnp.sum(
        jnp.where(jnp.logical_and(same_scene, ray_row < ray_column), 1, 0), axis=0, keepdims=True
    )
    rank_tall = jnp.sum(
        jnp.where(jnp.logical_and(same_scene, ray_column < ray_row), 1, 0), axis=1, keepdims=True
    )
    head_t[...] = (head_ref[...].astype(f32) * fan_scale).T.astype(bf16)
    grad_first[...] = jnp.zeros_like(grad_first)
    grad_second[...] = jnp.zeros_like(grad_second)

    wait_all()

    def turned_copy(other, place):
        return pltpu.make_async_remote_copy(
            src_ref=turned_own.at[other],
            dst_ref=turned.at[place],
            send_sem=turned_sent.at[other],
            recv_sem=turned_arrived.at[place],
            device_id=(group, other),
            device_id_type=MESH,
        )

    def weight_place(origin):
        return weights.at[pl.ds(pl.multiple_of(origin * rows, rows), rows)]

    def weight_of(origin):
        return weights[pl.ds(pl.multiple_of(origin * rows, rows), rows), :]

    others = [lax.rem(shard + step, shards) for step in range(1, shards)]
    start_counts, receive_counts, finish_counts = messages(
        groups, shards, lambda other: count_row, landed_counts, count_sent, count_arrived
    )
    start_weights, receive_weights, finish_weights = plane_gather(
        weight_ref, weight_place, weight_sent, weight_passed, weight_arrived
    )
    start_messages, receive_messages, finish_messages = messages(
        groups, shards, lambda other: message.at[other], landed, message_sent, message_arrived
    )
    start_lead, receive_lead, finish_lead = plane_gather(
        lead_own, lambda origin: leads.at[origin], lead_sent, lead_passed, lead_arrived
    )
    start_counts()
    for other in others:
        turned_copy(other, shard).start()
    start_weights()
    landed_counts[me] = count_row[...]
    turned[shard] = turned_own[shard]
    weights[pl.ds(pl.multiple_of(shard * rows, rows), rows), :] = weight_ref[...]

    receive_counts()
    counts = landed_counts[:, 0, :]
    hot_lanes = jnp.min(jnp.where(counts == slots, 1, 0), axis=0, keepdims=True)
    hot = jnp.sum(jnp.where(hot_lanes > 0, lane, 0), axis=1, keepdims=True)
    hot_here = hot // shards == group
    hot_ray = scene == hot
    hot_target = (hot // shards) * shards + (me * slots + rank_wide) % shards
    owner = iota((total, ray_count), 0)
    mine = jnp.where(hot_ray, -1, scene) == owner
    led = jnp.where(hot_ray, hot_target, -1) == owner
    payload = jnp.concatenate([points_ref[...], spacing_ref[...]], axis=1)
    chosen = jnp.concatenate(
        [jnp.where(jnp.where(mine, rank_wide, -1) == j, 1.0, 0.0) for j in range(slots)]
        + [jnp.where(led, 1.0, 0.0)],
        axis=0,
    )
    filled = select(chosen.astype(bf16), payload)
    for j in range(slots + 1):
        message[:, 2 * j, :] = filled[j * total : (j + 1) * total, :LANES]
        message[:, 2 * j + 1, :] = filled[j * total : (j + 1) * total, LANES:]
    spread = jnp.where(iota((3, LANES), 1) % 4 == iota((3, LANES), 0), 1.0, 0.0)
    extra = over_first_select(target_ref[...], spread.astype(bf16)) + jnp.where(lane % 4 == 3, 1.0, 0.0)
    own_extra = jnp.where(rank_tall == lane // 4, extra, 0.0)
    hot_extra = jnp.where(lane // 4 == slots, extra, 0.0)
    message[:, 2 * slots + 2, :] = select(chosen_as(mine), own_extra) + select(
        chosen_as(led), hot_extra
    )
    start_messages()
    landed[me] = message[me]

    for other in others:
        turned_copy(other, other).wait_recv()
    hot_shard = jnp.where(hot_here, hot % shards, -1)
    lead = jnp.zeros((rows, fold_rows), f32)
    for origin in range(shards):
        lead = lead + jnp.where(hot_shard == origin, turned[origin].astype(f32), 0.0)
    lead_own[...] = lead.astype(bf16)
    start_lead()
    leads[shard] = lead_own[...]

    field_sum = [over_first(turned_own[shard], weight_ref[...])]

    def add_field(origin):
        field_sum[0] = field_sum[0] + over_first(turned_own[origin], weight_of(origin))

    receive_weights(add_field)

    def set_weights(which, field):
        first_rows = (field[:FOLDED] + field[FOLDED : 2 * FOLDED]) * fan_scale
        second_rows = field[2 * FOLDED :].astype(bf16).astype(f32) * fan_scale
        for m in range(strips):
            strip = slice(m * width, (m + 1) * width)
            store_rows(wide_first, m, FOLDED, strips, first_rows[:, strip])
            store_rows(wide_second, m, per_layer, strips, second_rows[:, strip])
        first = joined(wide_first)[:FEATURES]
        wide = joined(wide_second)
        first_high = first.astype(bf16).astype(f32)
        first_t[which] = jnp.concatenate([first_high, first - first_high], axis=0).T.astype(bf16)
        second[which] = wide.astype(bf16)
        second_t[which] = wide.T.astype(bf16)

    set_weights(0, field_sum[0])

    receive_messages()
    wanted = jnp.where(lane == me, 1.0, 0.0) * jnp.where(hot == me, 0.0, 1.0)
    many = slots * total
    tall_counts = jnp.concatenate([counts] * slots, axis=0).astype(bf16)
    wanted = jnp.broadcast_to(wanted, (8, LANES)).astype(bf16)
    wide_numbers = over_last(wanted, tall_counts)[0:1]
    earlier = chosen_as(iota((total, many), 0) < iota((total, many), 1) % total)
    offsets = product(over_last(wanted, counts.astype(bf16)).astype(bf16), earlier)[0:1]
    extras = landed[:, 2 * slots + 2, :]

    def arrived_slot(j):
        lifted = extras if j == 0 else pltpu.roll(extras, LANES - 4 * j, 1)
        return jnp.concatenate([landed[:, 2 * j, :], landed[:, 2 * j + 1, :], lifted], axis=1)

    slot_of = (iota((1, many), 1) // total).astype(f32)
    slot_at = jnp.where(wide_numbers > slot_of, offsets + slot_of, -1.0)
    keep = chosen_as(slot_at == iota((own_rays, many), 0).astype(f32))
    own_slots = select(keep, jnp.concatenate([arrived_slot(j) for j in range(slots)], axis=0))
    hot_place = (iota((hot_rays, total), 0) * shards + shard) // slots
    hot_keep = chosen_as(hot_place == iota((hot_rays, total), 1))
    hot_slots = select(hot_keep, arrived_slot(slots))
    own_pairs, hot_pairs = own_rays // 2, hot_rays // 2
    all_pairs = own_pairs + hot_pairs
    lower = jnp.concatenate([own_slots[:own_pairs], hot_slots[:hot_pairs]], axis=0)
    upper = jnp.concatenate([own_slots[own_pairs:], hot_slots[hot_pairs:]], axis=0)
    low = lane < ray_depth

    def unpack(at):
        left, right = lower[:, at : at + LANES], upper[:, at : at + LANES]
        return (
            jnp.where(low, left, pltpu.roll(right, ray_depth, 1)),
            jnp.where(low, pltpu.roll(left, ray_depth, 1), right),
        )

    coords[0], coords[1] = unpack(0)
    coords[2], spacing = unpack(LANES)

    def widen(c):
        at = 2 * LANES + c
        return jnp.where(low, lower[:, at : at + 1], upper[:, at : at + 1])

    own_count = jnp.sum(jnp.where(slot_of == 0.0, wide_numbers, 0.0), axis=1, keepdims=True)
    own_factor = 1.0 / (total * jnp.maximum(own_count, 1.0))
    hot_factor = 1.0 / (total * total * slots)
    factor = widen(3) * jnp.where(iota((all_pairs, 1), 0) < own_pairs, own_factor, hot_factor)
    targets = [widen(c) for c in range(3)]
    own_blocks = own_pairs // 8
    blocks = all_pairs // 8

    def forward(which):
        def step(i, carry):
            forward_block(
                i,
                coords,
                first_t.at[which],
                second_t.at[which],
                head_ref,
                encoded,
                zeros_all,
                ones_all,
                twos_all,
                raw,
            )
            return carry

        return step

    lax.fori_loop(0, own_blocks, forward(0), 0)
    lead_field = [over_first(lead_own[...], weight_ref[...])]

    def add_lead(origin):
        lead_field[0] = lead_field[0] + over_first(leads[origin], weight_of(origin))

    receive_lead(add_lead)
    set_weights(1, lead_field[0])
    lax.fori_loop(own_blocks, blocks, forward(1), 0)
    colors, losses = render_middle(ray_depth, raw, spacing, targets, factor, draw)
    shade = jnp.where(
        lane == 4 * slots + 4,
        jnp.sum(losses, axis=(0, 1), keepdims=True) * (1.0 / ray_depth),
        0.0,
    )

    def color_rows(start, stop):
        columns = []
        for side in (0, ray_depth):
            values = jnp.zeros((stop - start, LANES), f32)
            for c in range(3):
                values = jnp.where(lane == c, colors[c][start:stop, side : side + 1], values)
            columns.append(values)
        return jnp.concatenate(columns, axis=0)

    own_colors = color_rows(0, own_pairs)
    hot_colors = color_rows(own_pairs, all_pairs)
    back = select(keep, own_colors, (0, 0))
    for j in range(slots):
        part_back = back[j * total : (j + 1) * total]
        shade = shade + (part_back if j == 0 else pltpu.roll(part_back, 4 * j, 1))
    shade = shade + pltpu.roll(select(hot_keep, hot_colors, (0, 0)), 4 * slots, 1)
    shades[:, 0, :] = shade
    start_shades, receive_shades, finish_shades = messages(
        groups, shards, lambda other: shades.at[other], landed_shades, shade_sent, shade_arrived
    )
    start_shades()
    landed_shades[me] = shades[me]

    def backward(which):
        def step(i, carry):
            backward_block(
                i, draw, second.at[which], head_t, zeros_all, ones_all, twos_all, grad_first, grad_second
            )
            return carry

        return step

    columns = model // HALVES
    piece = model // shards

    def field_strips():
        for lanes in range(width // LANES):
            at = slice(lanes * LANES, (lanes + 1) * LANES)
            wide_first[lanes, :FEATURES, :] = grad_first[:, at]
            wide_second[lanes] = grad_second[:, at]
        strip_values = []
        for m in range(strips):
            head_rows = load_rows(wide_first, m, FOLDED, strips)
            head_rows = jnp.where(iota((FOLDED, 1), 0) < period, head_rows, 0.0)
            strip_values.append(
                jnp.concatenate([head_rows, load_rows(wide_second, m, per_layer, strips)], axis=0)
            )
        return strip_values

    def hot_copy(other, place):
        return pltpu.make_async_remote_copy(
            src_ref=hot_part.at[other],
            dst_ref=hot_parts.at[place],
            send_sem=hot_sent.at[other],
            recv_sem=hot_arrived.at[place],
            device_id=(group, other),
            device_id_type=MESH,
        )

    lax.fori_loop(own_blocks, blocks, backward(1), 0)
    hot_strips = jnp.concatenate(field_strips(), axis=1)
    for p in range(shards):
        hot_part[p] = hot_strips[:, p * piece : (p + 1) * piece].astype(bf16)
    for other in others:
        hot_copy(other, shard).start()
    grad_first[...] = jnp.zeros_like(grad_first)
    grad_second[...] = jnp.zeros_like(grad_second)
    lax.fori_loop(0, own_blocks, backward(0), 0)
    for m, values in enumerate(field_strips()):
        half, place = divmod(m * width, columns)
        d_field[half, :, place : place + width] = values.astype(bf16)

    gathers = [
        plane_gather(
            d_field.at[half],
            lambda origin, half=half: fields.at[half, origin],
            field_sent.at[half],
            field_passed.at[half],
            field_arrived.at[half],
        )
        for half in range(HALVES)
    ]
    gathers[0][0]()
    piece_sum = hot_part[shard].astype(f32)
    for other in others:
        hot_copy(other, other).wait_recv()
        piece_sum = piece_sum + hot_parts[other].astype(f32)
    hot_piece[...] = piece_sum.astype(bf16)
    start_hot, receive_hot, finish_hot = plane_gather(
        hot_piece, lambda origin: hot_all.at[origin], piece_sent, piece_passed, piece_arrived
    )
    start_hot()
    for half in range(1, HALVES):
        gathers[half][0]()
    hot_all[shard] = hot_piece[...]

    group_steps = [lax.rem(group + step, groups) for step in range(1, groups)]

    def part_copy(half, other, place):
        return pltpu.make_async_remote_copy(
            src_ref=part.at[half, other],
            dst_ref=parts.at[half, place],
            send_sem=part_sent.at[half, other],
            recv_sem=part_arrived.at[half, place],
            device_id=(other, shard),
            device_id_type=MESH,
        )

    def done_copy(half, other, place):
        return pltpu.make_async_remote_copy(
            src_ref=done.at[half, place],
            dst_ref=done.at[half, place],
            send_sem=done_sent.at[half, other],
            recv_sem=done_arrived.at[half, place],
            device_id=(other, shard),
            device_id_type=MESH,
        )

    def head_term(origin, values):
        lead = values[:FOLDED]
        return product(turned[origin], jnp.concatenate([lead, lead, values[FOLDED:]], axis=0))

    def gather_half(half):
        head_sum = [head_term(shard, d_field[half])]

        def add_head(origin):
            head_sum[0] = head_sum[0] + head_term(origin, fields[half, origin])

        gathers[half][1](add_head)
        if half == 0:
            receive_hot(lambda origin: None)
        per_half = shards // HALVES
        hot_values = jnp.concatenate(
            [hot_all[p] for p in range(half * per_half, (half + 1) * per_half)], axis=1
        )
        hot_top = hot_values[:FOLDED]
        head_sum[0] = head_sum[0] + product(
            lead_own[...], jnp.concatenate([hot_top, hot_top, hot_values[FOLDED:]], axis=0)
        )
        part[half] = head_sum[0].astype(bf16).reshape(part.shape[1:])
        for other in group_steps:
            part_copy(half, other, group).start()

    gain_terms = []

    def sum_half(half):
        slice_sum = part[half, group].astype(f32)
        for other in group_steps:
            part_copy(half, other, other).wait_recv()
            slice_sum = slice_sum + parts[half, other].astype(f32)
        weight = weight_part_ref[group][:, half * columns : (half + 1) * columns].astype(f32)
        gain_terms.append(jnp.sum(slice_sum * weight, axis=1, keepdims=True))
        if half == HALVES - 1:
            same_row = iota((slice_rows, slice_rows), 0) == iota((slice_rows, slice_rows), 1)
            gain_row[0:1, :slice_rows] = jnp.sum(
                jnp.where(same_row, sum(gain_terms), 0.0), axis=0, keepdims=True
            )
            start_gain()
        done[half, group] = slice_sum.astype(bf16)
        for other in group_steps:
            done_copy(half, other, group).start()

    slice_rows = rows // groups
    start_gain, receive_gain, finish_gain = messages(
        groups, shards, lambda other: gain_row, landed_gain, gain_sent, gain_arrived
    )
    gather_half(0)
    gather_half(1)
    sum_half(0)
    sum_half(1)
    landed_gain[me] = gain_row[...]

    token = iota((tokens, sent_rows), 0)
    source = jnp.where(token < per_layer, token % period, token - per_layer + FOLDED)
    copies = jnp.where(source == iota((tokens, sent_rows), 1), 1.0, 0.0).astype(bf16)
    own_field = jnp.concatenate([d_field[half] for half in range(HALVES)], axis=1)
    hot_field = jnp.concatenate([hot_all[p] for p in range(shards)], axis=1)
    own_field = jnp.where(hot == me, hot_field.astype(f32), own_field.astype(f32)).astype(bf16)
    d_norm = over_last(product(copies, own_field).astype(bf16), weights[...])
    latent = latent_ref[...].astype(f32)
    inv_rms = lax.rsqrt(jnp.mean(latent * latent, axis=1, keepdims=True) + norm_eps)
    x_hat = latent * inv_rms
    d_scaled = d_norm * gain_ref[...]
    latent_grad_ref[...] = (
        inv_rms * (d_scaled - x_hat * jnp.mean(d_scaled * x_hat, axis=1, keepdims=True))
    ).astype(bf16)

    receive_shades()
    returned = landed_shades[:, 0, :]
    loss_ref[...] = jnp.sum(
        jnp.where(lane == 4 * slots + 4, returned, 0.0), axis=(0, 1), keepdims=True
    )
    picked = over_first_select(returned, chosen_as(mine) + chosen_as(led))
    first_place = jnp.where(hot_ray, 4 * slots, 4 * rank_wide)
    place = iota((LANES, ray_count), 0)
    for c in range(3):
        color_ref[c : c + 1, :] = jnp.sum(
            jnp.where(place == first_place + c, picked, 0.0), axis=0, keepdims=True
        )

    for half in range(HALVES):
        grad_ref[group, :, half * columns : (half + 1) * columns] = done[half, group]
        for other in group_steps:
            done_copy(half, other, other).wait_recv()
            grad_ref[other, :, half * columns : (half + 1) * columns] = done[half, other]
    receive_gain()
    gains = landed_gain[:, 0, :slice_rows]
    gains = jnp.concatenate([gains[g * shards : (g + 1) * shards] for g in range(groups)], axis=1)
    gain_grad_ref[...] = gains / gain_rows_ref[...]

    finish_counts()
    finish_weights()
    finish_messages()
    finish_lead()
    finish_hot()
    for other in others:
        hot_copy(other, shard).wait_send()
    finish_shades()
    finish_gain()
    for other in others:
        turned_copy(other, shard).wait_send()
    for half in range(HALVES):
        gathers[half][2]()
        for other in group_steps:
            part_copy(half, other, group).wait_send()
            done_copy(half, other, group).wait_send()


def body(
    latents,
    head_weight,
    norm_gain,
    color_head,
    sample_points,
    sample_spacing,
    ray_targets,
    ray_scene,
):
    groups, shards = lax.axis_size("grp"), lax.axis_size("shard")
    devices = groups * shards
    ray_count, ray_depth = sample_spacing.shape
    tokens, model = latents.shape
    width = color_head.shape[1]
    rows = model // shards
    slots = 4 * ray_count // devices
    per_layer = width * width // model
    fold_rows = 2 * FOLDED + per_layer
    sent_rows = FOLDED + per_layer
    samples = sum(ray_room(devices, shards, ray_count)) * ray_depth
    columns = model // HALVES
    slice_rows = rows // groups
    in_vmem = pl.BlockSpec(memory_space=pltpu.VMEM)
    dma = pltpu.SemaphoreType.DMA
    f32, bf16 = jnp.float32, jnp.bfloat16
    vmem = pltpu.VMEM
    colors, loss, head, gain, latent_grad = pl.pallas_call(
        functools.partial(whole_kernel, groups, shards),
        in_specs=[in_vmem] * 10,
        out_specs=[in_vmem] * 5,
        out_shape=[
            jax.ShapeDtypeStruct((3, ray_count), f32),
            jax.ShapeDtypeStruct((1, 1), f32),
            jax.ShapeDtypeStruct((groups, slice_rows, model), bf16),
            jax.ShapeDtypeStruct((shards, rows), f32),
            jax.ShapeDtypeStruct((tokens, model), bf16),
        ],
        scratch_shapes=[
            vmem((1, LANES), f32),
            vmem((devices, 1, LANES), f32),
            vmem((rows, fold_rows), bf16),
            vmem((shards, rows, fold_rows), bf16),
            vmem((shards, sent_rows, rows), bf16),
            vmem((shards, sent_rows, rows), bf16),
            vmem((sent_rows, rows), bf16),
            vmem((shards, sent_rows, rows), bf16),
            vmem((devices, 2 * slots + 3, LANES), f32),
            vmem((devices, 2 * slots + 3, LANES), f32),
            vmem((shards, rows, fold_rows), bf16),
            vmem((shards, rows, fold_rows), bf16),
            vmem((model, model), bf16),
            vmem((width // LANES, FOLDED * model // width, LANES), f32),
            vmem((width // LANES, width, LANES), f32),
            vmem((2, width, 2 * FEATURES), bf16),
            vmem((2, width, width), bf16),
            vmem((2, width, width), bf16),
            vmem((width, 4), bf16),
            vmem((8 * FEATURES, LANES), f32),
            vmem((3, samples // LANES, LANES), f32),
            vmem((FEATURES, samples), bf16),
            vmem((width, samples), bf16),
            vmem((width, samples), bf16),
            vmem((4, samples // LANES, LANES), f32),
            vmem((4, samples), f32),
            vmem((FEATURES, width), f32),
            vmem((width, width), f32),
            vmem((devices, 1, LANES), f32),
            vmem((devices, 1, LANES), f32),
            vmem((HALVES, sent_rows, columns), bf16),
            vmem((HALVES, shards, sent_rows, columns), bf16),
            vmem((HALVES, groups, slice_rows, columns), bf16),
            vmem((HALVES, groups, slice_rows, columns), bf16),
            vmem((HALVES, groups, slice_rows, columns), bf16),
            vmem((1, LANES), f32),
            vmem((devices, 1, LANES), f32),
            dma,
            dma,
            dma((shards,)),
            dma((shards,)),
            dma((shards,)),
            dma((shards,)),
            dma((shards,)),
            dma((shards,)),
            dma((shards,)),
            dma((shards,)),
            dma,
            dma,
            dma,
            dma,
            dma,
            dma,
            dma((shards,)),
            dma((shards,)),
            dma((shards,)),
            dma((shards,)),
            dma((shards,)),
            dma((HALVES, shards)),
            dma((HALVES, shards)),
            dma((HALVES, shards)),
            dma((HALVES, groups)),
            dma((HALVES, groups)),
            dma((HALVES, groups)),
            dma((HALVES, groups)),
        ],
        compiler_params=pltpu.CompilerParams(collective_id=1, has_side_effects=True),
    )(
        latents,
        head_weight,
        head_weight.reshape(groups, slice_rows, model),
        norm_gain.reshape(1, model),
        norm_gain.reshape(shards, rows),
        color_head,
        sample_points,
        sample_spacing,
        ray_targets,
        ray_scene.reshape(1, ray_count),
    )
    colors, loss, head_grad, gain, latent_grad = hand_out(colors, loss, head, gain, latent_grad)
    return (colors, loss[0, 0], head_grad, gain.reshape(model), latent_grad)


def hand_out_kernel(color_in, loss_in, head_in, gain_in, latent_in, color, loss, head, gain, latent):
    color[...] = color_in[...]
    loss[...] = loss_in[...]
    gain[...] = gain_in[...]
    head[...] = head_in[0].astype(jnp.float32)
    latent[...] = latent_in[...]


def hand_out(colors, loss, head, gain, latent_grad):
    groups, slice_rows, model = head.shape
    tokens = latent_grad.shape[0]
    fixed = lambda i: (0, 0)
    by_row = lambda i: (i, 0)
    small = [pl.BlockSpec(colors.shape, fixed), pl.BlockSpec(loss.shape, fixed)]
    gain_spec = pl.BlockSpec(gain.shape, fixed)
    latent_spec = pl.BlockSpec((tokens // groups, model), by_row)
    return pl.pallas_call(
        hand_out_kernel,
        grid=(groups,),
        in_specs=small
        + [pl.BlockSpec((1, slice_rows, model), lambda i: (i, 0, 0)), gain_spec, latent_spec],
        out_specs=small + [pl.BlockSpec((slice_rows, model), by_row), gain_spec, latent_spec],
        out_shape=[
            jax.ShapeDtypeStruct(colors.shape, colors.dtype),
            jax.ShapeDtypeStruct(loss.shape, loss.dtype),
            jax.ShapeDtypeStruct((groups * slice_rows, model), jnp.float32),
            jax.ShapeDtypeStruct(gain.shape, gain.dtype),
            jax.ShapeDtypeStruct(latent_grad.shape, latent_grad.dtype),
        ],
    )(colors, loss, head, gain, latent_grad)


def solution(mesh):
    placed = (
        P(("grp", "shard"), None),
        P("shard", None),
        P(),
        P(),
        P(("grp", "shard"), None),
        P(("grp", "shard"), None),
        P(None, ("grp", "shard")),
        P(("grp", "shard")),
    )
    return jax.shard_map(
        body,
        mesh=mesh,
        in_specs=placed,
        out_specs=(
            P(None, ("grp", "shard")),
            P(),
            P("shard", None),
            P(),
            P(("grp", "shard"), None),
        ),
        check_vma=False,
    )
```

```python
import functools

import jax
import jax.numpy as jnp
from jax import lax
from jax.experimental import pallas as pl
from jax.experimental.pallas import tpu as pltpu
from jax.sharding import PartitionSpec as P

norm_eps = 1e-06

LANES = 128
HALVES = 4
FEATURES = 48
FOLDED = 16
BLOCK = 1024
SINE = (3.14159265358979, -5.16771278004997, 2.55016403987735, -0.599264529320792, 0.0821458866111282, -0.00737043094571435, 0.000466302805767613, -0.0000219153534478303)
MESH = pl.DeviceIdType.MESH


def sine_of_pi(turns):
    whole = jnp.floor(turns + 0.5)
    rest = turns - whole
    odd = whole - 2.0 * jnp.floor(whole * 0.5)
    square = rest * rest
    value = jnp.full_like(square, SINE[-1])
    for coefficient in SINE[-2::-1]:
        value = value * square + coefficient
    return value * (rest * (1.0 - 2.0 * odd))


def product(a, b):
    return jnp.dot(a, b, preferred_element_type=jnp.float32)


def exact(a, b, contract=(1, 0)):
    return lax.dot_general(
        a,
        b,
        (((contract[0],), (contract[1],)), ((), ())),
        preferred_element_type=jnp.float32,
        precision=lax.Precision.HIGHEST,
    )


def select(onehot, values, contract=(1, 0)):
    total = 0.0
    for _ in range(3):
        term = values.astype(jnp.bfloat16)
        values = values - term.astype(jnp.float32)
        total = total + lax.dot_general(
            onehot,
            term,
            (((contract[0],), (contract[1],)), ((), ())),
            preferred_element_type=jnp.float32,
        )
    return total


def over_first_select(values, onehot):
    total = 0.0
    for _ in range(3):
        term = values.astype(jnp.bfloat16)
        values = values - term.astype(jnp.float32)
        total = total + over_first(term, onehot)
    return total


def chosen_as(mask):
    return jnp.where(mask, 1.0, 0.0).astype(jnp.bfloat16)


def over_first(a, b):
    return lax.dot_general(a, b, (((0,), (0,)), ((), ())), preferred_element_type=jnp.float32)


def over_last(a, b):
    return lax.dot_general(a, b, (((1,), (1,)), ((), ())), preferred_element_type=jnp.float32)


def iota(shape, axis):
    return lax.broadcasted_iota(jnp.int32, shape, axis)


def store_rows(ref, start, count, stride, values):
    for lanes in range(ref.shape[0]):
        ref[lanes, pl.ds(start, count, stride=stride), :] = values[:, lanes * LANES : (lanes + 1) * LANES]


def load_rows(ref, start, count, stride):
    return jnp.concatenate(
        [ref[lanes, pl.ds(start, count, stride=stride), :] for lanes in range(ref.shape[0])], axis=1
    )


def joined(ref):
    return jnp.concatenate([ref[lanes] for lanes in range(ref.shape[0])], axis=1)


def encode_rows(axes, encoded):
    sines = [sine_of_pi(a) for a in axes]
    cosines = [sine_of_pi(a + 0.5) for a in axes]
    octaves = FEATURES // 6
    for octave in range(octaves):
        for c in range(3):
            encoded[pl.ds(octave * 6 + c, 8, stride=FEATURES), :] = sines[c]
            encoded[pl.ds(octave * 6 + 3 + c, 8, stride=FEATURES), :] = cosines[c]
        if octave < octaves - 1:
            for c in range(3):
                twice = sines[c] + sines[c]
                sines[c], cosines[c] = twice * cosines[c], 1.0 - twice * sines[c]


def forward_block(i, coords, first, second_t, head, encoded, zeros_all, ones_all, twos_all, raw):
    row = pl.multiple_of(i * 8, 8)
    encode_rows([coords[c, pl.ds(row, 8), :] for c in range(3)], encoded)
    h_zero = jnp.concatenate(
        [encoded[FEATURES * r : FEATURES * (r + 1), :].astype(jnp.bfloat16) for r in range(8)], axis=1
    )
    at = pl.multiple_of(i * BLOCK, BLOCK)
    zeros_all[:, pl.ds(at, BLOCK)] = h_zero
    twice = jnp.concatenate([h_zero, h_zero], axis=0)
    h_one = jnp.maximum(product(first[...], twice).astype(jnp.bfloat16), 0)
    ones_all[:, pl.ds(at, BLOCK)] = h_one
    h_two = jnp.maximum(product(second_t[...], h_one).astype(jnp.bfloat16), 0)
    twos_all[:, pl.ds(at, BLOCK)] = h_two
    values = product(head[...], h_two)
    for r in range(8):
        for c in range(4):
            raw[c, pl.ds(row + r, 1), :] = values[c : c + 1, r * LANES : (r + 1) * LANES]


def backward_block(i, draw, second, head_t, zeros_all, ones_all, twos_all, grad_first, grad_second):
    at = pl.multiple_of(i * BLOCK, BLOCK)
    d_raw = draw[:, pl.ds(at, BLOCK)].astype(jnp.bfloat16)
    zero = jnp.zeros((), jnp.bfloat16)
    d_two = product(head_t[...], d_raw).astype(jnp.bfloat16)
    d_atwo = jnp.where(twos_all[:, pl.ds(at, BLOCK)] > 0, d_two, zero)
    h_one = ones_all[:, pl.ds(at, BLOCK)]
    grad_second[...] += over_last(h_one, d_atwo)
    d_one = product(second[...], d_atwo).astype(jnp.bfloat16)
    d_aone = jnp.where(h_one > 0, d_one, zero)
    grad_first[...] += over_last(zeros_all[:, pl.ds(at, BLOCK)], d_aone)


def render_middle(ray_depth, raw, spacing, targets, factor, draw):
    row = iota((LANES, LANES), 0)
    column = iota((LANES, LANES), 1)
    same = row // ray_depth == column // ray_depth
    before_sum = jnp.where(jnp.logical_and(same, row < column), 1.0, 0.0)
    behind_sum = jnp.where(jnp.logical_and(same, row > column), 1.0, 0.0)
    whole_sum = jnp.where(same, 1.0, 0.0)
    density_raw = raw[0]
    density = jnp.maximum(density_raw, 0.0) + jnp.log1p(jnp.exp(-jnp.abs(density_raw)))
    optical = density * spacing
    transmit = jnp.exp(-exact(optical, before_sum))
    survive = jnp.exp(-optical)
    blend = transmit * (1.0 - survive)
    d_blend = jnp.zeros_like(blend)
    loss = jnp.zeros_like(blend)
    tints = []
    colors = []
    for c in range(3):
        albedo = 1.0 / (1.0 + jnp.exp(-raw[c + 1]))
        color = exact(blend * (albedo - 1.0), whole_sum) + 1.0
        colors.append(color)
        residual = color - targets[c]
        loss = loss + residual * residual
        grad_color = 2.0 * residual * factor
        d_blend = d_blend + grad_color * (albedo - 1.0)
        tints.append(grad_color * blend * albedo * (1.0 - albedo))
    behind = exact(d_blend * blend, behind_sum)
    d_optical = d_blend * transmit * survive - behind
    d_density = d_optical * spacing * (1.0 / (1.0 + jnp.exp(-density_raw)))
    for c, value in enumerate([d_density] + tints):
        for i in range(value.shape[0]):
            draw[c : c + 1, i * LANES : (i + 1) * LANES] = value[i : i + 1, :]
    return colors, loss * factor


def ray_room(devices, shards, ray_count):
    slots = 4 * ray_count // devices
    others = pl.cdiv(devices * (ray_count - slots), devices - 1)
    return pl.cdiv(others, 16) * 16, pl.cdiv(pl.cdiv(slots * devices, shards), 16) * 16


def greet_all(groups, shards):
    me = lax.axis_index("grp") * shards + lax.axis_index("shard")
    total = groups * shards
    barrier = pltpu.get_barrier_semaphore()

    def greet(step, carry):
        other = lax.rem(me + step, total)
        pl.semaphore_signal(
            barrier, inc=1, device_id=(other // shards, lax.rem(other, shards)), device_id_type=MESH
        )
        return carry

    lax.fori_loop(1, total, greet, 0)
    return lambda: pl.semaphore_wait(barrier, total - 1)


def messages(groups, shards, source, landed, sent, arrived):
    me = lax.axis_index("grp") * shards + lax.axis_index("shard")
    total = groups * shards

    def start():
        def one(step, carry):
            other = lax.rem(me + step, total)
            pltpu.make_async_remote_copy(
                src_ref=source(other),
                dst_ref=landed.at[me],
                send_sem=sent,
                recv_sem=arrived,
                device_id=(other // shards, lax.rem(other, shards)),
                device_id_type=MESH,
            ).start()
            return carry

        lax.fori_loop(1, total, one, 0)

    everything = landed.at[pl.ds(0, total - 1)]

    def receive():
        pltpu.make_async_copy(everything, everything, arrived).wait()

    def finish():
        pltpu.make_async_copy(everything, everything, sent).wait()

    return start, receive, finish


def plane_gather(source, place, sent, passed, arrived):
    group = lax.axis_index("grp")
    shard = lax.axis_index("shard")
    shards = lax.axis_size("shard")
    chips = shards // 2
    chip = shard // 2
    core = lax.rem(shard, 2)
    partner = chip * 2 + 1 - core
    peers = [lax.rem(chip + step, chips) * 2 + core for step in range(1, chips)]
    origins = [lax.rem(chip + chips - step, chips) * 2 + core for step in range(1, chips)]

    def remote(src, dst, send_sem, recv_sem, to):
        return pltpu.make_async_remote_copy(
            src_ref=src,
            dst_ref=dst,
            send_sem=send_sem,
            recv_sem=recv_sem,
            device_id=(group, to),
            device_id_type=MESH,
        )

    def to(other):
        return remote(source, place(shard), sent.at[other], arrived.at[shard], other)

    def passing(origin):
        return remote(place(origin), place(origin), passed.at[origin], arrived.at[origin], partner)

    def start():
        for other in peers:
            to(other).start()
        to(partner).start()

    def receive(use):
        passing(partner).wait_recv()
        use(partner)
        for origin in origins:
            passing(origin).wait_recv()
            passing(origin).start()
            use(origin)
        for origin in origins:
            across = origin + 1 - 2 * core
            passing(across).wait_recv()
            use(across)

    def finish():
        for other in peers:
            to(other).wait_send()
        to(partner).wait_send()
        for origin in origins:
            passing(origin).wait_send()

    return start, receive, finish


def flipped(chip, step, chips):
    place, result = 1, 0
    while place < chips:
        bit = lax.rem(chip // place, 2)
        result = result + place * ((1 - bit) if step // place % 2 else bit)
        place *= 2
    return result


def weight_gather(source, weights, sent, far_sent, passed, far_passed, relayed, arrived, far_arrived):
    group = lax.axis_index("grp")
    shard = lax.axis_index("shard")
    groups = lax.axis_size("grp")
    chips = lax.axis_size("shard") // 2
    chip = shard // 2
    core = lax.rem(shard, 2)
    partner = chip * 2 + 1 - core
    rows, model = source.shape
    quarter = model // groups
    powers = [1 << b for b in range(chips.bit_length() - 1)]
    near = [flipped(chip, step, chips) * 2 + core for step in powers]
    far = [flipped(chip, s, chips) * 2 + core for s in range(1, chips) if s not in powers]
    steps = [lax.rem(group + step, groups) for step in range(1, groups)]

    def across(origin):
        return origin + 1 - 2 * core

    def whole(origin):
        return weights.at[pl.ds(pl.multiple_of(origin * rows, rows), rows)]

    def piece(origin, g):
        return weights.at[
            pl.ds(pl.multiple_of(origin * rows, rows), rows),
            pl.ds(pl.multiple_of(g * quarter, quarter), quarter),
        ]

    def remote(src, dst, send_sem, recv_sem, to_group, to):
        return pltpu.make_async_remote_copy(
            src_ref=src,
            dst_ref=dst,
            send_sem=send_sem,
            recv_sem=recv_sem,
            device_id=(to_group, to),
            device_id_type=MESH,
        )

    def near_to(other):
        return remote(source, whole(shard), sent.at[other], arrived.at[shard], group, other)

    def far_to(other):
        mine = source.at[:, pl.ds(pl.multiple_of(group * quarter, quarter), quarter)]
        return remote(
            mine, piece(shard, group), far_sent.at[other], far_arrived.at[shard, group], group, other
        )

    def near_pass(origin):
        return remote(
            whole(origin), whole(origin), passed.at[origin], arrived.at[origin], group, partner
        )

    def far_pass(origin, g):
        return remote(
            piece(origin, g),
            piece(origin, g),
            far_passed.at[origin, g],
            far_arrived.at[origin, g],
            group,
            partner,
        )

    def relay(origin, other):
        return remote(
            piece(origin, group),
            piece(origin, group),
            relayed.at[origin, other],
            far_arrived.at[origin, group],
            other,
            shard,
        )

    def start_far():
        for other in far:
            far_to(other).start()

    def start_near():
        for other in near:
            near_to(other).start()
        near_to(partner).start()

    def relay_far():
        for origin in far:
            far_pass(origin, group).wait_recv()
            for other in steps:
                relay(origin, other).start()
            far_pass(origin, group).start()

    def receive(use):
        near_pass(partner).wait_recv()
        use(partner)
        for origin in near:
            near_pass(origin).wait_recv()
            near_pass(origin).start()
            use(origin)
        for origin in far:
            for g in steps:
                far_pass(origin, g).wait_recv()
                far_pass(origin, g).start()
            use(origin)
        for origin in near:
            near_pass(across(origin)).wait_recv()
            use(across(origin))
        for origin in far:
            for g in range(groups):
                far_pass(across(origin), g).wait_recv()
            use(across(origin))

    def finish():
        for other in near:
            near_to(other).wait_send()
        near_to(partner).wait_send()
        for other in far:
            far_to(other).wait_send()
        for origin in near:
            near_pass(origin).wait_send()
        for origin in far:
            for g in range(groups):
                far_pass(origin, g).wait_send()
            for other in steps:
                relay(origin, other).wait_send()

    return start_far, start_near, relay_far, receive, finish


def whole_kernel(
    groups,
    shards,
    latent_ref,
    weight_ref,
    weight_part_ref,
    gain_ref,
    gain_rows_ref,
    head_ref,
    points_ref,
    spacing_ref,
    target_ref,
    scene_ref,
    color_ref,
    loss_ref,
    grad_ref,
    gain_grad_ref,
    latent_grad_ref,
    count_row,
    landed_counts,
    lead_own,
    leads,
    hot_part,
    hot_parts,
    hot_piece,
    hot_all,
    message,
    landed,
    turned_own,
    turned,
    weights,
    wide_first,
    wide_second,
    first_t,
    second,
    second_t,
    head_t,
    encoded,
    coords,
    zeros_all,
    ones_all,
    twos_all,
    raw,
    draw,
    grad_first,
    grad_second,
    shades,
    landed_shades,
    d_field,
    fields,
    part,
    parts,
    done,
    gain_row,
    landed_gain,
    count_sent,
    count_arrived,
    lead_sent,
    lead_passed,
    lead_arrived,
    hot_sent,
    hot_arrived,
    piece_sent,
    piece_passed,
    piece_arrived,
    message_sent,
    message_arrived,
    shade_sent,
    shade_arrived,
    gain_sent,
    gain_arrived,
    turned_sent,
    turned_arrived,
    weight_sent,
    weight_passed,
    weight_arrived,
    far_sent,
    far_passed,
    far_relayed,
    far_arrived,
    field_sent,
    field_passed,
    field_arrived,
    part_sent,
    part_arrived,
    done_sent,
    done_arrived,
):
    group = lax.axis_index("grp")
    shard = lax.axis_index("shard")
    me = group * shards + shard
    total = groups * shards
    tokens, model = latent_ref.shape
    rows = model // shards
    width = head_ref.shape[1]
    ray_count, ray_depth = spacing_ref.shape
    slots = 4 * ray_count // total
    fan_scale = width ** (-0.5)
    per_layer = width * width // model
    strips = model // width
    period = FEATURES // strips
    fold_rows = 2 * FOLDED + per_layer
    sent_rows = FOLDED + per_layer
    own_rays, hot_rays = ray_room(total, shards, ray_count)
    f32 = jnp.float32
    bf16 = jnp.bfloat16

    wait_all = greet_all(groups, shards)

    latent = latent_ref[...].astype(f32)
    inv_rms = lax.rsqrt(jnp.mean(latent * latent, axis=1, keepdims=True) + norm_eps)
    x_norm = (latent * inv_rms * gain_ref[...]).astype(bf16)
    fold = jnp.where(
        iota((FOLDED, per_layer), 1) % period == iota((FOLDED, per_layer), 0), 1.0, 0.0
    ).astype(bf16)
    folded = product(fold, x_norm[:per_layer])
    folded_high = folded.astype(bf16).astype(f32)
    stacked = jnp.concatenate(
        [folded_high, folded - folded_high, x_norm[per_layer:].astype(f32)], axis=0
    )
    turned_own[...] = stacked.T.astype(bf16).reshape(turned_own.shape)

    scene = scene_ref[...]
    lane = iota((1, LANES), 1)
    ray_row = iota((ray_count, ray_count), 0)
    ray_column = iota((ray_count, ray_count), 1)
    scene_wide = jnp.broadcast_to(scene, (ray_count, ray_count))
    scene_tall = jnp.sum(jnp.where(ray_row == ray_column, scene_wide, 0), axis=1, keepdims=True)
    count_row[...] = jnp.sum(jnp.where(scene_tall == lane, 1.0, 0.0), axis=0, keepdims=True)
    same_scene = scene_tall == scene_wide
    rank_wide = jnp.sum(
        jnp.where(jnp.logical_and(same_scene, ray_row < ray_column), 1, 0), axis=0, keepdims=True
    )
    rank_tall = jnp.sum(
        jnp.where(jnp.logical_and(same_scene, ray_column < ray_row), 1, 0), axis=1, keepdims=True
    )
    head_t[...] = (head_ref[...].astype(f32) * fan_scale).T.astype(bf16)
    grad_first[...] = jnp.zeros_like(grad_first)
    grad_second[...] = jnp.zeros_like(grad_second)

    wait_all()

    def turned_copy(other, place):
        return pltpu.make_async_remote_copy(
            src_ref=turned_own.at[other],
            dst_ref=turned.at[place],
            send_sem=turned_sent.at[other],
            recv_sem=turned_arrived.at[place],
            device_id=(group, other),
            device_id_type=MESH,
        )

    def weight_of(origin):
        return weights[pl.ds(pl.multiple_of(origin * rows, rows), rows), :]

    others = [lax.rem(shard + step, shards) for step in range(1, shards)]
    start_counts, receive_counts, finish_counts = messages(
        groups, shards, lambda other: count_row, landed_counts, count_sent, count_arrived
    )
    start_far, start_near, relay_far, receive_weights, finish_weights = weight_gather(
        weight_ref,
        weights,
        weight_sent,
        far_sent,
        weight_passed,
        far_passed,
        far_relayed,
        weight_arrived,
        far_arrived,
    )
    start_messages, receive_messages, finish_messages = messages(
        groups, shards, lambda other: message.at[other], landed, message_sent, message_arrived
    )
    start_lead, receive_lead, finish_lead = plane_gather(
        lead_own, lambda origin: leads.at[origin], lead_sent, lead_passed, lead_arrived
    )
    start_counts()
    start_far()
    for other in others:
        turned_copy(other, shard).start()
    start_near()
    landed_counts[me] = count_row[...]
    turned[shard] = turned_own[shard]
    weights[pl.ds(pl.multiple_of(shard * rows, rows), rows), :] = weight_ref[...]

    relay_far()
    receive_counts()
    counts = landed_counts[:, 0, :]
    hot_lanes = jnp.min(jnp.where(counts == slots, 1, 0), axis=0, keepdims=True)
    hot = jnp.sum(jnp.where(hot_lanes > 0, lane, 0), axis=1, keepdims=True)
    hot_here = hot // shards == group
    hot_ray = scene == hot
    hot_target = (hot // shards) * shards + (me * slots + rank_wide) % shards
    owner = iota((total, ray_count), 0)
    mine = jnp.where(hot_ray, -1, scene) == owner
    led = jnp.where(hot_ray, hot_target, -1) == owner
    payload = jnp.concatenate([points_ref[...], spacing_ref[...]], axis=1)
    chosen = jnp.concatenate(
        [jnp.where(jnp.where(mine, rank_wide, -1) == j, 1.0, 0.0) for j in range(slots)]
        + [jnp.where(led, 1.0, 0.0)],
        axis=0,
    )
    filled = select(chosen.astype(bf16), payload)
    for j in range(slots + 1):
        message[:, 2 * j, :] = filled[j * total : (j + 1) * total, :LANES]
        message[:, 2 * j + 1, :] = filled[j * total : (j + 1) * total, LANES:]
    spread = jnp.where(iota((3, LANES), 1) % 4 == iota((3, LANES), 0), 1.0, 0.0)
    extra = over_first_select(target_ref[...], spread.astype(bf16)) + jnp.where(lane % 4 == 3, 1.0, 0.0)
    own_extra = jnp.where(rank_tall == lane // 4, extra, 0.0)
    hot_extra = jnp.where(lane // 4 == slots, extra, 0.0)
    message[:, 2 * slots + 2, :] = select(chosen_as(mine), own_extra) + select(
        chosen_as(led), hot_extra
    )
    start_messages()
    landed[me] = message[me]

    for other in others:
        turned_copy(other, other).wait_recv()
    hot_shard = jnp.where(hot_here, hot % shards, -1)
    lead = jnp.zeros((rows, fold_rows), f32)
    for origin in range(shards):
        lead = lead + jnp.where(hot_shard == origin, turned[origin].astype(f32), 0.0)
    lead_own[...] = lead.astype(bf16)
    start_lead()
    leads[shard] = lead_own[...]

    field_sum = [over_first(turned_own[shard], weight_ref[...])]

    def add_field(origin):
        field_sum[0] = field_sum[0] + over_first(turned_own[origin], weight_of(origin))

    receive_weights(add_field)

    def set_weights(which, field):
        first_rows = (field[:FOLDED] + field[FOLDED : 2 * FOLDED]) * fan_scale
        second_rows = field[2 * FOLDED :].astype(bf16).astype(f32) * fan_scale
        for m in range(strips):
            strip = slice(m * width, (m + 1) * width)
            store_rows(wide_first, m, FOLDED, strips, first_rows[:, strip])
            store_rows(wide_second, m, per_layer, strips, second_rows[:, strip])
        first = joined(wide_first)[:FEATURES]
        wide = joined(wide_second)
        first_high = first.astype(bf16).astype(f32)
        first_t[which] = jnp.concatenate([first_high, first - first_high], axis=0).T.astype(bf16)
        second[which] = wide.astype(bf16)
        second_t[which] = wide.T.astype(bf16)

    set_weights(0, field_sum[0])

    receive_messages()
    wanted = jnp.where(lane == me, 1.0, 0.0) * jnp.where(hot == me, 0.0, 1.0)
    many = slots * total
    tall_counts = jnp.concatenate([counts] * slots, axis=0).astype(bf16)
    wanted = jnp.broadcast_to(wanted, (8, LANES)).astype(bf16)
    wide_numbers = over_last(wanted, tall_counts)[0:1]
    earlier = chosen_as(iota((total, many), 0) < iota((total, many), 1) % total)
    offsets = product(over_last(wanted, counts.astype(bf16)).astype(bf16), earlier)[0:1]
    extras = landed[:, 2 * slots + 2, :]

    def arrived_slot(j):
        lifted = extras if j == 0 else pltpu.roll(extras, LANES - 4 * j, 1)
        return jnp.concatenate([landed[:, 2 * j, :], landed[:, 2 * j + 1, :], lifted], axis=1)

    slot_of = (iota((1, many), 1) // total).astype(f32)
    slot_at = jnp.where(wide_numbers > slot_of, offsets + slot_of, -1.0)
    keep = chosen_as(slot_at == iota((own_rays, many), 0).astype(f32))
    own_slots = select(keep, jnp.concatenate([arrived_slot(j) for j in range(slots)], axis=0))
    hot_place = (iota((hot_rays, total), 0) * shards + shard) // slots
    hot_keep = chosen_as(hot_place == iota((hot_rays, total), 1))
    hot_slots = select(hot_keep, arrived_slot(slots))
    own_pairs, hot_pairs = own_rays // 2, hot_rays // 2
    all_pairs = own_pairs + hot_pairs
    lower = jnp.concatenate([own_slots[:own_pairs], hot_slots[:hot_pairs]], axis=0)
    upper = jnp.concatenate([own_slots[own_pairs:], hot_slots[hot_pairs:]], axis=0)
    low = lane < ray_depth

    def unpack(at):
        left, right = lower[:, at : at + LANES], upper[:, at : at + LANES]
        return (
            jnp.where(low, left, pltpu.roll(right, ray_depth, 1)),
            jnp.where(low, pltpu.roll(left, ray_depth, 1), right),
        )

    coords[0], coords[1] = unpack(0)
    coords[2], spacing = unpack(LANES)

    def widen(c):
        at = 2 * LANES + c
        return jnp.where(low, lower[:, at : at + 1], upper[:, at : at + 1])

    own_count = jnp.sum(jnp.where(slot_of == 0.0, wide_numbers, 0.0), axis=1, keepdims=True)
    own_factor = 1.0 / (total * jnp.maximum(own_count, 1.0))
    hot_factor = 1.0 / (total * total * slots)
    factor = widen(3) * jnp.where(iota((all_pairs, 1), 0) < own_pairs, own_factor, hot_factor)
    targets = [widen(c) for c in range(3)]
    own_blocks = own_pairs // 8
    blocks = all_pairs // 8

    def forward(which):
        def step(i, carry):
            forward_block(
                i,
                coords,
                first_t.at[which],
                second_t.at[which],
                head_ref,
                encoded,
                zeros_all,
                ones_all,
                twos_all,
                raw,
            )
            return carry

        return step

    lax.fori_loop(0, own_blocks, forward(0), 0)
    lead_field = [over_first(lead_own[...], weight_ref[...])]

    def add_lead(origin):
        lead_field[0] = lead_field[0] + over_first(leads[origin], weight_of(origin))

    receive_lead(add_lead)
    set_weights(1, lead_field[0])
    lax.fori_loop(own_blocks, blocks, forward(1), 0)
    colors, losses = render_middle(ray_depth, raw, spacing, targets, factor, draw)
    shade = jnp.where(
        lane == 4 * slots + 4,
        jnp.sum(losses, axis=(0, 1), keepdims=True) * (1.0 / ray_depth),
        0.0,
    )

    def color_rows(start, stop):
        columns = []
        for side in (0, ray_depth):
            values = jnp.zeros((stop - start, LANES), f32)
            for c in range(3):
                values = jnp.where(lane == c, colors[c][start:stop, side : side + 1], values)
            columns.append(values)
        return jnp.concatenate(columns, axis=0)

    own_colors = color_rows(0, own_pairs)
    hot_colors = color_rows(own_pairs, all_pairs)
    back = select(keep, own_colors, (0, 0))
    for j in range(slots):
        part_back = back[j * total : (j + 1) * total]
        shade = shade + (part_back if j == 0 else pltpu.roll(part_back, 4 * j, 1))
    shade = shade + pltpu.roll(select(hot_keep, hot_colors, (0, 0)), 4 * slots, 1)
    shades[:, 0, :] = shade
    start_shades, receive_shades, finish_shades = messages(
        groups, shards, lambda other: shades.at[other], landed_shades, shade_sent, shade_arrived
    )
    start_shades()
    landed_shades[me] = shades[me]

    def backward(which):
        def step(i, carry):
            backward_block(
                i, draw, second.at[which], head_t, zeros_all, ones_all, twos_all, grad_first, grad_second
            )
            return carry

        return step

    columns = model // HALVES
    piece = model // shards

    def field_strips():
        for lanes in range(width // LANES):
            at = slice(lanes * LANES, (lanes + 1) * LANES)
            wide_first[lanes, :FEATURES, :] = grad_first[:, at]
            wide_second[lanes] = grad_second[:, at]
        strip_values = []
        for m in range(strips):
            head_rows = load_rows(wide_first, m, FOLDED, strips)
            head_rows = jnp.where(iota((FOLDED, 1), 0) < period, head_rows, 0.0)
            strip_values.append(
                jnp.concatenate([head_rows, load_rows(wide_second, m, per_layer, strips)], axis=0)
            )
        return strip_values

    def hot_copy(other, place):
        return pltpu.make_async_remote_copy(
            src_ref=hot_part.at[other],
            dst_ref=hot_parts.at[place],
            send_sem=hot_sent.at[other],
            recv_sem=hot_arrived.at[place],
            device_id=(group, other),
            device_id_type=MESH,
        )

    lax.fori_loop(own_blocks, blocks, backward(1), 0)
    hot_strips = jnp.concatenate(field_strips(), axis=1)
    for p in range(shards):
        hot_part[p] = hot_strips[:, p * piece : (p + 1) * piece].astype(bf16)
    for other in others:
        hot_copy(other, shard).start()
    grad_first[...] = jnp.zeros_like(grad_first)
    grad_second[...] = jnp.zeros_like(grad_second)
    lax.fori_loop(0, own_blocks, backward(0), 0)
    for m, values in enumerate(field_strips()):
        half, place = divmod(m * width, columns)
        d_field[half, :, place : place + width] = values.astype(bf16)

    gathers = [
        plane_gather(
            d_field.at[half],
            lambda origin, half=half: fields.at[half, origin],
            field_sent.at[half],
            field_passed.at[half],
            field_arrived.at[half],
        )
        for half in range(HALVES)
    ]
    gathers[0][0]()
    piece_sum = hot_part[shard].astype(f32)
    for other in others:
        hot_copy(other, other).wait_recv()
        piece_sum = piece_sum + hot_parts[other].astype(f32)
    hot_piece[...] = piece_sum.astype(bf16)
    start_hot, receive_hot, finish_hot = plane_gather(
        hot_piece, lambda origin: hot_all.at[origin], piece_sent, piece_passed, piece_arrived
    )
    start_hot()
    for half in range(1, HALVES):
        gathers[half][0]()
    hot_all[shard] = hot_piece[...]

    group_steps = [lax.rem(group + step, groups) for step in range(1, groups)]

    def part_copy(half, other, place):
        return pltpu.make_async_remote_copy(
            src_ref=part.at[half, other],
            dst_ref=parts.at[half, place],
            send_sem=part_sent.at[half, other],
            recv_sem=part_arrived.at[half, place],
            device_id=(other, shard),
            device_id_type=MESH,
        )

    def done_copy(half, other, place):
        return pltpu.make_async_remote_copy(
            src_ref=done.at[half, place],
            dst_ref=done.at[half, place],
            send_sem=done_sent.at[half, other],
            recv_sem=done_arrived.at[half, place],
            device_id=(other, shard),
            device_id_type=MESH,
        )

    def head_term(origin, values):
        lead = values[:FOLDED]
        return product(turned[origin], jnp.concatenate([lead, lead, values[FOLDED:]], axis=0))

    def gather_half(half):
        head_sum = [head_term(shard, d_field[half])]

        def add_head(origin):
            head_sum[0] = head_sum[0] + head_term(origin, fields[half, origin])

        gathers[half][1](add_head)
        if half == 0:
            receive_hot(lambda origin: None)
        per_half = shards // HALVES
        hot_values = jnp.concatenate(
            [hot_all[p] for p in range(half * per_half, (half + 1) * per_half)], axis=1
        )
        hot_top = hot_values[:FOLDED]
        head_sum[0] = head_sum[0] + product(
            lead_own[...], jnp.concatenate([hot_top, hot_top, hot_values[FOLDED:]], axis=0)
        )
        part[half] = head_sum[0].astype(bf16).reshape(part.shape[1:])
        for other in group_steps:
            part_copy(half, other, group).start()

    gain_terms = []

    def sum_half(half):
        slice_sum = part[half, group].astype(f32)
        for other in group_steps:
            part_copy(half, other, other).wait_recv()
            slice_sum = slice_sum + parts[half, other].astype(f32)
        weight = weight_part_ref[group][:, half * columns : (half + 1) * columns].astype(f32)
        gain_terms.append(jnp.sum(slice_sum * weight, axis=1, keepdims=True))
        if half == HALVES - 1:
            same_row = iota((slice_rows, slice_rows), 0) == iota((slice_rows, slice_rows), 1)
            gain_row[0:1, :slice_rows] = jnp.sum(
                jnp.where(same_row, sum(gain_terms), 0.0), axis=0, keepdims=True
            )
            start_gain()
        done[half, group] = slice_sum.astype(bf16)
        for other in group_steps:
            done_copy(half, other, group).start()

    slice_rows = rows // groups
    start_gain, receive_gain, finish_gain = messages(
        groups, shards, lambda other: gain_row, landed_gain, gain_sent, gain_arrived
    )
    for half in range(HALVES):
        gather_half(half)
        if half > 0:
            sum_half(half - 1)
    sum_half(HALVES - 1)
    landed_gain[me] = gain_row[...]

    token = iota((tokens, sent_rows), 0)
    source = jnp.where(token < per_layer, token % period, token - per_layer + FOLDED)
    copies = jnp.where(source == iota((tokens, sent_rows), 1), 1.0, 0.0).astype(bf16)
    own_field = jnp.concatenate([d_field[half] for half in range(HALVES)], axis=1)
    hot_field = jnp.concatenate([hot_all[p] for p in range(shards)], axis=1)
    own_field = jnp.where(hot == me, hot_field.astype(f32), own_field.astype(f32)).astype(bf16)
    d_norm = over_last(product(copies, own_field).astype(bf16), weights[...])
    latent = latent_ref[...].astype(f32)
    inv_rms = lax.rsqrt(jnp.mean(latent * latent, axis=1, keepdims=True) + norm_eps)
    x_hat = latent * inv_rms
    d_scaled = d_norm * gain_ref[...]
    latent_grad_ref[...] = (
        inv_rms * (d_scaled - x_hat * jnp.mean(d_scaled * x_hat, axis=1, keepdims=True))
    ).astype(bf16)

    receive_shades()
    returned = landed_shades[:, 0, :]
    loss_ref[...] = jnp.sum(
        jnp.where(lane == 4 * slots + 4, returned, 0.0), axis=(0, 1), keepdims=True
    )
    picked = over_first_select(returned, chosen_as(mine) + chosen_as(led))
    first_place = jnp.where(hot_ray, 4 * slots, 4 * rank_wide)
    place = iota((LANES, ray_count), 0)
    for c in range(3):
        color_ref[c : c + 1, :] = jnp.sum(
            jnp.where(place == first_place + c, picked, 0.0), axis=0, keepdims=True
        )

    for half in range(HALVES):
        grad_ref[group, :, half * columns : (half + 1) * columns] = done[half, group]
        for other in group_steps:
            done_copy(half, other, other).wait_recv()
            grad_ref[other, :, half * columns : (half + 1) * columns] = done[half, other]
    receive_gain()
    gains = landed_gain[:, 0, :slice_rows]
    gains = jnp.concatenate([gains[g * shards : (g + 1) * shards] for g in range(groups)], axis=1)
    gain_grad_ref[...] = gains / gain_rows_ref[...]

    finish_counts()
    finish_weights()
    finish_messages()
    finish_lead()
    finish_hot()
    for other in others:
        hot_copy(other, shard).wait_send()
    finish_shades()
    finish_gain()
    for other in others:
        turned_copy(other, shard).wait_send()
    for half in range(HALVES):
        gathers[half][2]()
        for other in group_steps:
            part_copy(half, other, group).wait_send()
            done_copy(half, other, group).wait_send()


def body(
    latents,
    head_weight,
    norm_gain,
    color_head,
    sample_points,
    sample_spacing,
    ray_targets,
    ray_scene,
):
    groups, shards = lax.axis_size("grp"), lax.axis_size("shard")
    devices = groups * shards
    ray_count, ray_depth = sample_spacing.shape
    tokens, model = latents.shape
    width = color_head.shape[1]
    rows = model // shards
    slots = 4 * ray_count // devices
    per_layer = width * width // model
    fold_rows = 2 * FOLDED + per_layer
    sent_rows = FOLDED + per_layer
    samples = sum(ray_room(devices, shards, ray_count)) * ray_depth
    columns = model // HALVES
    slice_rows = rows // groups
    in_vmem = pl.BlockSpec(memory_space=pltpu.VMEM)
    dma = pltpu.SemaphoreType.DMA
    f32, bf16 = jnp.float32, jnp.bfloat16
    vmem = pltpu.VMEM
    colors, loss, head, gain, latent_grad = pl.pallas_call(
        functools.partial(whole_kernel, groups, shards),
        in_specs=[in_vmem] * 10,
        out_specs=[in_vmem] * 5,
        out_shape=[
            jax.ShapeDtypeStruct((3, ray_count), f32),
            jax.ShapeDtypeStruct((1, 1), f32),
            jax.ShapeDtypeStruct((groups, slice_rows, model), bf16),
            jax.ShapeDtypeStruct((shards, rows), f32),
            jax.ShapeDtypeStruct((tokens, model), bf16),
        ],
        scratch_shapes=[
            vmem((1, LANES), f32),
            vmem((devices, 1, LANES), f32),
            vmem((rows, fold_rows), bf16),
            vmem((shards, rows, fold_rows), bf16),
            vmem((shards, sent_rows, rows), bf16),
            vmem((shards, sent_rows, rows), bf16),
            vmem((sent_rows, rows), bf16),
            vmem((shards, sent_rows, rows), bf16),
            vmem((devices, 2 * slots + 3, LANES), f32),
            vmem((devices, 2 * slots + 3, LANES), f32),
            vmem((shards, rows, fold_rows), bf16),
            vmem((shards, rows, fold_rows), bf16),
            vmem((model, model), bf16),
            vmem((width // LANES, FOLDED * model // width, LANES), f32),
            vmem((width // LANES, width, LANES), f32),
            vmem((2, width, 2 * FEATURES), bf16),
            vmem((2, width, width), bf16),
            vmem((2, width, width), bf16),
            vmem((width, 4), bf16),
            vmem((8 * FEATURES, LANES), f32),
            vmem((3, samples // LANES, LANES), f32),
            vmem((FEATURES, samples), bf16),
            vmem((width, samples), bf16),
            vmem((width, samples), bf16),
            vmem((4, samples // LANES, LANES), f32),
            vmem((4, samples), f32),
            vmem((FEATURES, width), f32),
            vmem((width, width), f32),
            vmem((devices, 1, LANES), f32),
            vmem((devices, 1, LANES), f32),
            vmem((HALVES, sent_rows, columns), bf16),
            vmem((HALVES, shards, sent_rows, columns), bf16),
            vmem((HALVES, groups, slice_rows, columns), bf16),
            vmem((HALVES, groups, slice_rows, columns), bf16),
            vmem((HALVES, groups, slice_rows, columns), bf16),
            vmem((1, LANES), f32),
            vmem((devices, 1, LANES), f32),
            dma,
            dma,
            dma((shards,)),
            dma((shards,)),
            dma((shards,)),
            dma((shards,)),
            dma((shards,)),
            dma((shards,)),
            dma((shards,)),
            dma((shards,)),
            dma,
            dma,
            dma,
            dma,
            dma,
            dma,
            dma((shards,)),
            dma((shards,)),
            dma((shards,)),
            dma((shards,)),
            dma((shards,)),
            dma((shards,)),
            dma((shards, groups)),
            dma((shards, groups)),
            dma((shards, groups)),
            dma((HALVES, shards)),
            dma((HALVES, shards)),
            dma((HALVES, shards)),
            dma((HALVES, groups)),
            dma((HALVES, groups)),
            dma((HALVES, groups)),
            dma((HALVES, groups)),
        ],
        compiler_params=pltpu.CompilerParams(collective_id=1, has_side_effects=True),
    )(
        latents,
        head_weight,
        head_weight.reshape(groups, slice_rows, model),
        norm_gain.reshape(1, model),
        norm_gain.reshape(shards, rows),
        color_head,
        sample_points,
        sample_spacing,
        ray_targets,
        ray_scene.reshape(1, ray_count),
    )
    colors, loss, head_grad, gain, latent_grad = hand_out(colors, loss, head, gain, latent_grad)
    return (colors, loss[0, 0], head_grad, gain.reshape(model), latent_grad)


def hand_out_kernel(count, *refs):
    sources, targets = refs[:count], refs[count : 2 * count]
    buffers = refs[2 * count : 3 * count]
    wide, arrived, left = refs[3 * count :]
    inward = [
        pltpu.make_async_copy(sources[i], buffers[i], arrived.at[i]) for i in range(count)
    ]
    for copy in inward:
        copy.start()
    outward = [
        pltpu.make_async_copy(buffers[i], targets[i], left.at[i]) for i in range(1, count)
    ]
    groups, slice_rows, model = buffers[0].shape
    inward[0].wait()
    for g in range(groups):
        rows = pl.ds(g * slice_rows, slice_rows)
        wide[rows, :] = buffers[0][g].astype(jnp.float32)
        outward.append(
            pltpu.make_async_copy(wide.at[rows], targets[0].at[rows], left.at[count + g])
        )
        outward[-1].start()
    for i in range(1, count):
        inward[i].wait()
        outward[i - 1].start()
    for copy in outward:
        copy.wait()


def hand_out(colors, loss, head, gain, latent_grad):
    groups, slice_rows, model = head.shape
    values = [head, latent_grad, colors, loss, gain]
    count = len(values)
    full = jax.ShapeDtypeStruct((groups * slice_rows, model), jnp.float32)
    anywhere = pl.BlockSpec(memory_space=pl.ANY)
    head, latent_grad, colors, loss, gain = pl.pallas_call(
        functools.partial(hand_out_kernel, count),
        in_specs=[anywhere] * count,
        out_specs=[anywhere] * count,
        out_shape=[full] + [jax.ShapeDtypeStruct(v.shape, v.dtype) for v in values[1:]],
        scratch_shapes=[pltpu.VMEM(v.shape, v.dtype) for v in values]
        + [
            pltpu.VMEM(full.shape, full.dtype),
            pltpu.SemaphoreType.DMA((count,)),
            pltpu.SemaphoreType.DMA((count + groups,)),
        ],
    )(*values)
    return colors, loss, head, gain, latent_grad


def solution(mesh):
    placed = (
        P(("grp", "shard"), None),
        P("shard", None),
        P(),
        P(),
        P(("grp", "shard"), None),
        P(("grp", "shard"), None),
        P(None, ("grp", "shard")),
        P(("grp", "shard")),
    )
    return jax.shard_map(
        body,
        mesh=mesh,
        in_specs=placed,
        out_specs=(
            P(None, ("grp", "shard")),
            P(),
            P("shard", None),
            P(),
            P(("grp", "shard"), None),
        ),
        check_vma=False,
    )
```

```python
import functools

import jax
import jax.numpy as jnp
from jax import lax
from jax.experimental import pallas as pl
from jax.experimental.pallas import tpu as pltpu
from jax.sharding import PartitionSpec as P

norm_eps = 1e-06

LANES = 128
HALVES = 4
FEATURES = 48
FOLDED = 16
LAG = 3
BLOCK = 1024
SINE = (3.14159265358979, -5.16771278004997, 2.55016403987735, -0.599264529320792, 0.0821458866111282, -0.00737043094571435, 0.000466302805767613, -0.0000219153534478303)
MESH = pl.DeviceIdType.MESH


def sine_of_pi(turns):
    whole = jnp.floor(turns + 0.5)
    rest = turns - whole
    odd = whole - 2.0 * jnp.floor(whole * 0.5)
    square = rest * rest
    value = jnp.full_like(square, SINE[-1])
    for coefficient in SINE[-2::-1]:
        value = value * square + coefficient
    return value * (rest * (1.0 - 2.0 * odd))


def product(a, b):
    return jnp.dot(a, b, preferred_element_type=jnp.float32)


def exact(a, b, contract=(1, 0)):
    return lax.dot_general(
        a,
        b,
        (((contract[0],), (contract[1],)), ((), ())),
        preferred_element_type=jnp.float32,
        precision=lax.Precision.HIGHEST,
    )


def select(onehot, values, contract=(1, 0)):
    total = 0.0
    for _ in range(3):
        term = values.astype(jnp.bfloat16)
        values = values - term.astype(jnp.float32)
        total = total + lax.dot_general(
            onehot,
            term,
            (((contract[0],), (contract[1],)), ((), ())),
            preferred_element_type=jnp.float32,
        )
    return total


def over_first_select(values, onehot):
    total = 0.0
    for _ in range(3):
        term = values.astype(jnp.bfloat16)
        values = values - term.astype(jnp.float32)
        total = total + over_first(term, onehot)
    return total


def chosen_as(mask):
    return jnp.where(mask, 1.0, 0.0).astype(jnp.bfloat16)


def over_first(a, b):
    return lax.dot_general(a, b, (((0,), (0,)), ((), ())), preferred_element_type=jnp.float32)


def over_last(a, b):
    return lax.dot_general(a, b, (((1,), (1,)), ((), ())), preferred_element_type=jnp.float32)


def iota(shape, axis):
    return lax.broadcasted_iota(jnp.int32, shape, axis)


def store_rows(ref, start, count, stride, values):
    for lanes in range(ref.shape[0]):
        ref[lanes, pl.ds(start, count, stride=stride), :] = values[:, lanes * LANES : (lanes + 1) * LANES]


def load_rows(ref, start, count, stride):
    return jnp.concatenate(
        [ref[lanes, pl.ds(start, count, stride=stride), :] for lanes in range(ref.shape[0])], axis=1
    )


def joined(ref):
    return jnp.concatenate([ref[lanes] for lanes in range(ref.shape[0])], axis=1)


def encode_rows(axes, encoded):
    sines = [sine_of_pi(a) for a in axes]
    cosines = [sine_of_pi(a + 0.5) for a in axes]
    octaves = FEATURES // 6
    for octave in range(octaves):
        for c in range(3):
            encoded[pl.ds(octave * 6 + c, 8, stride=FEATURES), :] = sines[c]
            encoded[pl.ds(octave * 6 + 3 + c, 8, stride=FEATURES), :] = cosines[c]
        if octave < octaves - 1:
            for c in range(3):
                twice = sines[c] + sines[c]
                sines[c], cosines[c] = twice * cosines[c], 1.0 - twice * sines[c]


def forward_block(i, coords, first, second_t, head, encoded, zeros_all, ones_all, twos_all, raw):
    row = pl.multiple_of(i * 8, 8)
    encode_rows([coords[c, pl.ds(row, 8), :] for c in range(3)], encoded)
    h_zero = jnp.concatenate(
        [encoded[FEATURES * r : FEATURES * (r + 1), :].astype(jnp.bfloat16) for r in range(8)], axis=1
    )
    at = pl.multiple_of(i * BLOCK, BLOCK)
    zeros_all[:, pl.ds(at, BLOCK)] = h_zero
    twice = jnp.concatenate([h_zero, h_zero], axis=0)
    h_one = jnp.maximum(product(first[...], twice).astype(jnp.bfloat16), 0)
    ones_all[:, pl.ds(at, BLOCK)] = h_one
    h_two = jnp.maximum(product(second_t[...], h_one).astype(jnp.bfloat16), 0)
    twos_all[:, pl.ds(at, BLOCK)] = h_two
    values = product(head[...], h_two)
    for r in range(8):
        for c in range(4):
            raw[c, pl.ds(row + r, 1), :] = values[c : c + 1, r * LANES : (r + 1) * LANES]


def backward_block(i, draw, second, head_t, zeros_all, ones_all, twos_all, grad_first, grad_second):
    at = pl.multiple_of(i * BLOCK, BLOCK)
    d_raw = draw[:, pl.ds(at, BLOCK)].astype(jnp.bfloat16)
    zero = jnp.zeros((), jnp.bfloat16)
    d_two = product(head_t[...], d_raw).astype(jnp.bfloat16)
    d_atwo = jnp.where(twos_all[:, pl.ds(at, BLOCK)] > 0, d_two, zero)
    h_one = ones_all[:, pl.ds(at, BLOCK)]
    grad_second[...] += over_last(h_one, d_atwo)
    d_one = product(second[...], d_atwo).astype(jnp.bfloat16)
    d_aone = jnp.where(h_one > 0, d_one, zero)
    grad_first[...] += over_last(zeros_all[:, pl.ds(at, BLOCK)], d_aone)


def render_middle(ray_depth, raw, spacing, targets, factor, draw):
    row = iota((LANES, LANES), 0)
    column = iota((LANES, LANES), 1)
    same = row // ray_depth == column // ray_depth
    before_sum = jnp.where(jnp.logical_and(same, row < column), 1.0, 0.0)
    behind_sum = jnp.where(jnp.logical_and(same, row > column), 1.0, 0.0)
    whole_sum = jnp.where(same, 1.0, 0.0)
    density_raw = raw[0]
    density = jnp.maximum(density_raw, 0.0) + jnp.log1p(jnp.exp(-jnp.abs(density_raw)))
    optical = density * spacing
    transmit = jnp.exp(-exact(optical, before_sum))
    survive = jnp.exp(-optical)
    blend = transmit * (1.0 - survive)
    d_blend = jnp.zeros_like(blend)
    loss = jnp.zeros_like(blend)
    tints = []
    colors = []
    for c in range(3):
        albedo = 1.0 / (1.0 + jnp.exp(-raw[c + 1]))
        color = exact(blend * (albedo - 1.0), whole_sum) + 1.0
        colors.append(color)
        residual = color - targets[c]
        loss = loss + residual * residual
        grad_color = 2.0 * residual * factor
        d_blend = d_blend + grad_color * (albedo - 1.0)
        tints.append(grad_color * blend * albedo * (1.0 - albedo))
    behind = exact(d_blend * blend, behind_sum)
    d_optical = d_blend * transmit * survive - behind
    d_density = d_optical * spacing * (1.0 / (1.0 + jnp.exp(-density_raw)))
    for c, value in enumerate([d_density] + tints):
        for i in range(value.shape[0]):
            draw[c : c + 1, i * LANES : (i + 1) * LANES] = value[i : i + 1, :]
    return colors, loss * factor


def ray_room(devices, shards, ray_count):
    slots = 4 * ray_count // devices
    others = pl.cdiv(devices * (ray_count - slots), devices - 1)
    return pl.cdiv(others, 16) * 16, pl.cdiv(pl.cdiv(slots * devices, shards), 16) * 16


def greet_all(groups, shards):
    me = lax.axis_index("grp") * shards + lax.axis_index("shard")
    total = groups * shards
    barrier = pltpu.get_barrier_semaphore()

    def greet(step, carry):
        other = lax.rem(me + step, total)
        pl.semaphore_signal(
            barrier, inc=1, device_id=(other // shards, lax.rem(other, shards)), device_id_type=MESH
        )
        return carry

    lax.fori_loop(1, total, greet, 0)
    return lambda: pl.semaphore_wait(barrier, total - 1)


def messages(groups, shards, source, landed, sent, arrived):
    me = lax.axis_index("grp") * shards + lax.axis_index("shard")
    total = groups * shards

    def start():
        def one(step, carry):
            other = lax.rem(me + step, total)
            pltpu.make_async_remote_copy(
                src_ref=source(other),
                dst_ref=landed.at[me],
                send_sem=sent,
                recv_sem=arrived,
                device_id=(other // shards, lax.rem(other, shards)),
                device_id_type=MESH,
            ).start()
            return carry

        lax.fori_loop(1, total, one, 0)

    everything = landed.at[pl.ds(0, total - 1)]

    def receive():
        pltpu.make_async_copy(everything, everything, arrived).wait()

    def finish():
        pltpu.make_async_copy(everything, everything, sent).wait()

    return start, receive, finish


def plane_gather(source, place, sent, passed, arrived):
    group = lax.axis_index("grp")
    shard = lax.axis_index("shard")
    shards = lax.axis_size("shard")
    chips = shards // 2
    chip = shard // 2
    core = lax.rem(shard, 2)
    partner = chip * 2 + 1 - core
    peers = [lax.rem(chip + step, chips) * 2 + core for step in range(1, chips)]
    origins = [lax.rem(chip + chips - step, chips) * 2 + core for step in range(1, chips)]

    def remote(src, dst, send_sem, recv_sem, to):
        return pltpu.make_async_remote_copy(
            src_ref=src,
            dst_ref=dst,
            send_sem=send_sem,
            recv_sem=recv_sem,
            device_id=(group, to),
            device_id_type=MESH,
        )

    def to(other):
        return remote(source, place(shard), sent.at[other], arrived.at[shard], other)

    def passing(origin):
        return remote(place(origin), place(origin), passed.at[origin], arrived.at[origin], partner)

    def start():
        for other in peers:
            to(other).start()
        to(partner).start()

    def receive(use):
        passing(partner).wait_recv()
        use(partner)
        for origin in origins:
            passing(origin).wait_recv()
            passing(origin).start()
            use(origin)
        for origin in origins:
            across = origin + 1 - 2 * core
            passing(across).wait_recv()
            use(across)

    def finish():
        for other in peers:
            to(other).wait_send()
        to(partner).wait_send()
        for origin in origins:
            passing(origin).wait_send()

    return start, receive, finish


def flipped(chip, step, chips):
    place, result = 1, 0
    while place < chips:
        bit = lax.rem(chip // place, 2)
        result = result + place * ((1 - bit) if step // place % 2 else bit)
        place *= 2
    return result


def weight_gather(source, weights, sent, far_sent, passed, far_passed, relayed, arrived, far_arrived):
    group = lax.axis_index("grp")
    shard = lax.axis_index("shard")
    groups = lax.axis_size("grp")
    chips = lax.axis_size("shard") // 2
    chip = shard // 2
    core = lax.rem(shard, 2)
    partner = chip * 2 + 1 - core
    rows, model = source.shape
    quarter = model // groups
    powers = [1 << b for b in range(chips.bit_length() - 1)]
    near = [flipped(chip, step, chips) * 2 + core for step in powers]
    far = [flipped(chip, s, chips) * 2 + core for s in range(1, chips) if s not in powers]
    steps = [lax.rem(group + step, groups) for step in range(1, groups)]

    def across(origin):
        return origin + 1 - 2 * core

    def whole(origin):
        return weights.at[pl.ds(pl.multiple_of(origin * rows, rows), rows)]

    def piece(origin, g):
        return weights.at[
            pl.ds(pl.multiple_of(origin * rows, rows), rows),
            pl.ds(pl.multiple_of(g * quarter, quarter), quarter),
        ]

    def remote(src, dst, send_sem, recv_sem, to_group, to):
        return pltpu.make_async_remote_copy(
            src_ref=src,
            dst_ref=dst,
            send_sem=send_sem,
            recv_sem=recv_sem,
            device_id=(to_group, to),
            device_id_type=MESH,
        )

    def near_to(other):
        return remote(source, whole(shard), sent.at[other], arrived.at[shard], group, other)

    def far_to(other):
        mine = source.at[:, pl.ds(pl.multiple_of(group * quarter, quarter), quarter)]
        return remote(
            mine, piece(shard, group), far_sent.at[other], far_arrived.at[shard, group], group, other
        )

    def near_pass(origin):
        return remote(
            whole(origin), whole(origin), passed.at[origin], arrived.at[origin], group, partner
        )

    def far_pass(origin, g):
        return remote(
            piece(origin, g),
            piece(origin, g),
            far_passed.at[origin, g],
            far_arrived.at[origin, g],
            group,
            partner,
        )

    def relay(origin, other):
        return remote(
            piece(origin, group),
            piece(origin, group),
            relayed.at[origin, other],
            far_arrived.at[origin, group],
            other,
            shard,
        )

    def start_far():
        for other in far:
            far_to(other).start()

    def start_near():
        for other in near:
            near_to(other).start()
        near_to(partner).start()

    def relay_far():
        for origin in far:
            far_pass(origin, group).wait_recv()
            for other in steps:
                relay(origin, other).start()
            far_pass(origin, group).start()

    def receive(use):
        near_pass(partner).wait_recv()
        use(partner)
        for origin in near:
            near_pass(origin).wait_recv()
            near_pass(origin).start()
            use(origin)
        for origin in far:
            for g in steps:
                far_pass(origin, g).wait_recv()
                far_pass(origin, g).start()
            use(origin)
        for origin in near:
            near_pass(across(origin)).wait_recv()
            use(across(origin))
        for origin in far:
            for g in range(groups):
                far_pass(across(origin), g).wait_recv()
            use(across(origin))

    def finish():
        for other in near:
            near_to(other).wait_send()
        near_to(partner).wait_send()
        for other in far:
            far_to(other).wait_send()
        for origin in near:
            near_pass(origin).wait_send()
        for origin in far:
            for g in range(groups):
                far_pass(origin, g).wait_send()
            for other in steps:
                relay(origin, other).wait_send()

    return start_far, start_near, relay_far, receive, finish


def whole_kernel(
    groups,
    shards,
    latent_ref,
    weight_ref,
    weight_part_ref,
    gain_ref,
    gain_rows_ref,
    head_ref,
    points_ref,
    spacing_ref,
    target_ref,
    scene_ref,
    color_ref,
    loss_ref,
    grad_ref,
    gain_grad_ref,
    latent_grad_ref,
    count_row,
    landed_counts,
    lead_own,
    leads,
    hot_part,
    hot_parts,
    hot_piece,
    hot_all,
    message,
    landed,
    turned_own,
    turned,
    weights,
    wide_first,
    wide_second,
    first_t,
    second,
    second_t,
    head_t,
    encoded,
    coords,
    zeros_all,
    ones_all,
    twos_all,
    raw,
    draw,
    grad_first,
    grad_second,
    shades,
    landed_shades,
    d_field,
    fields,
    part,
    parts,
    done,
    gain_row,
    landed_gain,
    count_sent,
    count_arrived,
    lead_sent,
    lead_passed,
    lead_arrived,
    hot_sent,
    hot_arrived,
    piece_sent,
    piece_passed,
    piece_arrived,
    message_sent,
    message_arrived,
    shade_sent,
    shade_arrived,
    gain_sent,
    gain_arrived,
    turned_sent,
    turned_arrived,
    weight_sent,
    weight_passed,
    weight_arrived,
    far_sent,
    far_passed,
    far_relayed,
    far_arrived,
    field_sent,
    field_passed,
    field_arrived,
    part_sent,
    part_arrived,
    done_sent,
    done_arrived,
):
    group = lax.axis_index("grp")
    shard = lax.axis_index("shard")
    me = group * shards + shard
    total = groups * shards
    tokens, model = latent_ref.shape
    rows = model // shards
    width = head_ref.shape[1]
    ray_count, ray_depth = spacing_ref.shape
    slots = 4 * ray_count // total
    fan_scale = width ** (-0.5)
    per_layer = width * width // model
    strips = model // width
    period = FEATURES // strips
    fold_rows = 2 * FOLDED + per_layer
    sent_rows = FOLDED + per_layer
    own_rays, hot_rays = ray_room(total, shards, ray_count)
    f32 = jnp.float32
    bf16 = jnp.bfloat16

    wait_all = greet_all(groups, shards)

    latent = latent_ref[...].astype(f32)
    inv_rms = lax.rsqrt(jnp.mean(latent * latent, axis=1, keepdims=True) + norm_eps)
    x_norm = (latent * inv_rms * gain_ref[...]).astype(bf16)
    fold = jnp.where(
        iota((FOLDED, per_layer), 1) % period == iota((FOLDED, per_layer), 0), 1.0, 0.0
    ).astype(bf16)
    folded = product(fold, x_norm[:per_layer])
    folded_high = folded.astype(bf16).astype(f32)
    stacked = jnp.concatenate(
        [folded_high, folded - folded_high, x_norm[per_layer:].astype(f32)], axis=0
    )
    turned_own[...] = stacked.T.astype(bf16).reshape(turned_own.shape)

    scene = scene_ref[...]
    lane = iota((1, LANES), 1)
    ray_row = iota((ray_count, ray_count), 0)
    ray_column = iota((ray_count, ray_count), 1)
    scene_wide = jnp.broadcast_to(scene, (ray_count, ray_count))
    scene_tall = jnp.sum(jnp.where(ray_row == ray_column, scene_wide, 0), axis=1, keepdims=True)
    count_row[...] = jnp.sum(jnp.where(scene_tall == lane, 1.0, 0.0), axis=0, keepdims=True)
    same_scene = scene_tall == scene_wide
    rank_wide = jnp.sum(
        jnp.where(jnp.logical_and(same_scene, ray_row < ray_column), 1, 0), axis=0, keepdims=True
    )
    rank_tall = jnp.sum(
        jnp.where(jnp.logical_and(same_scene, ray_column < ray_row), 1, 0), axis=1, keepdims=True
    )
    head_t[...] = (head_ref[...].astype(f32) * fan_scale).T.astype(bf16)
    grad_first[...] = jnp.zeros_like(grad_first)
    grad_second[...] = jnp.zeros_like(grad_second)

    wait_all()

    def turned_copy(other, place):
        return pltpu.make_async_remote_copy(
            src_ref=turned_own.at[other],
            dst_ref=turned.at[place],
            send_sem=turned_sent.at[other],
            recv_sem=turned_arrived.at[place],
            device_id=(group, other),
            device_id_type=MESH,
        )

    def weight_of(origin):
        return weights[pl.ds(pl.multiple_of(origin * rows, rows), rows), :]

    others = [lax.rem(shard + step, shards) for step in range(1, shards)]
    start_counts, receive_counts, finish_counts = messages(
        groups, shards, lambda other: count_row, landed_counts, count_sent, count_arrived
    )
    start_far, start_near, relay_far, receive_weights, finish_weights = weight_gather(
        weight_ref,
        weights,
        weight_sent,
        far_sent,
        weight_passed,
        far_passed,
        far_relayed,
        weight_arrived,
        far_arrived,
    )
    start_messages, receive_messages, finish_messages = messages(
        groups, shards, lambda other: message.at[other], landed, message_sent, message_arrived
    )
    start_lead, receive_lead, finish_lead = plane_gather(
        lead_own, lambda origin: leads.at[origin], lead_sent, lead_passed, lead_arrived
    )
    start_counts()
    start_far()
    for other in others:
        turned_copy(other, shard).start()
    start_near()
    landed_counts[me] = count_row[...]
    turned[shard] = turned_own[shard]
    weights[pl.ds(pl.multiple_of(shard * rows, rows), rows), :] = weight_ref[...]

    relay_far()
    receive_counts()
    counts = landed_counts[:, 0, :]
    hot_lanes = jnp.min(jnp.where(counts == slots, 1, 0), axis=0, keepdims=True)
    hot = jnp.sum(jnp.where(hot_lanes > 0, lane, 0), axis=1, keepdims=True)
    hot_here = hot // shards == group
    hot_ray = scene == hot
    hot_target = (hot // shards) * shards + (me * slots + rank_wide) % shards
    owner = iota((total, ray_count), 0)
    mine = jnp.where(hot_ray, -1, scene) == owner
    led = jnp.where(hot_ray, hot_target, -1) == owner
    payload = jnp.concatenate([points_ref[...], spacing_ref[...]], axis=1)
    chosen = jnp.concatenate(
        [jnp.where(jnp.where(mine, rank_wide, -1) == j, 1.0, 0.0) for j in range(slots)]
        + [jnp.where(led, 1.0, 0.0)],
        axis=0,
    )
    filled = select(chosen.astype(bf16), payload)
    for j in range(slots + 1):
        message[:, 2 * j, :] = filled[j * total : (j + 1) * total, :LANES]
        message[:, 2 * j + 1, :] = filled[j * total : (j + 1) * total, LANES:]
    spread = jnp.where(iota((3, LANES), 1) % 4 == iota((3, LANES), 0), 1.0, 0.0)
    extra = over_first_select(target_ref[...], spread.astype(bf16)) + jnp.where(lane % 4 == 3, 1.0, 0.0)
    own_extra = jnp.where(rank_tall == lane // 4, extra, 0.0)
    hot_extra = jnp.where(lane // 4 == slots, extra, 0.0)
    message[:, 2 * slots + 2, :] = select(chosen_as(mine), own_extra) + select(
        chosen_as(led), hot_extra
    )
    start_messages()
    landed[me] = message[me]

    for other in others:
        turned_copy(other, other).wait_recv()
    hot_shard = jnp.where(hot_here, hot % shards, -1)
    lead = jnp.zeros((rows, fold_rows), f32)
    for origin in range(shards):
        lead = lead + jnp.where(hot_shard == origin, turned[origin].astype(f32), 0.0)
    lead_own[...] = lead.astype(bf16)
    start_lead()
    leads[shard] = lead_own[...]

    field_sum = [over_first(turned_own[shard], weight_ref[...])]

    def add_field(origin):
        field_sum[0] = field_sum[0] + over_first(turned_own[origin], weight_of(origin))

    receive_weights(add_field)

    def set_weights(which, field):
        first_rows = (field[:FOLDED] + field[FOLDED : 2 * FOLDED]) * fan_scale
        second_rows = field[2 * FOLDED :].astype(bf16).astype(f32) * fan_scale
        for m in range(strips):
            strip = slice(m * width, (m + 1) * width)
            store_rows(wide_first, m, FOLDED, strips, first_rows[:, strip])
            store_rows(wide_second, m, per_layer, strips, second_rows[:, strip])
        first = joined(wide_first)[:FEATURES]
        wide = joined(wide_second)
        first_high = first.astype(bf16).astype(f32)
        first_t[which] = jnp.concatenate([first_high, first - first_high], axis=0).T.astype(bf16)
        second[which] = wide.astype(bf16)
        second_t[which] = wide.T.astype(bf16)

    set_weights(0, field_sum[0])

    receive_messages()
    wanted = jnp.where(lane == me, 1.0, 0.0) * jnp.where(hot == me, 0.0, 1.0)
    many = slots * total
    tall_counts = jnp.concatenate([counts] * slots, axis=0).astype(bf16)
    wanted = jnp.broadcast_to(wanted, (8, LANES)).astype(bf16)
    wide_numbers = over_last(wanted, tall_counts)[0:1]
    earlier = chosen_as(iota((total, many), 0) < iota((total, many), 1) % total)
    offsets = product(over_last(wanted, counts.astype(bf16)).astype(bf16), earlier)[0:1]
    extras = landed[:, 2 * slots + 2, :]

    def arrived_slot(j):
        lifted = extras if j == 0 else pltpu.roll(extras, LANES - 4 * j, 1)
        return jnp.concatenate([landed[:, 2 * j, :], landed[:, 2 * j + 1, :], lifted], axis=1)

    slot_of = (iota((1, many), 1) // total).astype(f32)
    slot_at = jnp.where(wide_numbers > slot_of, offsets + slot_of, -1.0)
    keep = chosen_as(slot_at == iota((own_rays, many), 0).astype(f32))
    own_slots = select(keep, jnp.concatenate([arrived_slot(j) for j in range(slots)], axis=0))
    hot_place = (iota((hot_rays, total), 0) * shards + shard) // slots
    hot_keep = chosen_as(hot_place == iota((hot_rays, total), 1))
    hot_slots = select(hot_keep, arrived_slot(slots))
    own_pairs, hot_pairs = own_rays // 2, hot_rays // 2
    all_pairs = own_pairs + hot_pairs
    lower = jnp.concatenate([own_slots[:own_pairs], hot_slots[:hot_pairs]], axis=0)
    upper = jnp.concatenate([own_slots[own_pairs:], hot_slots[hot_pairs:]], axis=0)
    low = lane < ray_depth

    def unpack(at):
        left, right = lower[:, at : at + LANES], upper[:, at : at + LANES]
        return (
            jnp.where(low, left, pltpu.roll(right, ray_depth, 1)),
            jnp.where(low, pltpu.roll(left, ray_depth, 1), right),
        )

    coords[0], coords[1] = unpack(0)
    coords[2], spacing = unpack(LANES)

    def widen(c):
        at = 2 * LANES + c
        return jnp.where(low, lower[:, at : at + 1], upper[:, at : at + 1])

    own_count = jnp.sum(jnp.where(slot_of == 0.0, wide_numbers, 0.0), axis=1, keepdims=True)
    own_factor = 1.0 / (total * jnp.maximum(own_count, 1.0))
    hot_factor = 1.0 / (total * total * slots)
    factor = widen(3) * jnp.where(iota((all_pairs, 1), 0) < own_pairs, own_factor, hot_factor)
    targets = [widen(c) for c in range(3)]
    own_blocks = own_pairs // 8
    blocks = all_pairs // 8

    def forward(which):
        def step(i, carry):
            forward_block(
                i,
                coords,
                first_t.at[which],
                second_t.at[which],
                head_ref,
                encoded,
                zeros_all,
                ones_all,
                twos_all,
                raw,
            )
            return carry

        return step

    lax.fori_loop(0, own_blocks, forward(0), 0)
    lead_field = [over_first(lead_own[...], weight_ref[...])]

    def add_lead(origin):
        lead_field[0] = lead_field[0] + over_first(leads[origin], weight_of(origin))

    receive_lead(add_lead)
    set_weights(1, lead_field[0])
    lax.fori_loop(own_blocks, blocks, forward(1), 0)
    colors, losses = render_middle(ray_depth, raw, spacing, targets, factor, draw)
    def backward(which):
        def step(i, carry):
            backward_block(
                i, draw, second.at[which], head_t, zeros_all, ones_all, twos_all, grad_first, grad_second
            )
            return carry

        return step

    columns = model // HALVES
    piece = model // shards

    def field_strips():
        for lanes in range(width // LANES):
            at = slice(lanes * LANES, (lanes + 1) * LANES)
            wide_first[lanes, :FEATURES, :] = grad_first[:, at]
            wide_second[lanes] = grad_second[:, at]
        strip_values = []
        for m in range(strips):
            head_rows = load_rows(wide_first, m, FOLDED, strips)
            head_rows = jnp.where(iota((FOLDED, 1), 0) < period, head_rows, 0.0)
            strip_values.append(
                jnp.concatenate([head_rows, load_rows(wide_second, m, per_layer, strips)], axis=0)
            )
        return strip_values

    def hot_copy(other, place):
        return pltpu.make_async_remote_copy(
            src_ref=hot_part.at[other],
            dst_ref=hot_parts.at[place],
            send_sem=hot_sent.at[other],
            recv_sem=hot_arrived.at[place],
            device_id=(group, other),
            device_id_type=MESH,
        )

    lax.fori_loop(own_blocks, blocks, backward(1), 0)
    hot_strips = jnp.concatenate(field_strips(), axis=1)
    for p in range(shards):
        hot_part[p] = hot_strips[:, p * piece : (p + 1) * piece].astype(bf16)
    for other in others:
        hot_copy(other, shard).start()
    grad_first[...] = jnp.zeros_like(grad_first)
    grad_second[...] = jnp.zeros_like(grad_second)
    lax.fori_loop(0, own_blocks, backward(0), 0)
    for m, values in enumerate(field_strips()):
        half, place = divmod(m * width, columns)
        d_field[half, :, place : place + width] = values.astype(bf16)

    gathers = [
        plane_gather(
            d_field.at[half],
            lambda origin, half=half: fields.at[half, origin],
            field_sent.at[half],
            field_passed.at[half],
            field_arrived.at[half],
        )
        for half in range(HALVES)
    ]
    gathers[0][0]()

    shade = jnp.where(
        lane == 4 * slots + 4,
        jnp.sum(losses, axis=(0, 1), keepdims=True) * (1.0 / ray_depth),
        0.0,
    )

    def color_rows(start, stop):
        columns = []
        for side in (0, ray_depth):
            values = jnp.zeros((stop - start, LANES), f32)
            for c in range(3):
                values = jnp.where(lane == c, colors[c][start:stop, side : side + 1], values)
            columns.append(values)
        return jnp.concatenate(columns, axis=0)

    own_colors = color_rows(0, own_pairs)
    hot_colors = color_rows(own_pairs, all_pairs)
    back = select(keep, own_colors, (0, 0))
    for j in range(slots):
        part_back = back[j * total : (j + 1) * total]
        shade = shade + (part_back if j == 0 else pltpu.roll(part_back, 4 * j, 1))
    shade = shade + pltpu.roll(select(hot_keep, hot_colors, (0, 0)), 4 * slots, 1)
    shades[:, 0, :] = shade
    start_shades, receive_shades, finish_shades = messages(
        groups, shards, lambda other: shades.at[other], landed_shades, shade_sent, shade_arrived
    )
    start_shades()
    landed_shades[me] = shades[me]

    piece_sum = hot_part[shard].astype(f32)
    for other in others:
        hot_copy(other, other).wait_recv()
        piece_sum = piece_sum + hot_parts[other].astype(f32)
    hot_piece[...] = piece_sum.astype(bf16)
    start_hot, receive_hot, finish_hot = plane_gather(
        hot_piece, lambda origin: hot_all.at[origin], piece_sent, piece_passed, piece_arrived
    )
    start_hot()
    for half in range(1, HALVES):
        gathers[half][0]()
    hot_all[shard] = hot_piece[...]

    group_steps = [lax.rem(group + step, groups) for step in range(1, groups)]

    def part_copy(half, other, place):
        return pltpu.make_async_remote_copy(
            src_ref=part.at[half, other],
            dst_ref=parts.at[half, place],
            send_sem=part_sent.at[half, other],
            recv_sem=part_arrived.at[half, place],
            device_id=(other, shard),
            device_id_type=MESH,
        )

    def done_copy(half, other, place):
        return pltpu.make_async_remote_copy(
            src_ref=done.at[half, place],
            dst_ref=done.at[half, place],
            send_sem=done_sent.at[half, other],
            recv_sem=done_arrived.at[half, place],
            device_id=(other, shard),
            device_id_type=MESH,
        )

    def head_term(origin, values):
        lead = values[:FOLDED]
        return product(turned[origin], jnp.concatenate([lead, lead, values[FOLDED:]], axis=0))

    def gather_half(half):
        head_sum = [head_term(shard, d_field[half])]

        def add_head(origin):
            head_sum[0] = head_sum[0] + head_term(origin, fields[half, origin])

        gathers[half][1](add_head)
        if half == 0:
            receive_hot(lambda origin: None)
        per_half = shards // HALVES
        hot_values = jnp.concatenate(
            [hot_all[p] for p in range(half * per_half, (half + 1) * per_half)], axis=1
        )
        hot_top = hot_values[:FOLDED]
        head_sum[0] = head_sum[0] + product(
            lead_own[...], jnp.concatenate([hot_top, hot_top, hot_values[FOLDED:]], axis=0)
        )
        part[half] = head_sum[0].astype(bf16).reshape(part.shape[1:])
        for other in group_steps:
            part_copy(half, other, group).start()

    gain_terms = []

    def sum_half(half):
        slice_sum = part[half, group].astype(f32)
        for other in group_steps:
            part_copy(half, other, other).wait_recv()
            slice_sum = slice_sum + parts[half, other].astype(f32)
        weight = weight_part_ref[group][:, half * columns : (half + 1) * columns].astype(f32)
        gain_terms.append(jnp.sum(slice_sum * weight, axis=1, keepdims=True))
        if half == HALVES - 1:
            same_row = iota((slice_rows, slice_rows), 0) == iota((slice_rows, slice_rows), 1)
            gain_row[0:1, :slice_rows] = jnp.sum(
                jnp.where(same_row, sum(gain_terms), 0.0), axis=0, keepdims=True
            )
            start_gain()
        done[half, group] = slice_sum.astype(bf16)
        for other in group_steps:
            done_copy(half, other, group).start()

    slice_rows = rows // groups
    start_gain, receive_gain, finish_gain = messages(
        groups, shards, lambda other: gain_row, landed_gain, gain_sent, gain_arrived
    )
    for half in range(HALVES):
        gather_half(half)
        if half >= LAG:
            sum_half(half - LAG)
    for half in range(HALVES - LAG, HALVES):
        sum_half(half)
    landed_gain[me] = gain_row[...]

    token = iota((tokens, sent_rows), 0)
    source = jnp.where(token < per_layer, token % period, token - per_layer + FOLDED)
    copies = jnp.where(source == iota((tokens, sent_rows), 1), 1.0, 0.0).astype(bf16)
    own_field = jnp.concatenate([d_field[half] for half in range(HALVES)], axis=1)
    hot_field = jnp.concatenate([hot_all[p] for p in range(shards)], axis=1)
    own_field = jnp.where(hot == me, hot_field.astype(f32), own_field.astype(f32)).astype(bf16)
    d_norm = over_last(product(copies, own_field).astype(bf16), weights[...])
    latent = latent_ref[...].astype(f32)
    inv_rms = lax.rsqrt(jnp.mean(latent * latent, axis=1, keepdims=True) + norm_eps)
    x_hat = latent * inv_rms
    d_scaled = d_norm * gain_ref[...]
    latent_grad_ref[...] = (
        inv_rms * (d_scaled - x_hat * jnp.mean(d_scaled * x_hat, axis=1, keepdims=True))
    ).astype(bf16)

    receive_shades()
    returned = landed_shades[:, 0, :]
    loss_ref[...] = jnp.sum(
        jnp.where(lane == 4 * slots + 4, returned, 0.0), axis=(0, 1), keepdims=True
    )
    picked = over_first_select(returned, chosen_as(mine) + chosen_as(led))
    first_place = jnp.where(hot_ray, 4 * slots, 4 * rank_wide)
    place = iota((LANES, ray_count), 0)
    for c in range(3):
        color_ref[c : c + 1, :] = jnp.sum(
            jnp.where(place == first_place + c, picked, 0.0), axis=0, keepdims=True
        )

    for half in range(HALVES):
        grad_ref[group, :, half * columns : (half + 1) * columns] = done[half, group]
        for other in group_steps:
            done_copy(half, other, other).wait_recv()
            grad_ref[other, :, half * columns : (half + 1) * columns] = done[half, other]
    receive_gain()
    gains = landed_gain[:, 0, :slice_rows]
    gains = jnp.concatenate([gains[g * shards : (g + 1) * shards] for g in range(groups)], axis=1)
    gain_grad_ref[...] = gains / gain_rows_ref[...]

    finish_counts()
    finish_weights()
    finish_messages()
    finish_lead()
    finish_hot()
    for other in others:
        hot_copy(other, shard).wait_send()
    finish_shades()
    finish_gain()
    for other in others:
        turned_copy(other, shard).wait_send()
    for half in range(HALVES):
        gathers[half][2]()
        for other in group_steps:
            part_copy(half, other, group).wait_send()
            done_copy(half, other, group).wait_send()


def body(
    latents,
    head_weight,
    norm_gain,
    color_head,
    sample_points,
    sample_spacing,
    ray_targets,
    ray_scene,
):
    groups, shards = lax.axis_size("grp"), lax.axis_size("shard")
    devices = groups * shards
    ray_count, ray_depth = sample_spacing.shape
    tokens, model = latents.shape
    width = color_head.shape[1]
    rows = model // shards
    slots = 4 * ray_count // devices
    per_layer = width * width // model
    fold_rows = 2 * FOLDED + per_layer
    sent_rows = FOLDED + per_layer
    samples = sum(ray_room(devices, shards, ray_count)) * ray_depth
    columns = model // HALVES
    slice_rows = rows // groups
    in_vmem = pl.BlockSpec(memory_space=pltpu.VMEM)
    dma = pltpu.SemaphoreType.DMA
    f32, bf16 = jnp.float32, jnp.bfloat16
    vmem = pltpu.VMEM
    colors, loss, head, gain, latent_grad = pl.pallas_call(
        functools.partial(whole_kernel, groups, shards),
        in_specs=[in_vmem] * 10,
        out_specs=[in_vmem] * 5,
        out_shape=[
            jax.ShapeDtypeStruct((3, ray_count), f32),
            jax.ShapeDtypeStruct((1, 1), f32),
            jax.ShapeDtypeStruct((groups, slice_rows, model), bf16),
            jax.ShapeDtypeStruct((shards, rows), f32),
            jax.ShapeDtypeStruct((tokens, model), bf16),
        ],
        scratch_shapes=[
            vmem((1, LANES), f32),
            vmem((devices, 1, LANES), f32),
            vmem((rows, fold_rows), bf16),
            vmem((shards, rows, fold_rows), bf16),
            vmem((shards, sent_rows, rows), bf16),
            vmem((shards, sent_rows, rows), bf16),
            vmem((sent_rows, rows), bf16),
            vmem((shards, sent_rows, rows), bf16),
            vmem((devices, 2 * slots + 3, LANES), f32),
            vmem((devices, 2 * slots + 3, LANES), f32),
            vmem((shards, rows, fold_rows), bf16),
            vmem((shards, rows, fold_rows), bf16),
            vmem((model, model), bf16),
            vmem((width // LANES, FOLDED * model // width, LANES), f32),
            vmem((width // LANES, width, LANES), f32),
            vmem((2, width, 2 * FEATURES), bf16),
            vmem((2, width, width), bf16),
            vmem((2, width, width), bf16),
            vmem((width, 4), bf16),
            vmem((8 * FEATURES, LANES), f32),
            vmem((3, samples // LANES, LANES), f32),
            vmem((FEATURES, samples), bf16),
            vmem((width, samples), bf16),
            vmem((width, samples), bf16),
            vmem((4, samples // LANES, LANES), f32),
            vmem((4, samples), f32),
            vmem((FEATURES, width), f32),
            vmem((width, width), f32),
            vmem((devices, 1, LANES), f32),
            vmem((devices, 1, LANES), f32),
            vmem((HALVES, sent_rows, columns), bf16),
            vmem((HALVES, shards, sent_rows, columns), bf16),
            vmem((HALVES, groups, slice_rows, columns), bf16),
            vmem((HALVES, groups, slice_rows, columns), bf16),
            vmem((HALVES, groups, slice_rows, columns), bf16),
            vmem((1, LANES), f32),
            vmem((devices, 1, LANES), f32),
            dma,
            dma,
            dma((shards,)),
            dma((shards,)),
            dma((shards,)),
            dma((shards,)),
            dma((shards,)),
            dma((shards,)),
            dma((shards,)),
            dma((shards,)),
            dma,
            dma,
            dma,
            dma,
            dma,
            dma,
            dma((shards,)),
            dma((shards,)),
            dma((shards,)),
            dma((shards,)),
            dma((shards,)),
            dma((shards,)),
            dma((shards, groups)),
            dma((shards, groups)),
            dma((shards, groups)),
            dma((HALVES, shards)),
            dma((HALVES, shards)),
            dma((HALVES, shards)),
            dma((HALVES, groups)),
            dma((HALVES, groups)),
            dma((HALVES, groups)),
            dma((HALVES, groups)),
        ],
        compiler_params=pltpu.CompilerParams(collective_id=1, has_side_effects=True),
    )(
        latents,
        head_weight,
        head_weight.reshape(groups, slice_rows, model),
        norm_gain.reshape(1, model),
        norm_gain.reshape(shards, rows),
        color_head,
        sample_points,
        sample_spacing,
        ray_targets,
        ray_scene.reshape(1, ray_count),
    )
    colors, loss, head_grad, gain, latent_grad = hand_out(colors, loss, head, gain, latent_grad)
    return (colors, loss[0, 0], head_grad, gain.reshape(model), latent_grad)


def hand_out_kernel(count, *refs):
    sources, targets = refs[:count], refs[count : 2 * count]
    buffers = refs[2 * count : 3 * count]
    wide, arrived, left = refs[3 * count :]
    inward = [
        pltpu.make_async_copy(sources[i], buffers[i], arrived.at[i]) for i in range(count)
    ]
    for copy in inward:
        copy.start()
    outward = [
        pltpu.make_async_copy(buffers[i], targets[i], left.at[i]) for i in range(1, count)
    ]
    groups, slice_rows, model = buffers[0].shape
    inward[0].wait()
    for g in range(groups):
        rows = pl.ds(g * slice_rows, slice_rows)
        wide[rows, :] = buffers[0][g].astype(jnp.float32)
        outward.append(
            pltpu.make_async_copy(wide.at[rows], targets[0].at[rows], left.at[count + g])
        )
        outward[-1].start()
    for i in range(1, count):
        inward[i].wait()
        outward[i - 1].start()
    for copy in outward:
        copy.wait()


def hand_out(colors, loss, head, gain, latent_grad):
    groups, slice_rows, model = head.shape
    values = [head, latent_grad, colors, loss, gain]
    count = len(values)
    full = jax.ShapeDtypeStruct((groups * slice_rows, model), jnp.float32)
    anywhere = pl.BlockSpec(memory_space=pl.ANY)
    head, latent_grad, colors, loss, gain = pl.pallas_call(
        functools.partial(hand_out_kernel, count),
        in_specs=[anywhere] * count,
        out_specs=[anywhere] * count,
        out_shape=[full] + [jax.ShapeDtypeStruct(v.shape, v.dtype) for v in values[1:]],
        scratch_shapes=[pltpu.VMEM(v.shape, v.dtype) for v in values]
        + [
            pltpu.VMEM(full.shape, full.dtype),
            pltpu.SemaphoreType.DMA((count,)),
            pltpu.SemaphoreType.DMA((count + groups,)),
        ],
    )(*values)
    return colors, loss, head, gain, latent_grad


def solution(mesh):
    placed = (
        P(("grp", "shard"), None),
        P("shard", None),
        P(),
        P(),
        P(("grp", "shard"), None),
        P(("grp", "shard"), None),
        P(None, ("grp", "shard")),
        P(("grp", "shard")),
    )
    return jax.shard_map(
        body,
        mesh=mesh,
        in_specs=placed,
        out_specs=(
            P(None, ("grp", "shard")),
            P(),
            P("shard", None),
            P(),
            P(("grp", "shard"), None),
        ),
        check_vma=False,
    )
```

```python
import functools

import jax
import jax.numpy as jnp
from jax import lax
from jax.experimental import pallas as pl
from jax.experimental.pallas import tpu as pltpu
from jax.sharding import PartitionSpec as P

norm_eps = 1e-06

LANES = 128
HALVES = 4
FEATURES = 48
FOLDED = 16
LAG = 3
BLOCK = 1024
SINE = (3.14159265358979, -5.16771278004997, 2.55016403987735, -0.599264529320792, 0.0821458866111282, -0.00737043094571435, 0.000466302805767613, -0.0000219153534478303)
MESH = pl.DeviceIdType.MESH


def sine_of_pi(turns):
    whole = jnp.floor(turns + 0.5)
    rest = turns - whole
    odd = whole - 2.0 * jnp.floor(whole * 0.5)
    square = rest * rest
    value = jnp.full_like(square, SINE[-1])
    for coefficient in SINE[-2::-1]:
        value = value * square + coefficient
    return value * (rest * (1.0 - 2.0 * odd))


def product(a, b):
    return jnp.dot(a, b, preferred_element_type=jnp.float32)


def exact(a, b, contract=(1, 0)):
    return lax.dot_general(
        a,
        b,
        (((contract[0],), (contract[1],)), ((), ())),
        preferred_element_type=jnp.float32,
        precision=lax.Precision.HIGHEST,
    )


def select(onehot, values, contract=(1, 0)):
    total = 0.0
    for _ in range(3):
        term = values.astype(jnp.bfloat16)
        values = values - term.astype(jnp.float32)
        total = total + lax.dot_general(
            onehot,
            term,
            (((contract[0],), (contract[1],)), ((), ())),
            preferred_element_type=jnp.float32,
        )
    return total


def over_first_select(values, onehot):
    total = 0.0
    for _ in range(3):
        term = values.astype(jnp.bfloat16)
        values = values - term.astype(jnp.float32)
        total = total + over_first(term, onehot)
    return total


def chosen_as(mask):
    return jnp.where(mask, 1.0, 0.0).astype(jnp.bfloat16)


def over_first(a, b):
    return lax.dot_general(a, b, (((0,), (0,)), ((), ())), preferred_element_type=jnp.float32)


def over_last(a, b):
    return lax.dot_general(a, b, (((1,), (1,)), ((), ())), preferred_element_type=jnp.float32)


def iota(shape, axis):
    return lax.broadcasted_iota(jnp.int32, shape, axis)


def store_rows(ref, start, count, stride, values):
    for lanes in range(ref.shape[0]):
        ref[lanes, pl.ds(start, count, stride=stride), :] = values[:, lanes * LANES : (lanes + 1) * LANES]


def load_rows(ref, start, count, stride):
    return jnp.concatenate(
        [ref[lanes, pl.ds(start, count, stride=stride), :] for lanes in range(ref.shape[0])], axis=1
    )


def joined(ref):
    return jnp.concatenate([ref[lanes] for lanes in range(ref.shape[0])], axis=1)


def encode_rows(axes, encoded):
    sines = [sine_of_pi(a) for a in axes]
    cosines = [sine_of_pi(a + 0.5) for a in axes]
    octaves = FEATURES // 6
    for octave in range(octaves):
        for c in range(3):
            encoded[pl.ds(octave * 6 + c, 8, stride=FEATURES), :] = sines[c]
            encoded[pl.ds(octave * 6 + 3 + c, 8, stride=FEATURES), :] = cosines[c]
        if octave < octaves - 1:
            for c in range(3):
                twice = sines[c] + sines[c]
                sines[c], cosines[c] = twice * cosines[c], 1.0 - twice * sines[c]


def forward_block(i, coords, first, second_t, head, encoded, zeros_all, ones_all, twos_all, raw):
    row = pl.multiple_of(i * 8, 8)
    encode_rows([coords[c, pl.ds(row, 8), :] for c in range(3)], encoded)
    h_zero = jnp.concatenate(
        [encoded[FEATURES * r : FEATURES * (r + 1), :].astype(jnp.bfloat16) for r in range(8)], axis=1
    )
    at = pl.multiple_of(i * BLOCK, BLOCK)
    zeros_all[:, pl.ds(at, BLOCK)] = h_zero
    twice = jnp.concatenate([h_zero, h_zero], axis=0)
    h_one = jnp.maximum(product(first[...], twice).astype(jnp.bfloat16), 0)
    ones_all[:, pl.ds(at, BLOCK)] = h_one
    h_two = jnp.maximum(product(second_t[...], h_one).astype(jnp.bfloat16), 0)
    twos_all[:, pl.ds(at, BLOCK)] = h_two
    values = product(head[...], h_two)
    for r in range(8):
        for c in range(4):
            raw[c, pl.ds(row + r, 1), :] = values[c : c + 1, r * LANES : (r + 1) * LANES]


def backward_block(i, draw, second, head_t, zeros_all, ones_all, twos_all, grad_first, grad_second):
    at = pl.multiple_of(i * BLOCK, BLOCK)
    d_raw = draw[:, pl.ds(at, BLOCK)].astype(jnp.bfloat16)
    zero = jnp.zeros((), jnp.bfloat16)
    d_two = product(head_t[...], d_raw).astype(jnp.bfloat16)
    d_atwo = jnp.where(twos_all[:, pl.ds(at, BLOCK)] > 0, d_two, zero)
    h_one = ones_all[:, pl.ds(at, BLOCK)]
    grad_second[...] += over_last(h_one, d_atwo)
    d_one = product(second[...], d_atwo).astype(jnp.bfloat16)
    d_aone = jnp.where(h_one > 0, d_one, zero)
    grad_first[...] += over_last(zeros_all[:, pl.ds(at, BLOCK)], d_aone)


def render_middle(ray_depth, raw, spacing, targets, factor, draw):
    row = iota((LANES, LANES), 0)
    column = iota((LANES, LANES), 1)
    same = row // ray_depth == column // ray_depth
    before_sum = jnp.where(jnp.logical_and(same, row < column), 1.0, 0.0)
    behind_sum = jnp.where(jnp.logical_and(same, row > column), 1.0, 0.0)
    whole_sum = jnp.where(same, 1.0, 0.0)
    density_raw = raw[0]
    density = jnp.maximum(density_raw, 0.0) + jnp.log1p(jnp.exp(-jnp.abs(density_raw)))
    optical = density * spacing
    transmit = jnp.exp(-exact(optical, before_sum))
    survive = jnp.exp(-optical)
    blend = transmit * (1.0 - survive)
    d_blend = jnp.zeros_like(blend)
    loss = jnp.zeros_like(blend)
    tints = []
    colors = []
    for c in range(3):
        albedo = 1.0 / (1.0 + jnp.exp(-raw[c + 1]))
        color = exact(blend * (albedo - 1.0), whole_sum) + 1.0
        colors.append(color)
        residual = color - targets[c]
        loss = loss + residual * residual
        grad_color = 2.0 * residual * factor
        d_blend = d_blend + grad_color * (albedo - 1.0)
        tints.append(grad_color * blend * albedo * (1.0 - albedo))
    behind = exact(d_blend * blend, behind_sum)
    d_optical = d_blend * transmit * survive - behind
    d_density = d_optical * spacing * (1.0 / (1.0 + jnp.exp(-density_raw)))
    for c, value in enumerate([d_density] + tints):
        for i in range(value.shape[0]):
            draw[c : c + 1, i * LANES : (i + 1) * LANES] = value[i : i + 1, :]
    return colors, loss * factor


def ray_room(devices, shards, ray_count):
    slots = 4 * ray_count // devices
    others = pl.cdiv(devices * (ray_count - slots), devices - 1)
    return pl.cdiv(others, 16) * 16, pl.cdiv(pl.cdiv(slots * devices, shards), 16) * 16


def greet_all(groups, shards):
    me = lax.axis_index("grp") * shards + lax.axis_index("shard")
    total = groups * shards
    barrier = pltpu.get_barrier_semaphore()

    def greet(step, carry):
        other = lax.rem(me + step, total)
        pl.semaphore_signal(
            barrier, inc=1, device_id=(other // shards, lax.rem(other, shards)), device_id_type=MESH
        )
        return carry

    lax.fori_loop(1, total, greet, 0)
    return lambda: pl.semaphore_wait(barrier, total - 1)


def messages(groups, shards, source, landed, sent, arrived):
    me = lax.axis_index("grp") * shards + lax.axis_index("shard")
    total = groups * shards

    def start():
        def one(step, carry):
            other = lax.rem(me + step, total)
            pltpu.make_async_remote_copy(
                src_ref=source(other),
                dst_ref=landed.at[me],
                send_sem=sent,
                recv_sem=arrived,
                device_id=(other // shards, lax.rem(other, shards)),
                device_id_type=MESH,
            ).start()
            return carry

        lax.fori_loop(1, total, one, 0)

    everything = landed.at[pl.ds(0, total - 1)]

    def receive():
        pltpu.make_async_copy(everything, everything, arrived).wait()

    def finish():
        pltpu.make_async_copy(everything, everything, sent).wait()

    return start, receive, finish


def plane_gather(source, place, sent, passed, arrived):
    group = lax.axis_index("grp")
    shard = lax.axis_index("shard")
    shards = lax.axis_size("shard")
    chips = shards // 2
    chip = shard // 2
    core = lax.rem(shard, 2)
    partner = chip * 2 + 1 - core
    peers = [lax.rem(chip + step, chips) * 2 + core for step in range(1, chips)]
    origins = [lax.rem(chip + chips - step, chips) * 2 + core for step in range(1, chips)]

    def remote(src, dst, send_sem, recv_sem, to):
        return pltpu.make_async_remote_copy(
            src_ref=src,
            dst_ref=dst,
            send_sem=send_sem,
            recv_sem=recv_sem,
            device_id=(group, to),
            device_id_type=MESH,
        )

    def to(other):
        return remote(source, place(shard), sent.at[other], arrived.at[shard], other)

    def passing(origin):
        return remote(place(origin), place(origin), passed.at[origin], arrived.at[origin], partner)

    def start():
        for other in peers:
            to(other).start()
        to(partner).start()

    def receive(use):
        passing(partner).wait_recv()
        use(partner)
        for origin in origins:
            passing(origin).wait_recv()
            passing(origin).start()
            use(origin)
        for origin in origins:
            across = origin + 1 - 2 * core
            passing(across).wait_recv()
            use(across)

    def finish():
        for other in peers:
            to(other).wait_send()
        to(partner).wait_send()
        for origin in origins:
            passing(origin).wait_send()

    return start, receive, finish


def flipped(chip, step, chips):
    place, result = 1, 0
    while place < chips:
        bit = lax.rem(chip // place, 2)
        result = result + place * ((1 - bit) if step // place % 2 else bit)
        place *= 2
    return result


def weight_gather(source, weights, sent, far_sent, passed, far_passed, relayed, arrived, far_arrived):
    group = lax.axis_index("grp")
    shard = lax.axis_index("shard")
    groups = lax.axis_size("grp")
    chips = lax.axis_size("shard") // 2
    chip = shard // 2
    core = lax.rem(shard, 2)
    partner = chip * 2 + 1 - core
    rows, model = source.shape
    quarter = model // groups
    powers = [1 << b for b in range(chips.bit_length() - 1)]
    near = [flipped(chip, step, chips) * 2 + core for step in powers]
    far = [flipped(chip, s, chips) * 2 + core for s in range(1, chips) if s not in powers]
    steps = [lax.rem(group + step, groups) for step in range(1, groups)]

    def across(origin):
        return origin + 1 - 2 * core

    def whole(origin):
        return weights.at[pl.ds(pl.multiple_of(origin * rows, rows), rows)]

    def piece(origin, g):
        return weights.at[
            pl.ds(pl.multiple_of(origin * rows, rows), rows),
            pl.ds(pl.multiple_of(g * quarter, quarter), quarter),
        ]

    def remote(src, dst, send_sem, recv_sem, to_group, to):
        return pltpu.make_async_remote_copy(
            src_ref=src,
            dst_ref=dst,
            send_sem=send_sem,
            recv_sem=recv_sem,
            device_id=(to_group, to),
            device_id_type=MESH,
        )

    def near_to(other):
        return remote(source, whole(shard), sent.at[other], arrived.at[shard], group, other)

    def far_to(other):
        mine = source.at[:, pl.ds(pl.multiple_of(group * quarter, quarter), quarter)]
        return remote(
            mine, piece(shard, group), far_sent.at[other], far_arrived.at[shard, group], group, other
        )

    def near_pass(origin):
        return remote(
            whole(origin), whole(origin), passed.at[origin], arrived.at[origin], group, partner
        )

    def far_pass(origin, g):
        return remote(
            piece(origin, g),
            piece(origin, g),
            far_passed.at[origin, g],
            far_arrived.at[origin, g],
            group,
            partner,
        )

    def relay(origin, other):
        return remote(
            piece(origin, group),
            piece(origin, group),
            relayed.at[origin, other],
            far_arrived.at[origin, group],
            other,
            shard,
        )

    def start_far():
        for other in far:
            far_to(other).start()

    def start_near():
        for other in near:
            near_to(other).start()
        near_to(partner).start()

    def relay_far():
        for origin in far:
            far_pass(origin, group).wait_recv()
            for other in steps:
                relay(origin, other).start()
            far_pass(origin, group).start()

    def receive(use):
        near_pass(partner).wait_recv()
        use(partner)
        for origin in near:
            near_pass(origin).wait_recv()
            near_pass(origin).start()
            use(origin)
        for origin in far:
            for g in steps:
                far_pass(origin, g).wait_recv()
                far_pass(origin, g).start()
            use(origin)
        for origin in near:
            near_pass(across(origin)).wait_recv()
            use(across(origin))
        for origin in far:
            for g in range(groups):
                far_pass(across(origin), g).wait_recv()
            use(across(origin))

    def finish():
        for other in near:
            near_to(other).wait_send()
        near_to(partner).wait_send()
        for other in far:
            far_to(other).wait_send()
        for origin in near:
            near_pass(origin).wait_send()
        for origin in far:
            for g in range(groups):
                far_pass(origin, g).wait_send()
            for other in steps:
                relay(origin, other).wait_send()

    return start_far, start_near, relay_far, receive, finish


INPUTS = 10


def staged_kernel(groups, shards, *refs):
    wait_all = greet_all(groups, shards)
    sources, color, loss, grad, gain, latent = refs[:INPUTS], *refs[INPUTS : INPUTS + 5]
    rest = refs[INPUTS + 5 :]
    latent_buffer, buffers, arrived, left = rest[0], rest[1 : INPUTS + 1], *rest[-2:]
    inward = [
        pltpu.make_async_copy(sources[i], buffers[i], arrived.at[i]) for i in range(INPUTS)
    ]
    for copy in inward:
        copy.start()

    def latent_out():
        return pltpu.make_async_copy(latent_buffer, latent, left.at[HALVES])

    def grad_out(half, values):
        columns = values.shape[-1]
        strip = grad.at[:, :, half * columns : (half + 1) * columns]
        return pltpu.make_async_copy(values, strip, left.at[half])

    for copy in inward:
        copy.wait()
    whole_kernel(
        groups,
        shards,
        wait_all,
        latent_out,
        grad_out,
        *buffers,
        color,
        loss,
        gain,
        latent_buffer,
        *rest[INPUTS + 1 : -2],
    )


def whole_kernel(
    groups,
    shards,
    wait_all,
    latent_out,
    grad_out,
    latent_ref,
    weight_ref,
    weight_part_ref,
    gain_ref,
    gain_rows_ref,
    head_ref,
    points_ref,
    spacing_ref,
    target_ref,
    scene_ref,
    color_ref,
    loss_ref,
    gain_grad_ref,
    latent_grad_ref,
    count_row,
    landed_counts,
    lead_own,
    leads,
    hot_part,
    hot_parts,
    hot_piece,
    hot_all,
    message,
    landed,
    turned_own,
    turned,
    weights,
    wide_first,
    wide_second,
    first_t,
    second,
    second_t,
    head_t,
    encoded,
    coords,
    zeros_all,
    ones_all,
    twos_all,
    raw,
    draw,
    grad_first,
    grad_second,
    shades,
    landed_shades,
    d_field,
    fields,
    part,
    parts,
    done,
    gain_row,
    landed_gain,
    count_sent,
    count_arrived,
    lead_sent,
    lead_passed,
    lead_arrived,
    hot_sent,
    hot_arrived,
    piece_sent,
    piece_passed,
    piece_arrived,
    message_sent,
    message_arrived,
    shade_sent,
    shade_arrived,
    gain_sent,
    gain_arrived,
    turned_sent,
    turned_arrived,
    weight_sent,
    weight_passed,
    weight_arrived,
    far_sent,
    far_passed,
    far_relayed,
    far_arrived,
    field_sent,
    field_passed,
    field_arrived,
    part_sent,
    part_arrived,
    done_sent,
    done_arrived,
):
    group = lax.axis_index("grp")
    shard = lax.axis_index("shard")
    me = group * shards + shard
    total = groups * shards
    tokens, model = latent_ref.shape
    rows = model // shards
    width = head_ref.shape[1]
    ray_count, ray_depth = spacing_ref.shape
    slots = 4 * ray_count // total
    fan_scale = width ** (-0.5)
    per_layer = width * width // model
    strips = model // width
    period = FEATURES // strips
    fold_rows = 2 * FOLDED + per_layer
    sent_rows = FOLDED + per_layer
    own_rays, hot_rays = ray_room(total, shards, ray_count)
    f32 = jnp.float32
    bf16 = jnp.bfloat16

    latent = latent_ref[...].astype(f32)
    inv_rms = lax.rsqrt(jnp.mean(latent * latent, axis=1, keepdims=True) + norm_eps)
    x_norm = (latent * inv_rms * gain_ref[...]).astype(bf16)
    fold = jnp.where(
        iota((FOLDED, per_layer), 1) % period == iota((FOLDED, per_layer), 0), 1.0, 0.0
    ).astype(bf16)
    folded = product(fold, x_norm[:per_layer])
    folded_high = folded.astype(bf16).astype(f32)
    stacked = jnp.concatenate(
        [folded_high, folded - folded_high, x_norm[per_layer:].astype(f32)], axis=0
    )
    turned_own[...] = stacked.T.astype(bf16).reshape(turned_own.shape)

    scene = scene_ref[...]
    lane = iota((1, LANES), 1)
    ray_row = iota((ray_count, ray_count), 0)
    ray_column = iota((ray_count, ray_count), 1)
    scene_wide = jnp.broadcast_to(scene, (ray_count, ray_count))
    scene_tall = jnp.sum(jnp.where(ray_row == ray_column, scene_wide, 0), axis=1, keepdims=True)
    count_row[...] = jnp.sum(jnp.where(scene_tall == lane, 1.0, 0.0), axis=0, keepdims=True)
    same_scene = scene_tall == scene_wide
    rank_wide = jnp.sum(
        jnp.where(jnp.logical_and(same_scene, ray_row < ray_column), 1, 0), axis=0, keepdims=True
    )
    rank_tall = jnp.sum(
        jnp.where(jnp.logical_and(same_scene, ray_column < ray_row), 1, 0), axis=1, keepdims=True
    )
    head_t[...] = (head_ref[...].astype(f32) * fan_scale).T.astype(bf16)
    grad_first[...] = jnp.zeros_like(grad_first)
    grad_second[...] = jnp.zeros_like(grad_second)

    wait_all()

    def turned_copy(other, place):
        return pltpu.make_async_remote_copy(
            src_ref=turned_own.at[other],
            dst_ref=turned.at[place],
            send_sem=turned_sent.at[other],
            recv_sem=turned_arrived.at[place],
            device_id=(group, other),
            device_id_type=MESH,
        )

    def weight_of(origin):
        return weights[pl.ds(pl.multiple_of(origin * rows, rows), rows), :]

    others = [lax.rem(shard + step, shards) for step in range(1, shards)]
    start_counts, receive_counts, finish_counts = messages(
        groups, shards, lambda other: count_row, landed_counts, count_sent, count_arrived
    )
    start_far, start_near, relay_far, receive_weights, finish_weights = weight_gather(
        weight_ref,
        weights,
        weight_sent,
        far_sent,
        weight_passed,
        far_passed,
        far_relayed,
        weight_arrived,
        far_arrived,
    )
    start_messages, receive_messages, finish_messages = messages(
        groups, shards, lambda other: message.at[other], landed, message_sent, message_arrived
    )
    start_lead, receive_lead, finish_lead = plane_gather(
        lead_own, lambda origin: leads.at[origin], lead_sent, lead_passed, lead_arrived
    )
    start_counts()
    start_far()
    for other in others:
        turned_copy(other, shard).start()
    start_near()
    landed_counts[me] = count_row[...]
    turned[shard] = turned_own[shard]
    weights[pl.ds(pl.multiple_of(shard * rows, rows), rows), :] = weight_ref[...]

    relay_far()
    receive_counts()
    counts = landed_counts[:, 0, :]
    hot_lanes = jnp.min(jnp.where(counts == slots, 1, 0), axis=0, keepdims=True)
    hot = jnp.sum(jnp.where(hot_lanes > 0, lane, 0), axis=1, keepdims=True)
    hot_here = hot // shards == group
    hot_ray = scene == hot
    hot_target = (hot // shards) * shards + (me * slots + rank_wide) % shards
    owner = iota((total, ray_count), 0)
    mine = jnp.where(hot_ray, -1, scene) == owner
    led = jnp.where(hot_ray, hot_target, -1) == owner
    payload = jnp.concatenate([points_ref[...], spacing_ref[...]], axis=1)
    chosen = jnp.concatenate(
        [jnp.where(jnp.where(mine, rank_wide, -1) == j, 1.0, 0.0) for j in range(slots)]
        + [jnp.where(led, 1.0, 0.0)],
        axis=0,
    )
    filled = select(chosen.astype(bf16), payload)
    for j in range(slots + 1):
        message[:, 2 * j, :] = filled[j * total : (j + 1) * total, :LANES]
        message[:, 2 * j + 1, :] = filled[j * total : (j + 1) * total, LANES:]
    spread = jnp.where(iota((3, LANES), 1) % 4 == iota((3, LANES), 0), 1.0, 0.0)
    extra = over_first_select(target_ref[...], spread.astype(bf16)) + jnp.where(lane % 4 == 3, 1.0, 0.0)
    own_extra = jnp.where(rank_tall == lane // 4, extra, 0.0)
    hot_extra = jnp.where(lane // 4 == slots, extra, 0.0)
    message[:, 2 * slots + 2, :] = select(chosen_as(mine), own_extra) + select(
        chosen_as(led), hot_extra
    )
    start_messages()
    landed[me] = message[me]

    for other in others:
        turned_copy(other, other).wait_recv()
    hot_shard = jnp.where(hot_here, hot % shards, -1)
    lead = jnp.zeros((rows, fold_rows), f32)
    for origin in range(shards):
        lead = lead + jnp.where(hot_shard == origin, turned[origin].astype(f32), 0.0)
    lead_own[...] = lead.astype(bf16)
    start_lead()
    leads[shard] = lead_own[...]

    field_sum = [over_first(turned_own[shard], weight_ref[...])]

    def add_field(origin):
        field_sum[0] = field_sum[0] + over_first(turned_own[origin], weight_of(origin))

    receive_weights(add_field)

    def set_weights(which, field):
        first_rows = (field[:FOLDED] + field[FOLDED : 2 * FOLDED]) * fan_scale
        second_rows = field[2 * FOLDED :].astype(bf16).astype(f32) * fan_scale
        for m in range(strips):
            strip = slice(m * width, (m + 1) * width)
            store_rows(wide_first, m, FOLDED, strips, first_rows[:, strip])
            store_rows(wide_second, m, per_layer, strips, second_rows[:, strip])
        first = joined(wide_first)[:FEATURES]
        wide = joined(wide_second)
        first_high = first.astype(bf16).astype(f32)
        first_t[which] = jnp.concatenate([first_high, first - first_high], axis=0).T.astype(bf16)
        second[which] = wide.astype(bf16)
        second_t[which] = wide.T.astype(bf16)

    set_weights(0, field_sum[0])

    receive_messages()
    wanted = jnp.where(lane == me, 1.0, 0.0) * jnp.where(hot == me, 0.0, 1.0)
    many = slots * total
    tall_counts = jnp.concatenate([counts] * slots, axis=0).astype(bf16)
    wanted = jnp.broadcast_to(wanted, (8, LANES)).astype(bf16)
    wide_numbers = over_last(wanted, tall_counts)[0:1]
    earlier = chosen_as(iota((total, many), 0) < iota((total, many), 1) % total)
    offsets = product(over_last(wanted, counts.astype(bf16)).astype(bf16), earlier)[0:1]
    extras = landed[:, 2 * slots + 2, :]

    def arrived_slot(j):
        lifted = extras if j == 0 else pltpu.roll(extras, LANES - 4 * j, 1)
        return jnp.concatenate([landed[:, 2 * j, :], landed[:, 2 * j + 1, :], lifted], axis=1)

    slot_of = (iota((1, many), 1) // total).astype(f32)
    slot_at = jnp.where(wide_numbers > slot_of, offsets + slot_of, -1.0)
    keep = chosen_as(slot_at == iota((own_rays, many), 0).astype(f32))
    own_slots = select(keep, jnp.concatenate([arrived_slot(j) for j in range(slots)], axis=0))
    hot_place = (iota((hot_rays, total), 0) * shards + shard) // slots
    hot_keep = chosen_as(hot_place == iota((hot_rays, total), 1))
    hot_slots = select(hot_keep, arrived_slot(slots))
    own_pairs, hot_pairs = own_rays // 2, hot_rays // 2
    all_pairs = own_pairs + hot_pairs
    lower = jnp.concatenate([own_slots[:own_pairs], hot_slots[:hot_pairs]], axis=0)
    upper = jnp.concatenate([own_slots[own_pairs:], hot_slots[hot_pairs:]], axis=0)
    low = lane < ray_depth

    def unpack(at):
        left, right = lower[:, at : at + LANES], upper[:, at : at + LANES]
        return (
            jnp.where(low, left, pltpu.roll(right, ray_depth, 1)),
            jnp.where(low, pltpu.roll(left, ray_depth, 1), right),
        )

    coords[0], coords[1] = unpack(0)
    coords[2], spacing = unpack(LANES)

    def widen(c):
        at = 2 * LANES + c
        return jnp.where(low, lower[:, at : at + 1], upper[:, at : at + 1])

    own_count = jnp.sum(jnp.where(slot_of == 0.0, wide_numbers, 0.0), axis=1, keepdims=True)
    own_factor = 1.0 / (total * jnp.maximum(own_count, 1.0))
    hot_factor = 1.0 / (total * total * slots)
    factor = widen(3) * jnp.where(iota((all_pairs, 1), 0) < own_pairs, own_factor, hot_factor)
    targets = [widen(c) for c in range(3)]
    own_blocks = own_pairs // 8
    blocks = all_pairs // 8

    def forward(which):
        def step(i, carry):
            forward_block(
                i,
                coords,
                first_t.at[which],
                second_t.at[which],
                head_ref,
                encoded,
                zeros_all,
                ones_all,
                twos_all,
                raw,
            )
            return carry

        return step

    lax.fori_loop(0, own_blocks, forward(0), 0)
    lead_field = [over_first(lead_own[...], weight_ref[...])]

    def add_lead(origin):
        lead_field[0] = lead_field[0] + over_first(leads[origin], weight_of(origin))

    receive_lead(add_lead)
    set_weights(1, lead_field[0])
    lax.fori_loop(own_blocks, blocks, forward(1), 0)
    colors, losses = render_middle(ray_depth, raw, spacing, targets, factor, draw)
    def backward(which):
        def step(i, carry):
            backward_block(
                i, draw, second.at[which], head_t, zeros_all, ones_all, twos_all, grad_first, grad_second
            )
            return carry

        return step

    columns = model // HALVES
    piece = model // shards

    def field_strips():
        for lanes in range(width // LANES):
            at = slice(lanes * LANES, (lanes + 1) * LANES)
            wide_first[lanes, :FEATURES, :] = grad_first[:, at]
            wide_second[lanes] = grad_second[:, at]
        strip_values = []
        for m in range(strips):
            head_rows = load_rows(wide_first, m, FOLDED, strips)
            head_rows = jnp.where(iota((FOLDED, 1), 0) < period, head_rows, 0.0)
            strip_values.append(
                jnp.concatenate([head_rows, load_rows(wide_second, m, per_layer, strips)], axis=0)
            )
        return strip_values

    def hot_copy(other, place):
        return pltpu.make_async_remote_copy(
            src_ref=hot_part.at[other],
            dst_ref=hot_parts.at[place],
            send_sem=hot_sent.at[other],
            recv_sem=hot_arrived.at[place],
            device_id=(group, other),
            device_id_type=MESH,
        )

    lax.fori_loop(own_blocks, blocks, backward(1), 0)
    hot_strips = jnp.concatenate(field_strips(), axis=1)
    for p in range(shards):
        hot_part[p] = hot_strips[:, p * piece : (p + 1) * piece].astype(bf16)
    for other in others:
        hot_copy(other, shard).start()
    grad_first[...] = jnp.zeros_like(grad_first)
    grad_second[...] = jnp.zeros_like(grad_second)
    lax.fori_loop(0, own_blocks, backward(0), 0)
    for m, values in enumerate(field_strips()):
        half, place = divmod(m * width, columns)
        d_field[half, :, place : place + width] = values.astype(bf16)

    gathers = [
        plane_gather(
            d_field.at[half],
            lambda origin, half=half: fields.at[half, origin],
            field_sent.at[half],
            field_passed.at[half],
            field_arrived.at[half],
        )
        for half in range(HALVES)
    ]
    gathers[0][0]()

    shade = jnp.where(
        lane == 4 * slots + 4,
        jnp.sum(losses, axis=(0, 1), keepdims=True) * (1.0 / ray_depth),
        0.0,
    )

    def color_rows(start, stop):
        columns = []
        for side in (0, ray_depth):
            values = jnp.zeros((stop - start, LANES), f32)
            for c in range(3):
                values = jnp.where(lane == c, colors[c][start:stop, side : side + 1], values)
            columns.append(values)
        return jnp.concatenate(columns, axis=0)

    own_colors = color_rows(0, own_pairs)
    hot_colors = color_rows(own_pairs, all_pairs)
    back = select(keep, own_colors, (0, 0))
    for j in range(slots):
        part_back = back[j * total : (j + 1) * total]
        shade = shade + (part_back if j == 0 else pltpu.roll(part_back, 4 * j, 1))
    shade = shade + pltpu.roll(select(hot_keep, hot_colors, (0, 0)), 4 * slots, 1)
    shades[:, 0, :] = shade
    start_shades, receive_shades, finish_shades = messages(
        groups, shards, lambda other: shades.at[other], landed_shades, shade_sent, shade_arrived
    )
    start_shades()
    landed_shades[me] = shades[me]

    piece_sum = hot_part[shard].astype(f32)
    for other in others:
        hot_copy(other, other).wait_recv()
        piece_sum = piece_sum + hot_parts[other].astype(f32)
    hot_piece[...] = piece_sum.astype(bf16)
    start_hot, receive_hot, finish_hot = plane_gather(
        hot_piece, lambda origin: hot_all.at[origin], piece_sent, piece_passed, piece_arrived
    )
    start_hot()
    for half in range(1, HALVES):
        gathers[half][0]()
    hot_all[shard] = hot_piece[...]

    group_steps = [lax.rem(group + step, groups) for step in range(1, groups)]

    def part_copy(half, other, place):
        return pltpu.make_async_remote_copy(
            src_ref=part.at[half, other],
            dst_ref=parts.at[half, place],
            send_sem=part_sent.at[half, other],
            recv_sem=part_arrived.at[half, place],
            device_id=(other, shard),
            device_id_type=MESH,
        )

    def done_copy(half, other, place):
        return pltpu.make_async_remote_copy(
            src_ref=done.at[half, place],
            dst_ref=done.at[half, place],
            send_sem=done_sent.at[half, other],
            recv_sem=done_arrived.at[half, place],
            device_id=(other, shard),
            device_id_type=MESH,
        )

    def head_term(origin, values):
        lead = values[:FOLDED]
        return product(turned[origin], jnp.concatenate([lead, lead, values[FOLDED:]], axis=0))

    def gather_half(half):
        head_sum = [head_term(shard, d_field[half])]

        def add_head(origin):
            head_sum[0] = head_sum[0] + head_term(origin, fields[half, origin])

        gathers[half][1](add_head)
        if half == 0:
            receive_hot(lambda origin: None)
        per_half = shards // HALVES
        hot_values = jnp.concatenate(
            [hot_all[p] for p in range(half * per_half, (half + 1) * per_half)], axis=1
        )
        hot_top = hot_values[:FOLDED]
        head_sum[0] = head_sum[0] + product(
            lead_own[...], jnp.concatenate([hot_top, hot_top, hot_values[FOLDED:]], axis=0)
        )
        part[half] = head_sum[0].astype(bf16).reshape(part.shape[1:])
        for other in group_steps:
            part_copy(half, other, group).start()

    gain_terms = []

    def sum_half(half):
        slice_sum = part[half, group].astype(f32)
        for other in group_steps:
            part_copy(half, other, other).wait_recv()
            slice_sum = slice_sum + parts[half, other].astype(f32)
        weight = weight_part_ref[group][:, half * columns : (half + 1) * columns].astype(f32)
        gain_terms.append(jnp.sum(slice_sum * weight, axis=1, keepdims=True))
        if half == HALVES - 1:
            same_row = iota((slice_rows, slice_rows), 0) == iota((slice_rows, slice_rows), 1)
            gain_row[0:1, :slice_rows] = jnp.sum(
                jnp.where(same_row, sum(gain_terms), 0.0), axis=0, keepdims=True
            )
            start_gain()
        done[half, group] = slice_sum.astype(bf16)
        for other in group_steps:
            done_copy(half, other, group).start()

    slice_rows = rows // groups
    start_gain, receive_gain, finish_gain = messages(
        groups, shards, lambda other: gain_row, landed_gain, gain_sent, gain_arrived
    )
    for half in range(HALVES):
        gather_half(half)
        if half >= LAG:
            sum_half(half - LAG)
    for half in range(HALVES - LAG, HALVES):
        sum_half(half)
    landed_gain[me] = gain_row[...]

    token = iota((tokens, sent_rows), 0)
    source = jnp.where(token < per_layer, token % period, token - per_layer + FOLDED)
    copies = jnp.where(source == iota((tokens, sent_rows), 1), 1.0, 0.0).astype(bf16)
    own_field = jnp.concatenate([d_field[half] for half in range(HALVES)], axis=1)
    hot_field = jnp.concatenate([hot_all[p] for p in range(shards)], axis=1)
    own_field = jnp.where(hot == me, hot_field.astype(f32), own_field.astype(f32)).astype(bf16)
    d_norm = over_last(product(copies, own_field).astype(bf16), weights[...])
    latent = latent_ref[...].astype(f32)
    inv_rms = lax.rsqrt(jnp.mean(latent * latent, axis=1, keepdims=True) + norm_eps)
    x_hat = latent * inv_rms
    d_scaled = d_norm * gain_ref[...]
    latent_grad_ref[...] = (
        inv_rms * (d_scaled - x_hat * jnp.mean(d_scaled * x_hat, axis=1, keepdims=True))
    ).astype(bf16)

    latent_out().start()
    receive_shades()
    returned = landed_shades[:, 0, :]
    loss_ref[...] = jnp.sum(
        jnp.where(lane == 4 * slots + 4, returned, 0.0), axis=(0, 1), keepdims=True
    )
    picked = over_first_select(returned, chosen_as(mine) + chosen_as(led))
    first_place = jnp.where(hot_ray, 4 * slots, 4 * rank_wide)
    place = iota((LANES, ray_count), 0)
    for c in range(3):
        color_ref[c : c + 1, :] = jnp.sum(
            jnp.where(place == first_place + c, picked, 0.0), axis=0, keepdims=True
        )

    for half in range(HALVES):
        for other in group_steps:
            done_copy(half, other, other).wait_recv()
        grad_out(half, done.at[half]).start()
    receive_gain()
    gains = landed_gain[:, 0, :slice_rows]
    gains = jnp.concatenate([gains[g * shards : (g + 1) * shards] for g in range(groups)], axis=1)
    gain_grad_ref[...] = gains / gain_rows_ref[...]

    latent_out().wait()
    for half in range(HALVES):
        grad_out(half, done.at[half]).wait()
    finish_counts()
    finish_weights()
    finish_messages()
    finish_lead()
    finish_hot()
    for other in others:
        hot_copy(other, shard).wait_send()
    finish_shades()
    finish_gain()
    for other in others:
        turned_copy(other, shard).wait_send()
    for half in range(HALVES):
        gathers[half][2]()
        for other in group_steps:
            part_copy(half, other, group).wait_send()
            done_copy(half, other, group).wait_send()


def body(
    latents,
    head_weight,
    norm_gain,
    color_head,
    sample_points,
    sample_spacing,
    ray_targets,
    ray_scene,
):
    groups, shards = lax.axis_size("grp"), lax.axis_size("shard")
    devices = groups * shards
    ray_count, ray_depth = sample_spacing.shape
    tokens, model = latents.shape
    width = color_head.shape[1]
    rows = model // shards
    slots = 4 * ray_count // devices
    per_layer = width * width // model
    fold_rows = 2 * FOLDED + per_layer
    sent_rows = FOLDED + per_layer
    samples = sum(ray_room(devices, shards, ray_count)) * ray_depth
    columns = model // HALVES
    slice_rows = rows // groups
    in_vmem = pl.BlockSpec(memory_space=pltpu.VMEM)
    dma = pltpu.SemaphoreType.DMA
    f32, bf16 = jnp.float32, jnp.bfloat16
    vmem = pltpu.VMEM
    anywhere = pl.BlockSpec(memory_space=pl.ANY)
    inputs = (
        latents,
        head_weight,
        head_weight.reshape(groups, slice_rows, model),
        norm_gain.reshape(1, model),
        norm_gain.reshape(shards, rows),
        color_head,
        sample_points,
        sample_spacing,
        ray_targets,
        ray_scene.reshape(1, ray_count),
    )
    colors, loss, head, gain, latent_grad = pl.pallas_call(
        functools.partial(staged_kernel, groups, shards),
        in_specs=[anywhere] * INPUTS,
        out_specs=[in_vmem, in_vmem, anywhere, in_vmem, anywhere],
        out_shape=[
            jax.ShapeDtypeStruct((3, ray_count), f32),
            jax.ShapeDtypeStruct((1, 1), f32),
            jax.ShapeDtypeStruct((groups, slice_rows, model), bf16),
            jax.ShapeDtypeStruct((shards, rows), f32),
            jax.ShapeDtypeStruct((tokens, model), bf16),
        ],
        scratch_shapes=[vmem((tokens, model), bf16)]
        + [vmem(value.shape, value.dtype) for value in inputs]
        + [
            vmem((1, LANES), f32),
            vmem((devices, 1, LANES), f32),
            vmem((rows, fold_rows), bf16),
            vmem((shards, rows, fold_rows), bf16),
            vmem((shards, sent_rows, rows), bf16),
            vmem((shards, sent_rows, rows), bf16),
            vmem((sent_rows, rows), bf16),
            vmem((shards, sent_rows, rows), bf16),
            vmem((devices, 2 * slots + 3, LANES), f32),
            vmem((devices, 2 * slots + 3, LANES), f32),
            vmem((shards, rows, fold_rows), bf16),
            vmem((shards, rows, fold_rows), bf16),
            vmem((model, model), bf16),
            vmem((width // LANES, FOLDED * model // width, LANES), f32),
            vmem((width // LANES, width, LANES), f32),
            vmem((2, width, 2 * FEATURES), bf16),
            vmem((2, width, width), bf16),
            vmem((2, width, width), bf16),
            vmem((width, 4), bf16),
            vmem((8 * FEATURES, LANES), f32),
            vmem((3, samples // LANES, LANES), f32),
            vmem((FEATURES, samples), bf16),
            vmem((width, samples), bf16),
            vmem((width, samples), bf16),
            vmem((4, samples // LANES, LANES), f32),
            vmem((4, samples), f32),
            vmem((FEATURES, width), f32),
            vmem((width, width), f32),
            vmem((devices, 1, LANES), f32),
            vmem((devices, 1, LANES), f32),
            vmem((HALVES, sent_rows, columns), bf16),
            vmem((HALVES, shards, sent_rows, columns), bf16),
            vmem((HALVES, groups, slice_rows, columns), bf16),
            vmem((HALVES, groups, slice_rows, columns), bf16),
            vmem((HALVES, groups, slice_rows, columns), bf16),
            vmem((1, LANES), f32),
            vmem((devices, 1, LANES), f32),
            dma,
            dma,
            dma((shards,)),
            dma((shards,)),
            dma((shards,)),
            dma((shards,)),
            dma((shards,)),
            dma((shards,)),
            dma((shards,)),
            dma((shards,)),
            dma,
            dma,
            dma,
            dma,
            dma,
            dma,
            dma((shards,)),
            dma((shards,)),
            dma((shards,)),
            dma((shards,)),
            dma((shards,)),
            dma((shards,)),
            dma((shards, groups)),
            dma((shards, groups)),
            dma((shards, groups)),
            dma((HALVES, shards)),
            dma((HALVES, shards)),
            dma((HALVES, shards)),
            dma((HALVES, groups)),
            dma((HALVES, groups)),
            dma((HALVES, groups)),
            dma((HALVES, groups)),
            dma((INPUTS,)),
            dma((HALVES + 1,)),
        ],
        compiler_params=pltpu.CompilerParams(collective_id=1, has_side_effects=True),
    )(*inputs)
    colors, loss, head_grad, gain, latent_grad = hand_out(colors, loss, head, gain, latent_grad)
    return (colors, loss[0, 0], head_grad, gain.reshape(model), latent_grad)


def hand_out_kernel(count, *refs):
    sources, targets = refs[:count], refs[count : 2 * count]
    buffers = refs[2 * count : 3 * count]
    wide, arrived, left = refs[3 * count :]
    inward = [
        pltpu.make_async_copy(sources[i], buffers[i], arrived.at[i]) for i in range(count)
    ]
    for copy in inward:
        copy.start()
    outward = [
        pltpu.make_async_copy(buffers[i], targets[i], left.at[i]) for i in range(1, count)
    ]
    groups, slice_rows, model = buffers[0].shape
    inward[0].wait()
    for g in range(groups):
        rows = pl.ds(g * slice_rows, slice_rows)
        wide[rows, :] = buffers[0][g].astype(jnp.float32)
        outward.append(
            pltpu.make_async_copy(wide.at[rows], targets[0].at[rows], left.at[count + g])
        )
        outward[-1].start()
    for i in range(1, count):
        inward[i].wait()
        outward[i - 1].start()
    for copy in outward:
        copy.wait()


def hand_out(colors, loss, head, gain, latent_grad):
    groups, slice_rows, model = head.shape
    values = [head, latent_grad, colors, loss, gain]
    count = len(values)
    full = jax.ShapeDtypeStruct((groups * slice_rows, model), jnp.float32)
    anywhere = pl.BlockSpec(memory_space=pl.ANY)
    head, latent_grad, colors, loss, gain = pl.pallas_call(
        functools.partial(hand_out_kernel, count),
        in_specs=[anywhere] * count,
        out_specs=[anywhere] * count,
        out_shape=[full] + [jax.ShapeDtypeStruct(v.shape, v.dtype) for v in values[1:]],
        scratch_shapes=[pltpu.VMEM(v.shape, v.dtype) for v in values]
        + [
            pltpu.VMEM(full.shape, full.dtype),
            pltpu.SemaphoreType.DMA((count,)),
            pltpu.SemaphoreType.DMA((count + groups,)),
        ],
    )(*values)
    return colors, loss, head, gain, latent_grad


def solution(mesh):
    placed = (
        P(("grp", "shard"), None),
        P("shard", None),
        P(),
        P(),
        P(("grp", "shard"), None),
        P(("grp", "shard"), None),
        P(None, ("grp", "shard")),
        P(("grp", "shard")),
    )
    return jax.shard_map(
        body,
        mesh=mesh,
        in_specs=placed,
        out_specs=(
            P(None, ("grp", "shard")),
            P(),
            P("shard", None),
            P(),
            P(("grp", "shard"), None),
        ),
        check_vma=False,
    )
```

```python
import functools

import jax
import jax.numpy as jnp
from jax import lax
from jax.experimental import pallas as pl
from jax.experimental.pallas import tpu as pltpu
from jax.sharding import PartitionSpec as P

norm_eps = 1e-06

LANES = 128
HALVES = 4
FEATURES = 48
FOLDED = 16
LAG = 4
BLOCK = 1024
SINE = (3.14159265358979, -5.16771278004997, 2.55016403987735, -0.599264529320792, 0.0821458866111282, -0.00737043094571435, 0.000466302805767613, -0.0000219153534478303)
MESH = pl.DeviceIdType.MESH


def sine_of_pi(turns):
    whole = jnp.floor(turns + 0.5)
    rest = turns - whole
    odd = whole - 2.0 * jnp.floor(whole * 0.5)
    square = rest * rest
    value = jnp.full_like(square, SINE[-1])
    for coefficient in SINE[-2::-1]:
        value = value * square + coefficient
    return value * (rest * (1.0 - 2.0 * odd))


def product(a, b):
    return jnp.dot(a, b, preferred_element_type=jnp.float32)


def exact(a, b, contract=(1, 0)):
    return lax.dot_general(
        a,
        b,
        (((contract[0],), (contract[1],)), ((), ())),
        preferred_element_type=jnp.float32,
        precision=lax.Precision.HIGHEST,
    )


def select(onehot, values, contract=(1, 0)):
    total = 0.0
    for _ in range(3):
        term = values.astype(jnp.bfloat16)
        values = values - term.astype(jnp.float32)
        total = total + lax.dot_general(
            onehot,
            term,
            (((contract[0],), (contract[1],)), ((), ())),
            preferred_element_type=jnp.float32,
        )
    return total


def over_first_select(values, onehot):
    total = 0.0
    for _ in range(3):
        term = values.astype(jnp.bfloat16)
        values = values - term.astype(jnp.float32)
        total = total + over_first(term, onehot)
    return total


def chosen_as(mask):
    return jnp.where(mask, 1.0, 0.0).astype(jnp.bfloat16)


def over_first(a, b):
    return lax.dot_general(a, b, (((0,), (0,)), ((), ())), preferred_element_type=jnp.float32)


def over_last(a, b):
    return lax.dot_general(a, b, (((1,), (1,)), ((), ())), preferred_element_type=jnp.float32)


def iota(shape, axis):
    return lax.broadcasted_iota(jnp.int32, shape, axis)


def store_rows(ref, start, count, stride, values):
    for lanes in range(ref.shape[0]):
        ref[lanes, pl.ds(start, count, stride=stride), :] = values[:, lanes * LANES : (lanes + 1) * LANES]


def load_rows(ref, start, count, stride):
    return jnp.concatenate(
        [ref[lanes, pl.ds(start, count, stride=stride), :] for lanes in range(ref.shape[0])], axis=1
    )


def joined(ref):
    return jnp.concatenate([ref[lanes] for lanes in range(ref.shape[0])], axis=1)


def encode_rows(axes, encoded):
    sines = [sine_of_pi(a) for a in axes]
    cosines = [sine_of_pi(a + 0.5) for a in axes]
    octaves = FEATURES // 6
    for octave in range(octaves):
        for c in range(3):
            encoded[pl.ds(octave * 6 + c, 8, stride=FEATURES), :] = sines[c]
            encoded[pl.ds(octave * 6 + 3 + c, 8, stride=FEATURES), :] = cosines[c]
        if octave < octaves - 1:
            for c in range(3):
                twice = sines[c] + sines[c]
                sines[c], cosines[c] = twice * cosines[c], 1.0 - twice * sines[c]


def forward_block(i, coords, first, second_t, head, encoded, zeros_all, ones_all, twos_all, raw):
    row = pl.multiple_of(i * 8, 8)
    encode_rows([coords[c, pl.ds(row, 8), :] for c in range(3)], encoded)
    h_zero = jnp.concatenate(
        [encoded[FEATURES * r : FEATURES * (r + 1), :].astype(jnp.bfloat16) for r in range(8)], axis=1
    )
    at = pl.multiple_of(i * BLOCK, BLOCK)
    zeros_all[:, pl.ds(at, BLOCK)] = h_zero
    twice = jnp.concatenate([h_zero, h_zero], axis=0)
    h_one = jnp.maximum(product(first[...], twice).astype(jnp.bfloat16), 0)
    ones_all[:, pl.ds(at, BLOCK)] = h_one
    h_two = jnp.maximum(product(second_t[...], h_one).astype(jnp.bfloat16), 0)
    twos_all[:, pl.ds(at, BLOCK)] = h_two
    values = product(head[...], h_two)
    for r in range(8):
        for c in range(4):
            raw[c, pl.ds(row + r, 1), :] = values[c : c + 1, r * LANES : (r + 1) * LANES]


def backward_block(i, draw, second, head_t, zeros_all, ones_all, twos_all, grad_first, grad_second):
    at = pl.multiple_of(i * BLOCK, BLOCK)
    d_raw = draw[:, pl.ds(at, BLOCK)].astype(jnp.bfloat16)
    zero = jnp.zeros((), jnp.bfloat16)
    d_two = product(head_t[...], d_raw).astype(jnp.bfloat16)
    d_atwo = jnp.where(twos_all[:, pl.ds(at, BLOCK)] > 0, d_two, zero)
    h_one = ones_all[:, pl.ds(at, BLOCK)]
    grad_second[...] += over_last(h_one, d_atwo)
    d_one = product(second[...], d_atwo).astype(jnp.bfloat16)
    d_aone = jnp.where(h_one > 0, d_one, zero)
    grad_first[...] += over_last(zeros_all[:, pl.ds(at, BLOCK)], d_aone)


def render_middle(ray_depth, raw, spacing, targets, factor, draw):
    row = iota((LANES, LANES), 0)
    column = iota((LANES, LANES), 1)
    same = row // ray_depth == column // ray_depth
    before_sum = jnp.where(jnp.logical_and(same, row < column), 1.0, 0.0)
    behind_sum = jnp.where(jnp.logical_and(same, row > column), 1.0, 0.0)
    whole_sum = jnp.where(same, 1.0, 0.0)
    density_raw = raw[0]
    density = jnp.maximum(density_raw, 0.0) + jnp.log1p(jnp.exp(-jnp.abs(density_raw)))
    optical = density * spacing
    transmit = jnp.exp(-exact(optical, before_sum))
    survive = jnp.exp(-optical)
    blend = transmit * (1.0 - survive)
    d_blend = jnp.zeros_like(blend)
    loss = jnp.zeros_like(blend)
    tints = []
    colors = []
    for c in range(3):
        albedo = 1.0 / (1.0 + jnp.exp(-raw[c + 1]))
        color = exact(blend * (albedo - 1.0), whole_sum) + 1.0
        colors.append(color)
        residual = color - targets[c]
        loss = loss + residual * residual
        grad_color = 2.0 * residual * factor
        d_blend = d_blend + grad_color * (albedo - 1.0)
        tints.append(grad_color * blend * albedo * (1.0 - albedo))
    behind = exact(d_blend * blend, behind_sum)
    d_optical = d_blend * transmit * survive - behind
    d_density = d_optical * spacing * (1.0 / (1.0 + jnp.exp(-density_raw)))
    for c, value in enumerate([d_density] + tints):
        for i in range(value.shape[0]):
            draw[c : c + 1, i * LANES : (i + 1) * LANES] = value[i : i + 1, :]
    return colors, loss * factor


def ray_room(devices, shards, ray_count):
    slots = 4 * ray_count // devices
    others = pl.cdiv(devices * (ray_count - slots), devices - 1)
    return pl.cdiv(others, 16) * 16, pl.cdiv(pl.cdiv(slots * devices, shards), 16) * 16


def greet_all(groups, shards):
    me = lax.axis_index("grp") * shards + lax.axis_index("shard")
    total = groups * shards
    barrier = pltpu.get_barrier_semaphore()

    def greet(step, carry):
        other = lax.rem(me + step, total)
        pl.semaphore_signal(
            barrier, inc=1, device_id=(other // shards, lax.rem(other, shards)), device_id_type=MESH
        )
        return carry

    lax.fori_loop(1, total, greet, 0)
    return lambda: pl.semaphore_wait(barrier, total - 1)


def messages(groups, shards, source, landed, sent, arrived):
    me = lax.axis_index("grp") * shards + lax.axis_index("shard")
    total = groups * shards

    def start():
        def one(step, carry):
            other = lax.rem(me + step, total)
            pltpu.make_async_remote_copy(
                src_ref=source(other),
                dst_ref=landed.at[me],
                send_sem=sent,
                recv_sem=arrived,
                device_id=(other // shards, lax.rem(other, shards)),
                device_id_type=MESH,
            ).start()
            return carry

        lax.fori_loop(1, total, one, 0)

    everything = landed.at[pl.ds(0, total - 1)]

    def receive():
        pltpu.make_async_copy(everything, everything, arrived).wait()

    def finish():
        pltpu.make_async_copy(everything, everything, sent).wait()

    return start, receive, finish


def plane_gather(source, place, sent, passed, arrived):
    group = lax.axis_index("grp")
    shard = lax.axis_index("shard")
    shards = lax.axis_size("shard")
    chips = shards // 2
    chip = shard // 2
    core = lax.rem(shard, 2)
    partner = chip * 2 + 1 - core
    peers = [lax.rem(chip + step, chips) * 2 + core for step in range(1, chips)]
    origins = [lax.rem(chip + chips - step, chips) * 2 + core for step in range(1, chips)]

    def remote(src, dst, send_sem, recv_sem, to):
        return pltpu.make_async_remote_copy(
            src_ref=src,
            dst_ref=dst,
            send_sem=send_sem,
            recv_sem=recv_sem,
            device_id=(group, to),
            device_id_type=MESH,
        )

    def to(other):
        return remote(source, place(shard), sent.at[other], arrived.at[shard], other)

    def passing(origin):
        return remote(place(origin), place(origin), passed.at[origin], arrived.at[origin], partner)

    def start():
        for other in peers:
            to(other).start()
        to(partner).start()

    def receive(use):
        passing(partner).wait_recv()
        use(partner)
        for origin in origins:
            passing(origin).wait_recv()
            passing(origin).start()
            use(origin)
        for origin in origins:
            across = origin + 1 - 2 * core
            passing(across).wait_recv()
            use(across)

    def finish():
        for other in peers:
            to(other).wait_send()
        to(partner).wait_send()
        for origin in origins:
            passing(origin).wait_send()

    return start, receive, finish


def flipped(chip, step, chips):
    place, result = 1, 0
    while place < chips:
        bit = lax.rem(chip // place, 2)
        result = result + place * ((1 - bit) if step // place % 2 else bit)
        place *= 2
    return result


def weight_gather(source, weights, sent, far_sent, passed, far_passed, relayed, arrived, far_arrived):
    group = lax.axis_index("grp")
    shard = lax.axis_index("shard")
    groups = lax.axis_size("grp")
    chips = lax.axis_size("shard") // 2
    chip = shard // 2
    core = lax.rem(shard, 2)
    partner = chip * 2 + 1 - core
    rows, model = source.shape
    quarter = model // groups
    powers = [1 << b for b in range(chips.bit_length() - 1)]
    near = [flipped(chip, step, chips) * 2 + core for step in powers]
    far = [flipped(chip, s, chips) * 2 + core for s in range(1, chips) if s not in powers]
    steps = [lax.rem(group + step, groups) for step in range(1, groups)]

    def across(origin):
        return origin + 1 - 2 * core

    def whole(origin):
        return weights.at[pl.ds(pl.multiple_of(origin * rows, rows), rows)]

    def piece(origin, g):
        return weights.at[
            pl.ds(pl.multiple_of(origin * rows, rows), rows),
            pl.ds(pl.multiple_of(g * quarter, quarter), quarter),
        ]

    def remote(src, dst, send_sem, recv_sem, to_group, to):
        return pltpu.make_async_remote_copy(
            src_ref=src,
            dst_ref=dst,
            send_sem=send_sem,
            recv_sem=recv_sem,
            device_id=(to_group, to),
            device_id_type=MESH,
        )

    def near_to(other):
        return remote(source, whole(shard), sent.at[other], arrived.at[shard], group, other)

    def far_to(other):
        mine = source.at[:, pl.ds(pl.multiple_of(group * quarter, quarter), quarter)]
        return remote(
            mine, piece(shard, group), far_sent.at[other], far_arrived.at[shard, group], group, other
        )

    def near_pass(origin):
        return remote(
            whole(origin), whole(origin), passed.at[origin], arrived.at[origin], group, partner
        )

    def far_pass(origin, g):
        return remote(
            piece(origin, g),
            piece(origin, g),
            far_passed.at[origin, g],
            far_arrived.at[origin, g],
            group,
            partner,
        )

    def relay(origin, other):
        return remote(
            piece(origin, group),
            piece(origin, group),
            relayed.at[origin, other],
            far_arrived.at[origin, group],
            other,
            shard,
        )

    def start_far():
        for other in far:
            far_to(other).start()

    def start_near():
        for other in near:
            near_to(other).start()
        near_to(partner).start()

    def relay_far():
        for origin in far:
            far_pass(origin, group).wait_recv()
            for other in steps:
                relay(origin, other).start()
            far_pass(origin, group).start()

    def receive(use):
        near_pass(partner).wait_recv()
        use(partner)
        for origin in near:
            near_pass(origin).wait_recv()
            near_pass(origin).start()
            use(origin)
        for origin in far:
            for g in steps:
                far_pass(origin, g).wait_recv()
                far_pass(origin, g).start()
            use(origin)
        for origin in near:
            near_pass(across(origin)).wait_recv()
            use(across(origin))
        for origin in far:
            for g in range(groups):
                far_pass(across(origin), g).wait_recv()
            use(across(origin))

    def finish():
        for other in near:
            near_to(other).wait_send()
        near_to(partner).wait_send()
        for other in far:
            far_to(other).wait_send()
        for origin in near:
            near_pass(origin).wait_send()
        for origin in far:
            for g in range(groups):
                far_pass(origin, g).wait_send()
            for other in steps:
                relay(origin, other).wait_send()

    return start_far, start_near, relay_far, receive, finish


INPUTS = 10


def staged_kernel(groups, shards, *refs):
    wait_all = greet_all(groups, shards)
    sources, color, loss, grad, gain, latent = refs[:INPUTS], *refs[INPUTS : INPUTS + 5]
    rest = refs[INPUTS + 5 :]
    latent_buffer, buffers, arrived, left = rest[0], rest[1 : INPUTS + 1], *rest[-2:]
    inward = [
        pltpu.make_async_copy(sources[i], buffers[i], arrived.at[i]) for i in range(INPUTS)
    ]
    for copy in inward:
        copy.start()

    def latent_out():
        return pltpu.make_async_copy(latent_buffer, latent, left.at[HALVES])

    def grad_out(half, values):
        columns = values.shape[-1]
        strip = grad.at[:, :, half * columns : (half + 1) * columns]
        return pltpu.make_async_copy(values, strip, left.at[half])

    for copy in inward:
        copy.wait()
    whole_kernel(
        groups,
        shards,
        wait_all,
        latent_out,
        grad_out,
        *buffers,
        color,
        loss,
        gain,
        latent_buffer,
        *rest[INPUTS + 1 : -2],
    )


def whole_kernel(
    groups,
    shards,
    wait_all,
    latent_out,
    grad_out,
    latent_ref,
    weight_ref,
    weight_part_ref,
    gain_ref,
    gain_rows_ref,
    head_ref,
    points_ref,
    spacing_ref,
    target_ref,
    scene_ref,
    color_ref,
    loss_ref,
    gain_grad_ref,
    latent_grad_ref,
    count_row,
    landed_counts,
    lead_own,
    leads,
    hot_part,
    hot_parts,
    hot_piece,
    hot_all,
    message,
    landed,
    turned_own,
    turned,
    weights,
    wide_first,
    wide_second,
    first_t,
    second,
    second_t,
    head_t,
    encoded,
    coords,
    zeros_all,
    ones_all,
    twos_all,
    raw,
    draw,
    grad_first,
    grad_second,
    shades,
    landed_shades,
    d_field,
    fields,
    part,
    parts,
    done,
    gain_row,
    landed_gain,
    count_sent,
    count_arrived,
    lead_sent,
    lead_passed,
    lead_arrived,
    hot_sent,
    hot_arrived,
    piece_sent,
    piece_passed,
    piece_arrived,
    message_sent,
    message_arrived,
    shade_sent,
    shade_arrived,
    gain_sent,
    gain_arrived,
    turned_sent,
    turned_arrived,
    weight_sent,
    weight_passed,
    weight_arrived,
    far_sent,
    far_passed,
    far_relayed,
    far_arrived,
    field_sent,
    field_passed,
    field_arrived,
    part_sent,
    part_arrived,
    done_sent,
    done_arrived,
):
    group = lax.axis_index("grp")
    shard = lax.axis_index("shard")
    me = group * shards + shard
    total = groups * shards
    tokens, model = latent_ref.shape
    rows = model // shards
    width = head_ref.shape[1]
    ray_count, ray_depth = spacing_ref.shape
    slots = 4 * ray_count // total
    fan_scale = width ** (-0.5)
    per_layer = width * width // model
    strips = model // width
    period = FEATURES // strips
    fold_rows = 2 * FOLDED + per_layer
    sent_rows = FOLDED + per_layer
    own_rays, hot_rays = ray_room(total, shards, ray_count)
    f32 = jnp.float32
    bf16 = jnp.bfloat16

    latent = latent_ref[...].astype(f32)
    inv_rms = lax.rsqrt(jnp.mean(latent * latent, axis=1, keepdims=True) + norm_eps)
    x_norm = (latent * inv_rms * gain_ref[...]).astype(bf16)
    fold = jnp.where(
        iota((FOLDED, per_layer), 1) % period == iota((FOLDED, per_layer), 0), 1.0, 0.0
    ).astype(bf16)
    folded = product(fold, x_norm[:per_layer])
    folded_high = folded.astype(bf16).astype(f32)
    stacked = jnp.concatenate(
        [folded_high, folded - folded_high, x_norm[per_layer:].astype(f32)], axis=0
    )
    turned_own[...] = stacked.T.astype(bf16).reshape(turned_own.shape)

    scene = scene_ref[...]
    lane = iota((1, LANES), 1)
    ray_row = iota((ray_count, ray_count), 0)
    ray_column = iota((ray_count, ray_count), 1)
    scene_wide = jnp.broadcast_to(scene, (ray_count, ray_count))
    scene_tall = jnp.sum(jnp.where(ray_row == ray_column, scene_wide, 0), axis=1, keepdims=True)
    count_row[...] = jnp.sum(jnp.where(scene_tall == lane, 1.0, 0.0), axis=0, keepdims=True)
    same_scene = scene_tall == scene_wide
    rank_wide = jnp.sum(
        jnp.where(jnp.logical_and(same_scene, ray_row < ray_column), 1, 0), axis=0, keepdims=True
    )
    rank_tall = jnp.sum(
        jnp.where(jnp.logical_and(same_scene, ray_column < ray_row), 1, 0), axis=1, keepdims=True
    )
    head_t[...] = (head_ref[...].astype(f32) * fan_scale).T.astype(bf16)
    grad_first[...] = jnp.zeros_like(grad_first)
    grad_second[...] = jnp.zeros_like(grad_second)

    wait_all()

    def turned_copy(other, place):
        return pltpu.make_async_remote_copy(
            src_ref=turned_own.at[other],
            dst_ref=turned.at[place],
            send_sem=turned_sent.at[other],
            recv_sem=turned_arrived.at[place],
            device_id=(group, other),
            device_id_type=MESH,
        )

    def weight_of(origin):
        return weights[pl.ds(pl.multiple_of(origin * rows, rows), rows), :]

    others = [lax.rem(shard + step, shards) for step in range(1, shards)]
    start_counts, receive_counts, finish_counts = messages(
        groups, shards, lambda other: count_row, landed_counts, count_sent, count_arrived
    )
    start_far, start_near, relay_far, receive_weights, finish_weights = weight_gather(
        weight_ref,
        weights,
        weight_sent,
        far_sent,
        weight_passed,
        far_passed,
        far_relayed,
        weight_arrived,
        far_arrived,
    )
    start_messages, receive_messages, finish_messages = messages(
        groups, shards, lambda other: message.at[other], landed, message_sent, message_arrived
    )
    start_lead, receive_lead, finish_lead = plane_gather(
        lead_own, lambda origin: leads.at[origin], lead_sent, lead_passed, lead_arrived
    )
    start_counts()
    start_far()
    for other in others:
        turned_copy(other, shard).start()
    start_near()
    landed_counts[me] = count_row[...]
    turned[shard] = turned_own[shard]
    weights[pl.ds(pl.multiple_of(shard * rows, rows), rows), :] = weight_ref[...]

    relay_far()
    receive_counts()
    counts = landed_counts[:, 0, :]
    hot_lanes = jnp.min(jnp.where(counts == slots, 1, 0), axis=0, keepdims=True)
    hot = jnp.sum(jnp.where(hot_lanes > 0, lane, 0), axis=1, keepdims=True)
    hot_here = hot // shards == group
    hot_ray = scene == hot
    hot_target = (hot // shards) * shards + (me * slots + rank_wide) % shards
    owner = iota((total, ray_count), 0)
    mine = jnp.where(hot_ray, -1, scene) == owner
    led = jnp.where(hot_ray, hot_target, -1) == owner
    payload = jnp.concatenate([points_ref[...], spacing_ref[...]], axis=1)
    chosen = jnp.concatenate(
        [jnp.where(jnp.where(mine, rank_wide, -1) == j, 1.0, 0.0) for j in range(slots)]
        + [jnp.where(led, 1.0, 0.0)],
        axis=0,
    )
    filled = select(chosen.astype(bf16), payload)
    for j in range(slots + 1):
        message[:, 2 * j, :] = filled[j * total : (j + 1) * total, :LANES]
        message[:, 2 * j + 1, :] = filled[j * total : (j + 1) * total, LANES:]
    spread = jnp.where(iota((3, LANES), 1) % 4 == iota((3, LANES), 0), 1.0, 0.0)
    extra = over_first_select(target_ref[...], spread.astype(bf16)) + jnp.where(lane % 4 == 3, 1.0, 0.0)
    own_extra = jnp.where(rank_tall == lane // 4, extra, 0.0)
    hot_extra = jnp.where(lane // 4 == slots, extra, 0.0)
    message[:, 2 * slots + 2, :] = select(chosen_as(mine), own_extra) + select(
        chosen_as(led), hot_extra
    )
    start_messages()
    landed[me] = message[me]

    for other in others:
        turned_copy(other, other).wait_recv()
    hot_shard = jnp.where(hot_here, hot % shards, -1)
    lead = jnp.zeros((rows, fold_rows), f32)
    for origin in range(shards):
        lead = lead + jnp.where(hot_shard == origin, turned[origin].astype(f32), 0.0)
    lead_own[...] = lead.astype(bf16)
    start_lead()
    leads[shard] = lead_own[...]

    field_sum = [over_first(turned_own[shard], weight_ref[...])]

    def add_field(origin):
        field_sum[0] = field_sum[0] + over_first(turned_own[origin], weight_of(origin))

    receive_weights(add_field)

    def set_weights(which, field):
        first_rows = (field[:FOLDED] + field[FOLDED : 2 * FOLDED]) * fan_scale
        second_rows = field[2 * FOLDED :].astype(bf16).astype(f32) * fan_scale
        for m in range(strips):
            strip = slice(m * width, (m + 1) * width)
            store_rows(wide_first, m, FOLDED, strips, first_rows[:, strip])
            store_rows(wide_second, m, per_layer, strips, second_rows[:, strip])
        first = joined(wide_first)[:FEATURES]
        wide = joined(wide_second)
        first_high = first.astype(bf16).astype(f32)
        first_t[which] = jnp.concatenate([first_high, first - first_high], axis=0).T.astype(bf16)
        second[which] = wide.astype(bf16)
        second_t[which] = wide.T.astype(bf16)

    set_weights(0, field_sum[0])

    receive_messages()
    wanted = jnp.where(lane == me, 1.0, 0.0) * jnp.where(hot == me, 0.0, 1.0)
    many = slots * total
    tall_counts = jnp.concatenate([counts] * slots, axis=0).astype(bf16)
    wanted = jnp.broadcast_to(wanted, (8, LANES)).astype(bf16)
    wide_numbers = over_last(wanted, tall_counts)[0:1]
    earlier = chosen_as(iota((total, many), 0) < iota((total, many), 1) % total)
    offsets = product(over_last(wanted, counts.astype(bf16)).astype(bf16), earlier)[0:1]
    extras = landed[:, 2 * slots + 2, :]

    def arrived_slot(j):
        lifted = extras if j == 0 else pltpu.roll(extras, LANES - 4 * j, 1)
        return jnp.concatenate([landed[:, 2 * j, :], landed[:, 2 * j + 1, :], lifted], axis=1)

    slot_of = (iota((1, many), 1) // total).astype(f32)
    slot_at = jnp.where(wide_numbers > slot_of, offsets + slot_of, -1.0)
    keep = chosen_as(slot_at == iota((own_rays, many), 0).astype(f32))
    own_slots = select(keep, jnp.concatenate([arrived_slot(j) for j in range(slots)], axis=0))
    hot_place = (iota((hot_rays, total), 0) * shards + shard) // slots
    hot_keep = chosen_as(hot_place == iota((hot_rays, total), 1))
    hot_slots = select(hot_keep, arrived_slot(slots))
    own_pairs, hot_pairs = own_rays // 2, hot_rays // 2
    all_pairs = own_pairs + hot_pairs
    lower = jnp.concatenate([own_slots[:own_pairs], hot_slots[:hot_pairs]], axis=0)
    upper = jnp.concatenate([own_slots[own_pairs:], hot_slots[hot_pairs:]], axis=0)
    low = lane < ray_depth

    def unpack(at):
        left, right = lower[:, at : at + LANES], upper[:, at : at + LANES]
        return (
            jnp.where(low, left, pltpu.roll(right, ray_depth, 1)),
            jnp.where(low, pltpu.roll(left, ray_depth, 1), right),
        )

    coords[0], coords[1] = unpack(0)
    coords[2], spacing = unpack(LANES)

    def widen(c):
        at = 2 * LANES + c
        return jnp.where(low, lower[:, at : at + 1], upper[:, at : at + 1])

    own_count = jnp.sum(jnp.where(slot_of == 0.0, wide_numbers, 0.0), axis=1, keepdims=True)
    own_factor = 1.0 / (total * jnp.maximum(own_count, 1.0))
    hot_factor = 1.0 / (total * total * slots)
    factor = widen(3) * jnp.where(iota((all_pairs, 1), 0) < own_pairs, own_factor, hot_factor)
    targets = [widen(c) for c in range(3)]
    own_blocks = own_pairs // 8
    blocks = all_pairs // 8

    def forward(which):
        def step(i, carry):
            forward_block(
                i,
                coords,
                first_t.at[which],
                second_t.at[which],
                head_ref,
                encoded,
                zeros_all,
                ones_all,
                twos_all,
                raw,
            )
            return carry

        return step

    lax.fori_loop(0, own_blocks, forward(0), 0)
    lead_field = [over_first(lead_own[...], weight_ref[...])]

    def add_lead(origin):
        lead_field[0] = lead_field[0] + over_first(leads[origin], weight_of(origin))

    receive_lead(add_lead)
    set_weights(1, lead_field[0])
    lax.fori_loop(own_blocks, blocks, forward(1), 0)
    colors, losses = render_middle(ray_depth, raw, spacing, targets, factor, draw)
    def backward(which):
        def step(i, carry):
            backward_block(
                i, draw, second.at[which], head_t, zeros_all, ones_all, twos_all, grad_first, grad_second
            )
            return carry

        return step

    columns = model // HALVES
    piece = model // shards

    def field_strips():
        for lanes in range(width // LANES):
            at = slice(lanes * LANES, (lanes + 1) * LANES)
            wide_first[lanes, :FEATURES, :] = grad_first[:, at]
            wide_second[lanes] = grad_second[:, at]
        strip_values = []
        for m in range(strips):
            head_rows = load_rows(wide_first, m, FOLDED, strips)
            head_rows = jnp.where(iota((FOLDED, 1), 0) < period, head_rows, 0.0)
            strip_values.append(
                jnp.concatenate([head_rows, load_rows(wide_second, m, per_layer, strips)], axis=0)
            )
        return strip_values

    def hot_copy(other, place):
        return pltpu.make_async_remote_copy(
            src_ref=hot_part.at[other],
            dst_ref=hot_parts.at[place],
            send_sem=hot_sent.at[other],
            recv_sem=hot_arrived.at[place],
            device_id=(group, other),
            device_id_type=MESH,
        )

    lax.fori_loop(own_blocks, blocks, backward(1), 0)
    hot_strips = jnp.concatenate(field_strips(), axis=1)
    for p in range(shards):
        hot_part[p] = hot_strips[:, p * piece : (p + 1) * piece].astype(bf16)
    for other in others:
        hot_copy(other, shard).start()
    grad_first[...] = jnp.zeros_like(grad_first)
    grad_second[...] = jnp.zeros_like(grad_second)
    lax.fori_loop(0, own_blocks, backward(0), 0)
    for m, values in enumerate(field_strips()):
        half, place = divmod(m * width, columns)
        d_field[half, :, place : place + width] = values.astype(bf16)

    gathers = [
        plane_gather(
            d_field.at[half],
            lambda origin, half=half: fields.at[half, origin],
            field_sent.at[half],
            field_passed.at[half],
            field_arrived.at[half],
        )
        for half in range(HALVES)
    ]
    gathers[0][0]()

    shade = jnp.where(
        lane == 4 * slots + 4,
        jnp.sum(losses, axis=(0, 1), keepdims=True) * (1.0 / ray_depth),
        0.0,
    )

    def color_rows(start, stop):
        columns = []
        for side in (0, ray_depth):
            values = jnp.zeros((stop - start, LANES), f32)
            for c in range(3):
                values = jnp.where(lane == c, colors[c][start:stop, side : side + 1], values)
            columns.append(values)
        return jnp.concatenate(columns, axis=0)

    own_colors = color_rows(0, own_pairs)
    hot_colors = color_rows(own_pairs, all_pairs)
    back = select(keep, own_colors, (0, 0))
    for j in range(slots):
        part_back = back[j * total : (j + 1) * total]
        shade = shade + (part_back if j == 0 else pltpu.roll(part_back, 4 * j, 1))
    shade = shade + pltpu.roll(select(hot_keep, hot_colors, (0, 0)), 4 * slots, 1)
    shades[:, 0, :] = shade
    start_shades, receive_shades, finish_shades = messages(
        groups, shards, lambda other: shades.at[other], landed_shades, shade_sent, shade_arrived
    )
    start_shades()
    landed_shades[me] = shades[me]

    piece_sum = hot_part[shard].astype(f32)
    for other in others:
        hot_copy(other, other).wait_recv()
        piece_sum = piece_sum + hot_parts[other].astype(f32)
    hot_piece[...] = piece_sum.astype(bf16)
    start_hot, receive_hot, finish_hot = plane_gather(
        hot_piece, lambda origin: hot_all.at[origin], piece_sent, piece_passed, piece_arrived
    )
    start_hot()
    for half in range(1, HALVES):
        gathers[half][0]()
    hot_all[shard] = hot_piece[...]

    group_steps = [lax.rem(group + step, groups) for step in range(1, groups)]

    def part_copy(half, other, place):
        return pltpu.make_async_remote_copy(
            src_ref=part.at[half, other],
            dst_ref=parts.at[half, place],
            send_sem=part_sent.at[half, other],
            recv_sem=part_arrived.at[half, place],
            device_id=(other, shard),
            device_id_type=MESH,
        )

    def done_copy(half, other, place):
        return pltpu.make_async_remote_copy(
            src_ref=done.at[half, place],
            dst_ref=done.at[half, place],
            send_sem=done_sent.at[half, other],
            recv_sem=done_arrived.at[half, place],
            device_id=(other, shard),
            device_id_type=MESH,
        )

    def head_term(origin, values):
        lead = values[:FOLDED]
        return product(turned[origin], jnp.concatenate([lead, lead, values[FOLDED:]], axis=0))

    def gather_half(half):
        head_sum = [head_term(shard, d_field[half])]

        def add_head(origin):
            head_sum[0] = head_sum[0] + head_term(origin, fields[half, origin])

        gathers[half][1](add_head)
        if half == 0:
            receive_hot(lambda origin: None)
        per_half = shards // HALVES
        hot_values = jnp.concatenate(
            [hot_all[p] for p in range(half * per_half, (half + 1) * per_half)], axis=1
        )
        hot_top = hot_values[:FOLDED]
        head_sum[0] = head_sum[0] + product(
            lead_own[...], jnp.concatenate([hot_top, hot_top, hot_values[FOLDED:]], axis=0)
        )
        part[half] = head_sum[0].astype(bf16).reshape(part.shape[1:])
        for other in group_steps:
            part_copy(half, other, group).start()

    gain_terms = []

    def sum_half(half):
        slice_sum = part[half, group].astype(f32)
        for other in group_steps:
            part_copy(half, other, other).wait_recv()
            slice_sum = slice_sum + parts[half, other].astype(f32)
        weight = weight_part_ref[group][:, half * columns : (half + 1) * columns].astype(f32)
        gain_terms.append(jnp.sum(slice_sum * weight, axis=1, keepdims=True))
        if half == HALVES - 1:
            same_row = iota((slice_rows, slice_rows), 0) == iota((slice_rows, slice_rows), 1)
            gain_row[0:1, :slice_rows] = jnp.sum(
                jnp.where(same_row, sum(gain_terms), 0.0), axis=0, keepdims=True
            )
            start_gain()
        done[half, group] = slice_sum.astype(bf16)
        for other in group_steps:
            done_copy(half, other, group).start()

    slice_rows = rows // groups
    start_gain, receive_gain, finish_gain = messages(
        groups, shards, lambda other: gain_row, landed_gain, gain_sent, gain_arrived
    )
    for half in range(HALVES):
        gather_half(half)
        if half >= LAG:
            sum_half(half - LAG)
    for half in range(HALVES - LAG, HALVES):
        sum_half(half)
    landed_gain[me] = gain_row[...]

    token = iota((tokens, sent_rows), 0)
    source = jnp.where(token < per_layer, token % period, token - per_layer + FOLDED)
    copies = jnp.where(source == iota((tokens, sent_rows), 1), 1.0, 0.0).astype(bf16)
    own_field = jnp.concatenate([d_field[half] for half in range(HALVES)], axis=1)
    hot_field = jnp.concatenate([hot_all[p] for p in range(shards)], axis=1)
    own_field = jnp.where(hot == me, hot_field.astype(f32), own_field.astype(f32)).astype(bf16)
    d_norm = over_last(product(copies, own_field).astype(bf16), weights[...])
    latent = latent_ref[...].astype(f32)
    inv_rms = lax.rsqrt(jnp.mean(latent * latent, axis=1, keepdims=True) + norm_eps)
    x_hat = latent * inv_rms
    d_scaled = d_norm * gain_ref[...]
    latent_grad_ref[...] = (
        inv_rms * (d_scaled - x_hat * jnp.mean(d_scaled * x_hat, axis=1, keepdims=True))
    ).astype(bf16)

    latent_out().start()
    receive_shades()
    returned = landed_shades[:, 0, :]
    loss_ref[...] = jnp.sum(
        jnp.where(lane == 4 * slots + 4, returned, 0.0), axis=(0, 1), keepdims=True
    )
    picked = over_first_select(returned, chosen_as(mine) + chosen_as(led))
    first_place = jnp.where(hot_ray, 4 * slots, 4 * rank_wide)
    place = iota((LANES, ray_count), 0)
    for c in range(3):
        color_ref[c : c + 1, :] = jnp.sum(
            jnp.where(place == first_place + c, picked, 0.0), axis=0, keepdims=True
        )

    for half in range(HALVES):
        for other in group_steps:
            done_copy(half, other, other).wait_recv()
        grad_out(half, done.at[half]).start()
    receive_gain()
    gains = landed_gain[:, 0, :slice_rows]
    gains = jnp.concatenate([gains[g * shards : (g + 1) * shards] for g in range(groups)], axis=1)
    gain_grad_ref[...] = gains / gain_rows_ref[...]

    latent_out().wait()
    for half in range(HALVES):
        grad_out(half, done.at[half]).wait()
    finish_counts()
    finish_weights()
    finish_messages()
    finish_lead()
    finish_hot()
    for other in others:
        hot_copy(other, shard).wait_send()
    finish_shades()
    finish_gain()
    for other in others:
        turned_copy(other, shard).wait_send()
    for half in range(HALVES):
        gathers[half][2]()
        for other in group_steps:
            part_copy(half, other, group).wait_send()
            done_copy(half, other, group).wait_send()


def body(
    latents,
    head_weight,
    norm_gain,
    color_head,
    sample_points,
    sample_spacing,
    ray_targets,
    ray_scene,
):
    groups, shards = lax.axis_size("grp"), lax.axis_size("shard")
    devices = groups * shards
    ray_count, ray_depth = sample_spacing.shape
    tokens, model = latents.shape
    width = color_head.shape[1]
    rows = model // shards
    slots = 4 * ray_count // devices
    per_layer = width * width // model
    fold_rows = 2 * FOLDED + per_layer
    sent_rows = FOLDED + per_layer
    samples = sum(ray_room(devices, shards, ray_count)) * ray_depth
    columns = model // HALVES
    slice_rows = rows // groups
    in_vmem = pl.BlockSpec(memory_space=pltpu.VMEM)
    dma = pltpu.SemaphoreType.DMA
    f32, bf16 = jnp.float32, jnp.bfloat16
    vmem = pltpu.VMEM
    anywhere = pl.BlockSpec(memory_space=pl.ANY)
    inputs = (
        latents,
        head_weight,
        head_weight.reshape(groups, slice_rows, model),
        norm_gain.reshape(1, model),
        norm_gain.reshape(shards, rows),
        color_head,
        sample_points,
        sample_spacing,
        ray_targets,
        ray_scene.reshape(1, ray_count),
    )
    colors, loss, head, gain, latent_grad = pl.pallas_call(
        functools.partial(staged_kernel, groups, shards),
        in_specs=[anywhere] * INPUTS,
        out_specs=[in_vmem, in_vmem, anywhere, in_vmem, anywhere],
        out_shape=[
            jax.ShapeDtypeStruct((3, ray_count), f32),
            jax.ShapeDtypeStruct((1, 1), f32),
            jax.ShapeDtypeStruct((groups, slice_rows, model), bf16),
            jax.ShapeDtypeStruct((shards, rows), f32),
            jax.ShapeDtypeStruct((tokens, model), bf16),
        ],
        scratch_shapes=[vmem((tokens, model), bf16)]
        + [vmem(value.shape, value.dtype) for value in inputs]
        + [
            vmem((1, LANES), f32),
            vmem((devices, 1, LANES), f32),
            vmem((rows, fold_rows), bf16),
            vmem((shards, rows, fold_rows), bf16),
            vmem((shards, sent_rows, rows), bf16),
            vmem((shards, sent_rows, rows), bf16),
            vmem((sent_rows, rows), bf16),
            vmem((shards, sent_rows, rows), bf16),
            vmem((devices, 2 * slots + 3, LANES), f32),
            vmem((devices, 2 * slots + 3, LANES), f32),
            vmem((shards, rows, fold_rows), bf16),
            vmem((shards, rows, fold_rows), bf16),
            vmem((model, model), bf16),
            vmem((width // LANES, FOLDED * model // width, LANES), f32),
            vmem((width // LANES, width, LANES), f32),
            vmem((2, width, 2 * FEATURES), bf16),
            vmem((2, width, width), bf16),
            vmem((2, width, width), bf16),
            vmem((width, 4), bf16),
            vmem((8 * FEATURES, LANES), f32),
            vmem((3, samples // LANES, LANES), f32),
            vmem((FEATURES, samples), bf16),
            vmem((width, samples), bf16),
            vmem((width, samples), bf16),
            vmem((4, samples // LANES, LANES), f32),
            vmem((4, samples), f32),
            vmem((FEATURES, width), f32),
            vmem((width, width), f32),
            vmem((devices, 1, LANES), f32),
            vmem((devices, 1, LANES), f32),
            vmem((HALVES, sent_rows, columns), bf16),
            vmem((HALVES, shards, sent_rows, columns), bf16),
            vmem((HALVES, groups, slice_rows, columns), bf16),
            vmem((HALVES, groups, slice_rows, columns), bf16),
            vmem((HALVES, groups, slice_rows, columns), bf16),
            vmem((1, LANES), f32),
            vmem((devices, 1, LANES), f32),
            dma,
            dma,
            dma((shards,)),
            dma((shards,)),
            dma((shards,)),
            dma((shards,)),
            dma((shards,)),
            dma((shards,)),
            dma((shards,)),
            dma((shards,)),
            dma,
            dma,
            dma,
            dma,
            dma,
            dma,
            dma((shards,)),
            dma((shards,)),
            dma((shards,)),
            dma((shards,)),
            dma((shards,)),
            dma((shards,)),
            dma((shards, groups)),
            dma((shards, groups)),
            dma((shards, groups)),
            dma((HALVES, shards)),
            dma((HALVES, shards)),
            dma((HALVES, shards)),
            dma((HALVES, groups)),
            dma((HALVES, groups)),
            dma((HALVES, groups)),
            dma((HALVES, groups)),
            dma((INPUTS,)),
            dma((HALVES + 1,)),
        ],
        compiler_params=pltpu.CompilerParams(collective_id=1, has_side_effects=True),
    )(*inputs)
    colors, loss, head_grad, gain, latent_grad = hand_out(colors, loss, head, gain, latent_grad)
    return (colors, loss[0, 0], head_grad, gain.reshape(model), latent_grad)


def hand_out_kernel(count, *refs):
    sources, targets = refs[:count], refs[count : 2 * count]
    buffers = refs[2 * count : 3 * count]
    wide, arrived, left = refs[3 * count :]
    inward = [
        pltpu.make_async_copy(sources[i], buffers[i], arrived.at[i]) for i in range(count)
    ]
    for copy in inward:
        copy.start()
    outward = [
        pltpu.make_async_copy(buffers[i], targets[i], left.at[i]) for i in range(1, count)
    ]
    groups, slice_rows, model = buffers[0].shape
    inward[0].wait()
    for g in range(groups):
        rows = pl.ds(g * slice_rows, slice_rows)
        wide[rows, :] = buffers[0][g].astype(jnp.float32)
        outward.append(
            pltpu.make_async_copy(wide.at[rows], targets[0].at[rows], left.at[count + g])
        )
        outward[-1].start()
    for i in range(1, count):
        inward[i].wait()
        outward[i - 1].start()
    for copy in outward:
        copy.wait()


def hand_out(colors, loss, head, gain, latent_grad):
    groups, slice_rows, model = head.shape
    values = [head, latent_grad, colors, loss, gain]
    count = len(values)
    full = jax.ShapeDtypeStruct((groups * slice_rows, model), jnp.float32)
    anywhere = pl.BlockSpec(memory_space=pl.ANY)
    head, latent_grad, colors, loss, gain = pl.pallas_call(
        functools.partial(hand_out_kernel, count),
        in_specs=[anywhere] * count,
        out_specs=[anywhere] * count,
        out_shape=[full] + [jax.ShapeDtypeStruct(v.shape, v.dtype) for v in values[1:]],
        scratch_shapes=[pltpu.VMEM(v.shape, v.dtype) for v in values]
        + [
            pltpu.VMEM(full.shape, full.dtype),
            pltpu.SemaphoreType.DMA((count,)),
            pltpu.SemaphoreType.DMA((count + groups,)),
        ],
    )(*values)
    return colors, loss, head, gain, latent_grad


def solution(mesh):
    placed = (
        P(("grp", "shard"), None),
        P("shard", None),
        P(),
        P(),
        P(("grp", "shard"), None),
        P(("grp", "shard"), None),
        P(None, ("grp", "shard")),
        P(("grp", "shard")),
    )
    return jax.shard_map(
        body,
        mesh=mesh,
        in_specs=placed,
        out_specs=(
            P(None, ("grp", "shard")),
            P(),
            P("shard", None),
            P(),
            P(("grp", "shard"), None),
        ),
        check_vma=False,
    )
```
